32 devices in a mesh: lat: 4 (over z), lon: 8 (over y, x, core).
Axes of the slice: x: 2, y: 2, z: 4, core: 2. Of those that a mesh axis runs over, the one named last changes fastest.
Arguments:
- tracers: float32 [16, 8, 64, 1024], P(None, None, 'lat', 'lon'), may hold values from -6 to 6
- winds: float32 [3, 8, 64, 1024], P(None, None, 'lat', 'lon'), may hold values from -4 to 4
- depart_first: int32 [3, 8, 64, 1024], P(None, None, 'lat', 'lon'), may hold values from -3 to 2, as said below
- depart_second: int32 [3, 8, 64, 1024], P(None, None, 'lat', 'lon'), may hold values from -2 to 1, as said below
- fluxes: bfloat16 [384, 128, 256], P(('lat', 'lon')), may hold values from 0.049804688 to 5
- remap_weights: bfloat16 [384, 4, 256, 128], P(('lat', 'lon')), may hold values from 0.00019931793 to 0.019897461
- target_device: int32 [384, 4], P(('lat', 'lon')), may hold values from 0 to 31, all different within a row; in each aligned block of 12 rows (0 to 11, 12 to 23, ...) at most 2 rows name the same one
- target_block: int32 [384, 4], P(('lat', 'lon')), may hold values from 0 to 15
Outputs:
- advected: float32 [16, 8, 64, 1024], P(None, None, 'lat', 'lon')
The draws below stay inside these ranges and needn't reach their ends.
Inputs may be any that keep to these rules, and one draw needn't show every extreme that they name: `depart_first`: component 0 (levels) is -1 or 0; components 1 and 2 are row and column offsets. `depart_second`: component 0 (levels) is -1 or 0; components 1 and 2 are row and column offsets. `target_device`: device g is the one at lat index g // 8 and lon index g % 8. Each row names 4 different devices; among the rows of one device no device is named more than 2 times.
All inputs are finite; a program needn't handle non-finite values.
Results may differ from the reference program's by a relative error of at most 0.00088.
Values may be sent and summed in bfloat16 or wider, within the bound.
A program may use at most 192 MiB of HBM per device.

```python
import math
import jax
import jax.numpy as jnp
import numpy as np
from jax import lax

NTR = 16
LEV = 8
CLAT = 16
CLON = 128
K = 4
CAP = 2
NTILE = 12
TILE_CELLS = 256
BLK_DEV = 16
HMAX = 3
ROWS = 128
BCOLS = 128
NLAT = 64
NLON = 1024
TILES = 384
N_LAT = 4
N_LON = 8
DEVICES = 32


def offsets_first(key):
    vertical = jax.random.randint(jax.random.fold_in(key, 1), (1, LEV, NLAT, NLON), -1, 1)
    across = jax.random.randint(jax.random.fold_in(key, 2), (2, LEV, NLAT, NLON), -HMAX, HMAX)
    return jnp.concatenate([vertical, across], axis=0).astype(jnp.int32)


def draw_depart_first(key, part):
    return offsets_first(jax.random.fold_in(key, 11))


def draw_depart_second(key, part):
    first = offsets_first(jax.random.fold_in(key, 11))
    extra = jax.random.randint(jax.random.fold_in(key, 12), first.shape, 0, 2)
    return jnp.floor_divide(first + extra, 2).astype(jnp.int32)


def draw_winds(key, part):
    first = offsets_first(jax.random.fold_in(key, 11)).astype(jnp.float32)
    phase = jax.random.uniform(jax.random.fold_in(key, 13), first.shape, jnp.float32, -0.25, 1.25)
    return -(first + phase)


def touch_ends(entries, stream_key, low, top_value):
    longest = entries.shape.index(max(entries.shape))
    spots = []
    for shift in (0, 1):
        where = [jax.random.randint(jax.random.fold_in(stream_key, axis), (), 0, length) for axis, length in enumerate(entries.shape)]
        where[longest] = (where[longest] + shift) % entries.shape[longest]
        spots.append(tuple(where))
    return entries.at[spots[0]].set(low).at[spots[1]].set(top_value)


def level_of(rng, extent, pieces, smallest, largest):
    gain, own = 1.0, jax.random.fold_in(rng, 6)
    for dim, blocks in pieces:
        steps = jnp.exp(jax.random.uniform(jax.random.fold_in(own, dim), (blocks,), jnp.float32, smallest / len(pieces), largest / len(pieces)))
        gain = gain * jnp.repeat(steps, extent[dim] // blocks).reshape([-1 if axis == dim else 1 for axis in range(len(extent))])
    return gain


def deal_out(key, own, number, rows, count, top, reach, lean):
    order = jax.random.permutation(key, count)
    crowded, usual = load_shares(count, rows * top, reach, lean, True), load_shares(count, rows * top, reach, lean, False)
    places = jnp.arange(count)

    def named(tallies, offset_by):
        used = int((tallies > 0).sum())
        fixed = max(1, used // 4)
        passed = fixed + (places - fixed + offset_by * (used - fixed)) % max(1, count - fixed)
        return jnp.zeros((count,), jnp.int32).at[order[jnp.where(places < fixed, places, passed)]].set(jnp.asarray(tallies, jnp.int32))

    tallies = jnp.where(number % 4 == 0, named(crowded, number // 4), named(usual, number - number // 4 - 1))
    mixed = jax.random.permutation(jax.random.fold_in(own, 3), count)
    source_of, sink = mixed[0:count // 2 * 2:2], mixed[1:count // 2 * 2:2]
    slack = jnp.minimum(tallies[source_of] - 1, reach - tallies[sink]) // 2
    slack = jnp.where((source_of == order[0]) | (sink == order[0]) | (tallies[sink] == 0), 0, jnp.maximum(slack, 0))
    passed = jax.random.randint(jax.random.fold_in(own, 4), (count // 2,), 0, 1 << 20) % (slack + 1)
    tallies = tallies.at[source_of].add(-passed).at[sink].add(passed)
    labels = jnp.searchsorted(jnp.cumsum(tallies), jnp.arange(rows * top), side="right").astype(jnp.int32)
    table = labels.reshape(top, rows).T
    table = table[jax.random.permutation(jax.random.fold_in(own, 1), rows)]
    offset_by = jax.random.randint(jax.random.fold_in(own, 2), (rows, 1), 0, top)
    return jnp.take_along_axis(table, (jnp.arange(top)[None, :] + offset_by) % top, axis=1)


def load_shares(amount, total, most, slope, full):
    loads = [(1 << 20) // math.isqrt(grade ** slope) + 1 for grade in range(1, amount + 1)]
    largest = most if full else min(most, max(-(-total // amount), total * loads[0] // sum(loads)))
    least = 1 if total - largest >= amount - 1 else 0
    counts, surplus = [largest] + [least] * (amount - 1), total - largest - least * (amount - 1)
    while surplus > 0:
        movable = [i for i in range(1, amount) if counts[i] < largest] or [i for i in range(1, amount) if counts[i] < most]
        pool, left = sum([loads[i] for i in movable]), surplus
        for i in movable:
            addition = min(most - counts[i], max(1, left * loads[i] // pool), surplus)
            counts[i] = counts[i] + addition
            surplus = surplus - addition
    return np.array(counts)


def bell_draw(key, dims, deviation, bound, cuts=(), held_as=jnp.bfloat16):
    result = deviation * jax.random.normal(key, dims, jnp.float32)
    if cuts:
        result = result * level_of(key, dims, cuts, -0.22, 0.18)
    return jnp.clip(result, -bound, bound).astype(held_as)


def setup_inputs(seed: int = 0) -> dict:
    key_of = jax.random.split(jax.random.key(seed), 9)
    tracers = bell_draw(key_of[0], (NTR, LEV, NLAT, NLON), 1.0, 6.0, ((2, 4), (3, 8)), jnp.float32)
    winds = draw_winds(jax.random.fold_in(key_of[8], 71), 0)
    depart_first = draw_depart_first(jax.random.fold_in(key_of[8], 71), 0)
    depart_second = draw_depart_second(jax.random.fold_in(key_of[8], 71), 0)
    fluxes = jnp.clip(jnp.exp(math.log(5.0) - 4.609084 * jax.random.uniform(key_of[4], (TILES, ROWS, TILE_CELLS), jnp.float32) ** level_of(key_of[4], (TILES, ROWS, TILE_CELLS), ((0, 32),), -0.2, 0.2)), 0.049804688, 5.0).astype(jnp.bfloat16)
    remap_weights = jnp.clip(jnp.exp(math.log(0.019897461) - 4.603446 * jax.random.uniform(key_of[5], (TILES, K, TILE_CELLS, BCOLS), jnp.float32) ** level_of(key_of[5], (TILES, K, TILE_CELLS, BCOLS), ((0, 32),), -0.2, 0.2)), 0.00019931793, 0.019897461).astype(jnp.bfloat16)
    target_device_keys = jax.random.split(jax.random.fold_in(key_of[6], 1), TILES // NTILE)
    target_device_turns = jax.random.permutation(jax.random.fold_in(key_of[6], 3), TILES // NTILE)
    target_device = jax.vmap(lambda own, number: deal_out(jax.random.fold_in(key_of[6], 2), own, number, NTILE, DEVICES, K, CAP, 2))(target_device_keys, target_device_turns).reshape((TILES, K))
    target_block = touch_ends(jax.random.randint(key_of[7], (TILES, K), 0, BLK_DEV), jax.random.fold_in(key_of[7], 1), 0, BLK_DEV - 1).astype(jnp.int32)
    return {"tracers": tracers, "winds": winds, "depart_first": depart_first, "depart_second": depart_second, "fluxes": fluxes, "remap_weights": remap_weights, "target_device": target_device, "target_block": target_block}


def cubic_weights(frac):
    first = -frac * (frac - 1.0) * (frac - 2.0) / 6.0
    second = (frac + 1.0) * (frac - 1.0) * (frac - 2.0) / 2.0
    third = -(frac + 1.0) * frac * (frac - 2.0) / 2.0
    fourth = (frac + 1.0) * frac * (frac - 1.0) / 6.0
    return (first, second, third, fourth)


def tricubic(padded, base, frac):
    chans, levels, rows, cols = padded.shape
    flat = padded.reshape(chans, levels * rows * cols)
    level_w = cubic_weights(frac[0])
    row_w = cubic_weights(frac[1])
    col_w = jnp.stack(cubic_weights(frac[2]))
    col_index = jnp.stack([base[2] + step for step in (-1, 0, 1, 2)]).astype(jnp.int32)
    total = jnp.zeros((chans,) + base.shape[1:], jnp.float32)
    for above in range(4):
        level_index = jnp.clip(base[0] + above - 1, 0, levels - 1).astype(jnp.int32)
        for across in range(4):
            row_index = (base[1] + across - 1).astype(jnp.int32)
            index = ((level_index * rows + row_index) * cols)[None] + col_index
            picked = jnp.take(flat, index.reshape(-1), axis=1).reshape((chans,) + index.shape)
            summed = jnp.sum(picked * col_w[None], axis=1)
            total = total + (level_w[above] * row_w[across])[None] * summed
    return total


def per_channel(padded, base, frac):
    return lax.map(lambda single: tricubic(single[None], base, frac)[0], padded)


def extend(field, width):
    padded = jnp.pad(field, ((0, 0), (0, 0), (width, width), (0, 0)))
    return jnp.concatenate([padded[..., -width:], padded, padded[..., :width]], axis=3)


def reference(tracers, winds, depart_first, depart_second, fluxes, remap_weights, target_device, target_block):
    width = HMAX + 1
    shape = (LEV, NLAT, NLON)
    position = jnp.stack([
        lax.broadcasted_iota(jnp.int32, shape, 0),
        lax.broadcasted_iota(jnp.int32, shape, 1) + width,
        lax.broadcasted_iota(jnp.int32, shape, 2) + width,
    ])
    frac_first = jnp.clip(-winds - depart_first.astype(winds.dtype), 0.0, 1.0)
    midwind = per_channel(extend(winds, width), position + depart_first, frac_first)
    frac_second = jnp.clip(-(winds + midwind) * 0.5 - depart_second.astype(winds.dtype), 0.0, 1.0)
    moved = per_channel(extend(tracers, width), position + depart_second, frac_second)

    groups = TILES // NTILE
    block_ids = (target_device * BLK_DEV + target_block).astype(jnp.int32)

    def accumulate(total, piece):
        flux_group, weight_group, id_group = piece
        product = jnp.einsum("trc,tkcb->tkrb", flux_group.astype(jnp.float32), weight_group.astype(jnp.float32))
        product = lax.optimization_barrier(product.astype(jnp.bfloat16)).astype(jnp.float32)
        total = total.at[id_group.reshape(-1)].add(product.reshape(-1, ROWS, BCOLS))
        return total, None

    start = jnp.zeros((groups * BLK_DEV, ROWS, BCOLS), jnp.float32)
    blocks, unused = lax.scan(accumulate, start, (
        fluxes.reshape(groups, NTILE, ROWS, TILE_CELLS),
        remap_weights.reshape(groups, NTILE, K, TILE_CELLS, BCOLS),
        block_ids.reshape(groups, NTILE, K)))
    grid = blocks.reshape(N_LAT, N_LON, BLK_DEV, NTR, LEV, BCOLS).transpose(3, 4, 0, 1, 2, 5)
    grid = grid.reshape(NTR, LEV, N_LAT, N_LON, CLAT, CLON).transpose(0, 1, 2, 4, 3, 5)
    emission = grid.reshape(NTR, LEV, NLAT, NLON)
    return moved + emission
```

```python
import functools

import jax
import jax.numpy as jnp
from jax import lax
from jax.experimental import pallas as pl
from jax.experimental.pallas import tpu as pltpu
from jax.sharding import PartitionSpec as P

CAP = 2
HMAX = 3
MESH = pl.DeviceIdType.MESH
LANES = 128
BIG = 1 << 20


def cubic_weights(frac):
    first = -frac * (frac - 1.0) * (frac - 2.0) / 6.0
    second = (frac + 1.0) * (frac - 1.0) * (frac - 2.0) / 2.0
    third = -(frac + 1.0) * frac * (frac - 2.0) / 2.0
    fourth = (frac + 1.0) * frac * (frac - 1.0) / 6.0
    return (first, second, third, fourth)


def level_weights(offset, frac):
    s0, s1, s2, s3 = cubic_weights(frac)
    down = offset < 0
    zero = jnp.zeros_like(frac)
    return [
        jnp.where(down, s0, zero),
        jnp.where(down, s1, s0),
        jnp.where(down, s2, s1),
        jnp.where(down, s3, s2),
        jnp.where(down, zero, s3),
    ]


def offset_weights(offset, frac, reach):
    stencil = cubic_weights(frac)
    spread = []
    for target in range(-reach, reach + 1):
        weight = jnp.zeros(frac.shape, jnp.float32)
        for step in range(4):
            weight = jnp.where(offset == target - step + 1, stencil[step], weight)
        spread.append(weight)
    return spread


def step_kernel(
    dims,
    winds_hbm, first_hbm, second_hbm, tracers_hbm, fluxes_hbm, weights_hbm, owner_ref, block_ref,
    moved_ref, arrived_ref, labels_ref,
    winds_v, first_v, second_v, tracers_v, fluxes_v, weights_v,
    outgoing, codes_v, codes_s, marks_v,
    wind_pack, wind_rows, tracer_pack, tracer_rows,
    wind_side, wind_diag, wind_far, tracer_side, tracer_diag, tracer_far,
    shifted, lhs, rhs_a, rhs_b, masks, lev_w, row_w, col_w, col_at,
    load_sem, code_sem, halo_send, halo_recv, item_send, item_recv, mark_send, mark_recv,
):
    chans, levels, rows, comps, tiles, links, blocks, wide, narrow = dims
    lanes = LANES
    plane = levels * rows
    taps, reach = 2 * wide + 1, 2 * narrow + 1
    lat, lon = lax.axis_index("lat"), lax.axis_index("lon")
    lat_count, lon_count = lax.axis_size("lat"), lax.axis_size("lon")
    devices = lat_count * lon_count
    me = lat * lon_count + lon

    loads = [
        pltpu.make_async_copy(source, target, load_sem.at[n])
        for n, (source, target) in enumerate(
            (
                (winds_hbm, winds_v),
                (tracers_hbm, tracers_v),
                (fluxes_hbm, fluxes_v),
                (weights_hbm, weights_v),
                (first_hbm, first_v),
                (second_hbm, second_v),
            )
        )
    ]
    for load in loads:
        load.start()

    barrier = pltpu.get_barrier_semaphore()

    def greet(k, carry):
        p = lax.rem(me + k, devices)
        pl.semaphore_signal(
            barrier, inc=1, device_id=(p // lon_count, lax.rem(p, lon_count)), device_id_type=MESH
        )
        return carry

    lax.fori_loop(1, devices, greet, 0)

    width = codes_v.shape[1]
    spot = lax.broadcasted_iota(jnp.int32, (1, width), 1)
    lowest = jnp.full((1, width), BIG, jnp.int32)
    highest = jnp.full((1, width), -1, jnp.int32)
    for t in range(tiles):
        for k in range(links):
            code = (t * links + k) * blocks + block_ref[t, k]
            hit = spot == owner_ref[t, k]
            lowest = jnp.minimum(lowest, jnp.where(hit, code, BIG))
            highest = jnp.maximum(highest, jnp.where(hit, code, -1))
    used = highest >= 0
    twice = highest != lowest
    low_code = jnp.where(used, lowest, 0)
    high_code = jnp.where(used, highest, 0)
    codes_v[...] = jnp.concatenate([low_code // blocks, high_code // blocks], axis=0)
    marks_v[...] = jnp.concatenate(
        [
            jnp.where(used, low_code % blocks, -1),
            jnp.where(jnp.logical_and(used, twice), high_code % blocks, -1),
        ],
        axis=0,
    )
    code_copy = pltpu.make_async_copy(codes_v, codes_s, code_sem)
    code_copy.start()

    lane8 = lax.broadcasted_iota(jnp.int32, (8, lanes), 1)
    lane16 = lax.broadcasted_iota(jnp.int32, (chans, lanes), 1)

    def wind_main(ref, comp, i):
        return ref[pl.ds(comp * plane + i, levels, stride=rows), :]

    def tracer_main(level, r):
        return tracers_v[pl.ds(level * rows + r, chans, stride=plane), :]

    loads[0].wait()
    for half in range(rows // 8):
        for comp in range(comps):
            packed = jnp.zeros((levels, lanes), jnp.float32)
            for p in range(8):
                value = wind_main(winds_v, comp, half * 8 + p)
                packed = jnp.where(
                    lane8 // 16 == p, pltpu.roll(value, (16 * p + 8) % lanes, 1), packed
                )
            wind_pack[half, comp] = packed
    for comp in range(comps):
        for r in range(wide):
            wind_rows[0, comp, r] = wind_main(winds_v, comp, r)
            wind_rows[1, comp, r] = wind_main(winds_v, comp, rows - wide + r)
    loads[1].wait()

    def pack_row(r, carry):
        packed = jnp.zeros((chans, lanes), jnp.float32)
        for level in range(levels):
            value = tracer_main(level, r)
            packed = jnp.where(
                lane16 // 16 == level, pltpu.roll(value, (16 * level + 8) % lanes, 1), packed
            )
        tracer_pack[r] = packed
        return carry

    lax.fori_loop(0, rows, pack_row, 0)
    for r in range(narrow):
        for level in range(levels):
            tracer_rows[0, r, level] = tracer_main(level, r)
            tracer_rows[1, r, level] = tracer_main(level, rows - narrow + r)

    pl.semaphore_wait(barrier, devices - 1)

    west, east = lax.rem(lon + lon_count - 1, lon_count), lax.rem(lon + 1, lon_count)
    north, south = lat - 1, lat + 1

    def halo(n, source, target, where):
        return pltpu.make_async_remote_copy(
            src_ref=source, dst_ref=target, send_sem=halo_send.at[n], recv_sem=halo_recv.at[n],
            device_id=where, device_id_type=MESH,
        )

    def side_copies(base, pack, side):
        return [halo(base, pack, side.at[0], (lat, east)), halo(base + 1, pack, side.at[1], (lat, west))]

    def north_copies(base, cut, whole, diag, far):
        return [
            halo(base, cut, diag.at[1, 0], (north, east)),
            halo(base + 1, cut, diag.at[1, 1], (north, west)),
            halo(base + 2, whole, far.at[1], (north, lon)),
        ]

    def south_copies(base, cut, whole, diag, far):
        return [
            halo(base, cut, diag.at[0, 0], (south, east)),
            halo(base + 1, cut, diag.at[0, 1], (south, west)),
            halo(base + 2, whole, far.at[0], (south, lon)),
        ]

    wind_sides = side_copies(0, wind_pack, wind_side)
    wind_north = north_copies(2, wind_pack.at[0], wind_rows.at[0], wind_diag, wind_far)
    wind_south = south_copies(5, wind_pack.at[rows // 8 - 1], wind_rows.at[1], wind_diag, wind_far)
    tracer_sides = side_copies(8, tracer_pack, tracer_side)
    tracer_north = north_copies(
        10, tracer_pack.at[pl.ds(0, narrow)], tracer_rows.at[0], tracer_diag, tracer_far
    )
    tracer_south = south_copies(
        13, tracer_pack.at[pl.ds(rows - narrow, narrow)], tracer_rows.at[1], tracer_diag, tracer_far
    )
    has_north, has_south = lat > 0, lat < lat_count - 1

    for copy in wind_sides:
        copy.start()

    @pl.when(has_north)
    def _():
        for copy in wind_north:
            copy.start()

    @pl.when(has_south)
    def _():
        for copy in wind_south:
            copy.start()

    @pl.when(has_north)
    def _():
        for copy in tracer_north:
            copy.start()

    @pl.when(has_south)
    def _():
        for copy in tracer_south:
            copy.start()

    for copy in tracer_sides:
        copy.start()

    code_copy.wait()
    loads[2].wait()
    loads[3].wait()

    def item_copy(p):
        return pltpu.make_async_remote_copy(
            src_ref=outgoing.at[p], dst_ref=arrived_ref.at[me],
            send_sem=item_send.at[p], recv_sem=item_recv.at[me],
            device_id=(p // lon_count, lax.rem(p, lon_count)), device_id_type=MESH,
        )

    def mark_copy(p):
        return pltpu.make_async_remote_copy(
            src_ref=marks_v, dst_ref=labels_ref.at[me],
            send_sem=mark_send.at[p], recv_sem=mark_recv.at[me],
            device_id=(p // lon_count, lax.rem(p, lon_count)), device_id_type=MESH,
        )

    def product(p, c):
        item = codes_s[c, p]
        return jnp.dot(
            fluxes_v[item // links], weights_v[item], preferred_element_type=jnp.float32
        ).astype(jnp.bfloat16)

    middle = lat_count // 2
    order = sorted(range(lat_count), key=lambda away: abs(2 * away - lat_count) * 2 + (away > middle))
    order = [(away, side) for away in order for side in range(lon_count) if away or side]
    total_peers = devices - 1

    def peer_at(n):
        away = n // lon_count
        step = (away + 1) // 2
        signed = jnp.where(away % 2 == 1, -step, step)
        there = lax.rem(lat + middle + signed + lat_count, lat_count)
        return there, lax.rem(lon + n + 1, lon_count)

    def emit(n, carry):
        there, side = peer_at(n)
        p = there * lon_count + side
        for c in range(CAP):
            outgoing[p, c] = product(p, c)

        @pl.when(n > 0)
        def _():
            before, beside = peer_at(n - 1)
            item_copy(before * lon_count + beside).start()

        mark_copy(p).start()
        return carry

    lax.fori_loop(0, total_peers, emit, 0)
    there, side = peer_at(total_peers - 1)
    for c in range(CAP):
        arrived_ref[me, c] = product(me, c)
    labels_ref[me] = marks_v[...]
    item_copy(there * lon_count + side).start()

    loads[4].wait()
    loads[5].wait()
    for copy in wind_sides:
        copy.wait_recv()

    @pl.when(has_north)
    def _():
        for copy in wind_south:
            copy.wait_recv()

    @pl.when(has_south)
    def _():
        for copy in wind_north:
            copy.wait_recv()

    from_west = lane8 % 16 < 8

    def put_shifts(comp, r, main, edge):
        for e in range(taps):
            d = e - wide
            if d > 0:
                piece = pltpu.roll(jnp.where(lane8 < d, edge, main), lanes - d, 1)
            elif d < 0:
                piece = pltpu.roll(jnp.where(lane8 >= lanes + d, edge, main), -d, 1)
            else:
                piece = main
            low, high = piece[:1], piece[levels - 1 :]
            shifted[e * 5 + 0, comp, r] = jnp.concatenate([low, low, piece[: levels - 2]], axis=0)
            shifted[e * 5 + 1, comp, r] = jnp.concatenate([low, piece[: levels - 1]], axis=0)
            shifted[e * 5 + 2, comp, r] = piece
            shifted[e * 5 + 3, comp, r] = jnp.concatenate([piece[1:], high], axis=0)
            shifted[e * 5 + 4, comp, r] = jnp.concatenate([piece[2:], high, high], axis=0)

    for half in range(rows // 8):
        for comp in range(comps):
            def shift_row(p, carry, half=half, comp=comp):
                merged = jnp.where(from_west, wind_side[0, half, comp], wind_side[1, half, comp])
                edge = pltpu.roll(merged, lax.rem(2 * lanes - 8 - 16 * p, lanes), 1)
                put_shifts(comp, wide + half * 8 + p, wind_main(winds_v, comp, half * 8 + p), edge)
                return carry

            lax.fori_loop(0, 8, shift_row, 0)

    def far_rows(place, present, start, first_row):
        for comp in range(comps):
            def far_row(r, carry, comp=comp):
                merged = jnp.where(from_west, wind_diag[place, 0, comp], wind_diag[place, 1, comp])
                edge = pltpu.roll(merged, lax.rem(2 * lanes - 8 - 16 * (first_row + r), lanes), 1)
                main = wind_far[place, comp, r]
                edge = jnp.where(present, edge, 0.0)
                main = jnp.where(present, main, 0.0)
                put_shifts(comp, start + r, main, edge)
                return carry

            lax.fori_loop(0, wide, far_row, 0)

    far_rows(0, has_north, 0, 8 - wide)
    far_rows(1, has_south, wide + rows, 0)

    column = lax.broadcasted_iota(jnp.int32, (levels, lanes), 1)

    def wind_row(i, carry):
        wind = [wind_main(winds_v, comp, i) for comp in range(comps)]
        off = [wind_main(first_v, comp, i) for comp in range(comps)]
        frac = [
            jnp.clip(-wind[comp] - off[comp].astype(jnp.float32), 0.0, 1.0) for comp in range(comps)
        ]
        lw = level_weights(off[0], frac[0])
        rw = offset_weights(off[1], frac[1], wide)
        cw = offset_weights(off[2], frac[2], wide)
        total = [jnp.zeros((levels, lanes), jnp.float32) for comp in range(comps)]
        for across in range(taps):
            for above in range(5):
                pair = lw[above] * rw[across]
                for comp in range(comps):
                    inner = cw[0] * shifted[above, comp, i + across]
                    for e in range(1, taps):
                        inner = inner + cw[e] * shifted[e * 5 + above, comp, i + across]
                    total[comp] = total[comp] + pair * inner
        off = [wind_main(second_v, comp, i) for comp in range(comps)]
        frac = [
            jnp.clip(
                -(wind[comp] + total[comp]) * 0.5 - off[comp].astype(jnp.float32), 0.0, 1.0
            )
            for comp in range(comps)
        ]
        for n, weight in enumerate(level_weights(off[0], frac[0])):
            lev_w[n, i] = weight
        for n, weight in enumerate(offset_weights(off[1], frac[1], narrow)):
            row_w[n, i] = weight
        for n, weight in enumerate(cubic_weights(frac[2])):
            col_w[n, i] = weight
        col_at[i] = off[2] - 1 + column
        return carry

    lax.fori_loop(0, rows, wind_row, 0)

    for copy in tracer_sides:
        copy.wait_recv()

    @pl.when(has_north)
    def _():
        for copy in tracer_south:
            copy.wait_recv()

    @pl.when(has_south)
    def _():
        for copy in tracer_north:
            copy.wait_recv()

    from_west16 = lane16 % 16 < 8

    def put_split(r, merged, main):
        turned = [merged] + [
            pltpu.roll(merged, lanes - 16 * s, 1) for s in range(1, levels)
        ]
        for level in range(levels):
            value = main(level)
            top = value.astype(jnp.bfloat16)
            lhs[level, r, :, 0:lanes] = top
            lhs[level, r, :, lanes : 2 * lanes] = (value - top.astype(jnp.float32)).astype(jnp.bfloat16)
            edge = jnp.where(
                lane16 < 16,
                turned[level],
                jnp.where(lane16 < 32, turned[(level - 1) % levels], turned[(level - 2) % levels]),
            )
            edge_top = edge.astype(jnp.bfloat16).astype(jnp.float32)
            edge = jnp.where(lane16 < 32, edge_top, edge - edge_top)
            lhs[level, r, :, 2 * lanes : 3 * lanes] = edge.astype(jnp.bfloat16)

    def split_row(r, carry):
        merged = jnp.where(from_west16, tracer_side[0, r], tracer_side[1, r])
        put_split(narrow + r, merged, lambda level: tracer_main(level, r))
        return carry

    lax.fori_loop(0, rows, split_row, 0)

    def split_far(place, present, start):
        def far_row(r, carry):
            merged = jnp.where(from_west16, tracer_diag[place, 0, r], tracer_diag[place, 1, r])
            merged = jnp.where(present, merged, 0.0)
            put_split(
                start + r, merged, lambda level: jnp.where(present, tracer_far[place, r, level], 0.0)
            )
            return carry

        lax.fori_loop(0, narrow, far_row, 0)

    split_far(0, has_north, 0)
    split_far(1, has_south, narrow + rows)

    deep, across16 = (
        lax.broadcasted_iota(jnp.int32, (16, lanes), 0),
        lax.broadcasted_iota(jnp.int32, (16, lanes), 1),
    )
    groups = lanes // 16
    for t in range(groups):
        near = jnp.abs(16 * t + deep - across16) <= narrow
        masks[t] = jnp.where(near, 1.0, 0.0).astype(jnp.bfloat16)
    outer = jnp.where(deep < 8, deep - 8, deep + (lanes - 8))
    masks[groups] = jnp.where(jnp.abs(outer - across16) <= narrow, 1.0, 0.0).astype(jnp.bfloat16)
    rhs_a[...] = jnp.zeros_like(rhs_a)
    rhs_b[...] = jnp.zeros_like(rhs_b)
    deep8 = lax.broadcasted_iota(jnp.int32, (8, lanes), 0)

    def build(level, pair, rhs):
        for side in range(2):
            i = pair * 2 + side
            cols = slice(side * lanes, (side + 1) * lanes)
            at = col_at[i, pl.ds(level, 1), :]
            away = jnp.bitwise_and(deep8 - at, 7)
            value = jnp.zeros((8, lanes), jnp.float32)
            for n in range(4):
                value = jnp.where(away == n, col_w[n, i, pl.ds(level, 1), :], value)
            rest = value - value.astype(jnp.bfloat16).astype(jnp.float32)
            top16 = jnp.concatenate([value, value], axis=0).astype(jnp.bfloat16)
            rest16 = jnp.concatenate([rest, rest], axis=0).astype(jnp.bfloat16)
            for t in range(groups):
                top = top16 * masks[t]
                rhs[16 * t : 16 * t + 16, cols] = top
                rhs[2 * lanes + 16 * t : 2 * lanes + 16 * t + 16, cols] = top
                rhs[lanes + 16 * t : lanes + 16 * t + 16, cols] = rest16 * masks[t]
            top = top16 * masks[groups]
            rhs[3 * lanes : 3 * lanes + 16, cols] = top
            rhs[3 * lanes + 16 : 3 * lanes + 32, cols] = rest16 * masks[groups]
            rhs[3 * lanes + 32 : 3 * lanes + 48, cols] = top

    span = reach + 1

    def apply(level, pair, rhs):
        low, high = max(level - 2, 0), min(level + 2, levels - 1)
        count = high - low + 1
        part = lambda at: lhs[low : high + 1, pl.ds(pair * 2, span), :, at * lanes : (at + 1) * lanes].reshape(
            count * span * chans, lanes
        )
        top, rest, edge = part(0), part(1), part(2)
        left = jnp.concatenate([top, top, rest, edge], axis=1)
        done = jnp.dot(left, rhs[...], preferred_element_type=jnp.float32)
        for side in range(2):
            i = pair * 2 + side
            cols = slice(side * lanes, (side + 1) * lanes)
            rw = [row_w[n, i, pl.ds(level, 1), :] for n in range(reach)]
            total = jnp.zeros((chans, lanes), jnp.float32)
            for m in range(count):
                lw = None
                for n in range(5):
                    if min(max(level - 2 + n, 0), levels - 1) == low + m:
                        weight = lev_w[n, i, pl.ds(level, 1), :]
                        lw = weight if lw is None else lw + weight
                inner = jnp.zeros((chans, lanes), jnp.float32)
                for n in range(reach):
                    start = (m * span + n + side) * chans
                    inner = inner + rw[n] * done[start : start + chans, cols]
                total = total + lw * inner
            moved_ref[pl.ds(i * chans * levels + level, chans, stride=levels), :] = total

    pairs = rows // 2
    for level in range(levels):
        build(level, 0, rhs_a)

        def both(q, carry, level=level):
            build(level, 2 * q + 1, rhs_b)
            apply(level, 2 * q, rhs_a)
            build(level, jnp.minimum(2 * q + 2, pairs - 1), rhs_a)
            apply(level, 2 * q + 1, rhs_b)
            return carry

        lax.fori_loop(0, pairs // 2, both, 0)

    for copy in wind_sides + tracer_sides:
        copy.wait_send()

    @pl.when(has_north)
    def _():
        for copy in wind_north + tracer_north:
            copy.wait_send()

    @pl.when(has_south)
    def _():
        for copy in wind_south + tracer_south:
            copy.wait_send()

    def finish(n, carry):
        p = lax.rem(me + n, devices)
        where = (p // lon_count, lax.rem(p, lon_count))
        item_copy(p).wait_send()
        mark_copy(p).wait_send()
        pltpu.make_async_remote_copy(
            src_ref=outgoing.at[p], dst_ref=arrived_ref.at[p],
            send_sem=item_send.at[p], recv_sem=item_recv.at[p],
            device_id=where, device_id_type=MESH,
        ).wait_recv()
        pltpu.make_async_remote_copy(
            src_ref=marks_v, dst_ref=labels_ref.at[p],
            send_sem=mark_send.at[p], recv_sem=mark_recv.at[p],
            device_id=where, device_id_type=MESH,
        ).wait_recv()
        return carry

    lax.fori_loop(1, devices, finish, 0)


def join_kernel(dims, moved_ref, arrived_ref, labels_ref, out_ref, total):
    chans, levels, rows, blocks = dims
    me = lax.axis_index("lat") * lax.axis_size("lon") + lax.axis_index("lon")
    depth = chans * levels
    for s in range(rows):
        total[s] = moved_ref[s * depth : (s + 1) * depth, :]

    def add(n, carry):
        for c in range(CAP):
            label = labels_ref[n, c, me]
            at = jnp.where(label < 0, blocks, label)
            total[at] = total[at] + arrived_ref[n, c].astype(jnp.float32)
        return carry

    lax.fori_loop(0, arrived_ref.shape[0], add, 0)
    for s in range(rows):
        for g in range(depth // 8):
            out_ref[pl.ds(g * 8 * rows + s, 8, stride=rows), :] = total[s, g * 8 : g * 8 + 8, :]


def body(
    tracers, winds, depart_first, depart_second, fluxes, remap_weights, target_device, target_block
):
    wide = HMAX + 1
    narrow = max((HMAX + 1) // 2 + 1, HMAX // 2 + 2)
    chans, levels, rows, lanes = tracers.shape
    comps = winds.shape[0]
    tiles, links = target_device.shape
    depth, cells = fluxes.shape[1:]
    cols = remap_weights.shape[3]
    blocks = rows * lanes // cols
    devices = lax.axis_size("lat") * lax.axis_size("lon")
    height = rows + 2 * narrow
    padded = -(-devices // LANES) * LANES
    dims = (chans, levels, rows, comps, tiles, links, blocks, wide, narrow)
    flat = lambda array: array.reshape(-1, lanes)
    hbm = pl.BlockSpec(memory_space=pl.ANY)
    vmem = pl.BlockSpec(memory_space=pltpu.VMEM)
    smem = pl.BlockSpec(memory_space=pltpu.SMEM)
    f32, b16, i32 = jnp.float32, jnp.bfloat16, jnp.int32
    dma = pltpu.SemaphoreType.DMA
    moved, arrived, labels = pl.pallas_call(
        functools.partial(step_kernel, dims),
        out_shape=(
            jax.ShapeDtypeStruct((chans * levels * rows, lanes), f32),
            jax.ShapeDtypeStruct((devices, CAP, depth, cols), b16),
            jax.ShapeDtypeStruct((devices, CAP, padded), i32),
        ),
        in_specs=[hbm] * 6 + [smem] * 2,
        out_specs=(vmem, vmem, vmem),
        scratch_shapes=[
            pltpu.VMEM((comps * levels * rows, lanes), f32),
            pltpu.VMEM((comps * levels * rows, lanes), i32),
            pltpu.VMEM((comps * levels * rows, lanes), i32),
            pltpu.VMEM((chans * levels * rows, lanes), f32),
            pltpu.VMEM((tiles, depth, cells), b16),
            pltpu.VMEM((tiles * links, cells, cols), b16),
            pltpu.VMEM((devices, CAP, depth, cols), b16),
            pltpu.VMEM((CAP, padded), i32),
            pltpu.SMEM((CAP, padded), i32),
            pltpu.VMEM((CAP, padded), i32),
            pltpu.VMEM((rows // 8, comps, levels, lanes), f32),
            pltpu.VMEM((2, comps, wide, levels, lanes), f32),
            pltpu.VMEM((rows, chans, lanes), f32),
            pltpu.VMEM((2, narrow, levels, chans, lanes), f32),
            pltpu.VMEM((2, rows // 8, comps, levels, lanes), f32),
            pltpu.VMEM((2, 2, comps, levels, lanes), f32),
            pltpu.VMEM((2, comps, wide, levels, lanes), f32),
            pltpu.VMEM((2, rows, chans, lanes), f32),
            pltpu.VMEM((2, 2, narrow, chans, lanes), f32),
            pltpu.VMEM((2, narrow, levels, chans, lanes), f32),
            pltpu.VMEM((5 * (2 * wide + 1), comps, rows + 2 * wide, levels, lanes), f32),
            pltpu.VMEM((levels, height, chans, 3 * lanes), b16),
            pltpu.VMEM((4 * lanes, 2 * lanes), b16),
            pltpu.VMEM((4 * lanes, 2 * lanes), b16),
            pltpu.VMEM((lanes // 16 + 1, 16, lanes), b16),
            pltpu.VMEM((5, rows, levels, lanes), f32),
            pltpu.VMEM((2 * narrow + 1, rows, levels, lanes), f32),
            pltpu.VMEM((4, rows, levels, lanes), f32),
            pltpu.VMEM((rows, levels, lanes), i32),
            dma((6,)),
            dma(()),
            dma((16,)),
            dma((16,)),
            dma((devices,)),
            dma((devices,)),
            dma((devices,)),
            dma((devices,)),
        ],
        compiler_params=pltpu.CompilerParams(
            collective_id=0, has_side_effects=True, vmem_limit_bytes=62 * 1024 * 1024
        ),
        name="step",
    )(
        flat(winds), flat(depart_first), flat(depart_second), flat(tracers), fluxes,
        remap_weights.reshape(tiles * links, cells, cols), target_device, target_block,
    )
    out = pl.pallas_call(
        functools.partial(join_kernel, (chans, levels, rows, blocks)),
        out_shape=jax.ShapeDtypeStruct((chans * levels * rows, lanes), f32),
        in_specs=[vmem, vmem, smem],
        out_specs=vmem,
        scratch_shapes=[pltpu.VMEM((blocks + 1, chans * levels, lanes), f32)],
        name="join",
    )(moved, arrived, labels)
    return out.reshape(chans, levels, rows, lanes)


def solution(mesh):
    in_specs = (
        P(None, None, "lat", "lon"),
        P(None, None, "lat", "lon"),
        P(None, None, "lat", "lon"),
        P(None, None, "lat", "lon"),
        P(("lat", "lon"), None, None),
        P(("lat", "lon"), None, None, None),
        P(("lat", "lon"), None),
        P(("lat", "lon"), None),
    )
    out_specs = P(None, None, "lat", "lon")
    return jax.shard_map(body, mesh=mesh, in_specs=in_specs, out_specs=out_specs, check_vma=False)
```

```python
import functools

import jax
import jax.numpy as jnp
from jax import lax
from jax.experimental import pallas as pl
from jax.experimental.pallas import tpu as pltpu
from jax.sharding import PartitionSpec as P

CAP = 2
HMAX = 3
MESH = pl.DeviceIdType.MESH
LANES = 128
BIG = 1 << 20


def cubic_weights(frac):
    first = -frac * (frac - 1.0) * (frac - 2.0) / 6.0
    second = (frac + 1.0) * (frac - 1.0) * (frac - 2.0) / 2.0
    third = -(frac + 1.0) * frac * (frac - 2.0) / 2.0
    fourth = (frac + 1.0) * frac * (frac - 1.0) / 6.0
    return (first, second, third, fourth)


def level_weights(offset, frac):
    s0, s1, s2, s3 = cubic_weights(frac)
    down = offset < 0
    zero = jnp.zeros_like(frac)
    return [
        jnp.where(down, s0, zero),
        jnp.where(down, s1, s0),
        jnp.where(down, s2, s1),
        jnp.where(down, s3, s2),
        jnp.where(down, zero, s3),
    ]


def offset_weights(offset, frac, reach):
    stencil = cubic_weights(frac)
    spread = []
    for target in range(-reach, reach + 1):
        weight = jnp.zeros(frac.shape, jnp.float32)
        for step in range(4):
            weight = jnp.where(offset == target - step + 1, stencil[step], weight)
        spread.append(weight)
    return spread


def step_kernel(
    dims,
    winds_hbm, first_hbm, second_hbm, tracers_hbm, fluxes_hbm, weights_hbm, owner_ref, block_ref,
    moved_ref, arrived_ref, labels_ref,
    wind_pad, first_v, second_v, tracer_pad, fluxes_v, weights_v,
    products, outgoing, codes_v, codes_s, marks_v,
    wind_pack, tracer_pack, wind_edge, tracer_edge,
    shifted, lhs, rhs_a, rhs_b, masks, wind_w, wind_sum, lev_w, row_w, col_w, col_at, moved_v,
    wind_sem, tracer_sem, first_sem, second_sem, load_sem, code_sem, moved_sem,
    halo_send, halo_recv, item_send, item_recv, mark_send, mark_recv,
):
    chans, levels, rows, comps, tiles, links, blocks, wide, narrow = dims
    lanes = LANES
    taps, reach = 2 * wide + 1, 2 * narrow + 1
    lat, lon = lax.axis_index("lat"), lax.axis_index("lon")
    lat_count, lon_count = lax.axis_size("lat"), lax.axis_size("lon")
    devices = lat_count * lon_count
    me = lat * lon_count + lon

    def by_level(source, target, sem, start):
        return [
            pltpu.make_async_copy(
                source.at[:, level], target.at[:, pl.ds(start, rows), level, :], sem.at[level]
            )
            for level in range(levels)
        ]

    wind_loads = by_level(winds_hbm, wind_pad, wind_sem, wide)
    tracer_loads = [
        pltpu.make_async_copy(
            tracers_hbm.at[chan], tracer_pad.at[:, pl.ds(narrow, rows), chan, :], tracer_sem.at[chan]
        )
        for chan in range(chans)
    ]
    flux_load = pltpu.make_async_copy(fluxes_hbm, fluxes_v, load_sem.at[0])
    weight_load = pltpu.make_async_copy(weights_hbm, weights_v, load_sem.at[1])
    late_loads = by_level(first_hbm, first_v, first_sem, 0) + by_level(second_hbm, second_v, second_sem, 0)
    for load in wind_loads + tracer_loads + [flux_load, weight_load] + late_loads:
        load.start()

    barrier = pltpu.get_barrier_semaphore()

    def greet(k, carry):
        p = lax.rem(me + k, devices)
        pl.semaphore_signal(
            barrier, inc=1, device_id=(p // lon_count, lax.rem(p, lon_count)), device_id_type=MESH
        )
        return carry

    lax.fori_loop(1, devices, greet, 0)

    width = codes_v.shape[1]
    spot = lax.broadcasted_iota(jnp.int32, (1, width), 1)
    lowest = jnp.full((1, width), BIG, jnp.int32)
    highest = jnp.full((1, width), -1, jnp.int32)
    for t in range(tiles):
        for k in range(links):
            code = (t * links + k) * blocks + block_ref[k, t]
            hit = spot == owner_ref[k, t]
            lowest = jnp.minimum(lowest, jnp.where(hit, code, BIG))
            highest = jnp.maximum(highest, jnp.where(hit, code, -1))
    used = highest >= 0
    twice = highest != lowest
    low_code = jnp.where(used, lowest, 0)
    high_code = jnp.where(used, highest, 0)
    codes_v[...] = jnp.concatenate([low_code // blocks, high_code // blocks], axis=0)
    marks_v[...] = jnp.concatenate(
        [
            jnp.where(used, low_code % blocks, -1),
            jnp.where(jnp.logical_and(used, twice), high_code % blocks, -1),
        ],
        axis=0,
    )
    code_copy = pltpu.make_async_copy(codes_v, codes_s, code_sem)
    code_copy.start()

    lane8 = lax.broadcasted_iota(jnp.int32, (levels, lanes), 1)
    lane16 = lax.broadcasted_iota(jnp.int32, (chans, lanes), 1)
    west, east = lax.rem(lon + lon_count - 1, lon_count), lax.rem(lon + 1, lon_count)
    north, south = lat - 1, lat + 1
    has_north, has_south = lat > 0, lat < lat_count - 1
    halves = rows // 8

    for load in wind_loads:
        load.wait()
    for half in range(halves):
        for comp in range(comps):
            packed = jnp.zeros((levels, lanes), jnp.float32)
            for p in range(8):
                value = wind_pad[comp, wide + half * 8 + p]
                packed = jnp.where(
                    lane8 // 16 == p, pltpu.roll(value, (16 * p + 8) % lanes, 1), packed
                )
            wind_pack[half, comp] = packed
    for load in tracer_loads:
        load.wait()

    def pack_row(r, carry):
        for side in range(2):
            packed = jnp.zeros((chans, lanes), jnp.float32)
            for level in range(levels):
                value = tracer_pad[level, narrow + 2 * r + side]
                packed = jnp.where(
                    lane16 // 16 == level, pltpu.roll(value, (16 * level + 8) % lanes, 1), packed
                )
            tracer_pack[2 * r + side] = packed
        return carry

    lax.fori_loop(0, rows // 2, pack_row, 0)

    @pl.when(jnp.logical_not(has_north))
    def _():
        wind_pad[:, 0:wide] = jnp.zeros((comps, wide, levels, lanes), jnp.float32)
        wind_edge[:, 0] = jnp.zeros((2, comps, levels, lanes), jnp.float32)
        tracer_pad[:, 0:narrow] = jnp.zeros((levels, narrow, chans, lanes), jnp.float32)
        tracer_edge[:, 0:narrow] = jnp.zeros((2, narrow, chans, lanes), jnp.float32)

    @pl.when(jnp.logical_not(has_south))
    def _():
        wind_pad[:, wide + rows :] = jnp.zeros((comps, wide, levels, lanes), jnp.float32)
        wind_edge[:, halves + 1] = jnp.zeros((2, comps, levels, lanes), jnp.float32)
        tracer_pad[:, narrow + rows :] = jnp.zeros((levels, narrow, chans, lanes), jnp.float32)
        tracer_edge[:, narrow + rows :] = jnp.zeros((2, narrow, chans, lanes), jnp.float32)

    pl.semaphore_wait(barrier, devices - 1)

    def halo(n, source, target, where):
        return pltpu.make_async_remote_copy(
            src_ref=source, dst_ref=target, send_sem=halo_send.at[n], recv_sem=halo_recv.at[n],
            device_id=where, device_id_type=MESH,
        )

    wind_sides = [
        halo(0, wind_pack, wind_edge.at[0, pl.ds(1, halves)], (lat, east)),
        halo(1, wind_pack, wind_edge.at[1, pl.ds(1, halves)], (lat, west)),
    ]
    wind_north = [
        halo(2, wind_pad.at[:, pl.ds(wide, wide)], wind_pad.at[:, pl.ds(wide + rows, wide)], (north, lon)),
        halo(3, wind_pack.at[0], wind_edge.at[0, halves + 1], (north, east)),
        halo(4, wind_pack.at[0], wind_edge.at[1, halves + 1], (north, west)),
    ]
    wind_south = [
        halo(5, wind_pad.at[:, pl.ds(rows, wide)], wind_pad.at[:, pl.ds(0, wide)], (south, lon)),
        halo(6, wind_pack.at[halves - 1], wind_edge.at[0, 0], (south, east)),
        halo(7, wind_pack.at[halves - 1], wind_edge.at[1, 0], (south, west)),
    ]
    first_rows, last_rows = pl.ds(0, narrow), pl.ds(rows - narrow, narrow)
    above_rows, below_rows = pl.ds(0, narrow), pl.ds(narrow + rows, narrow)
    tracer_sides = [
        halo(8, tracer_pack, tracer_edge.at[0, pl.ds(narrow, rows)], (lat, east)),
        halo(9, tracer_pack, tracer_edge.at[1, pl.ds(narrow, rows)], (lat, west)),
    ]
    tracer_north = [
        halo(10, tracer_pad.at[:, pl.ds(narrow, narrow)], tracer_pad.at[:, below_rows], (north, lon)),
        halo(11, tracer_pack.at[first_rows], tracer_edge.at[0, below_rows], (north, east)),
        halo(12, tracer_pack.at[first_rows], tracer_edge.at[1, below_rows], (north, west)),
    ]
    tracer_south = [
        halo(13, tracer_pad.at[:, pl.ds(rows, narrow)], tracer_pad.at[:, above_rows], (south, lon)),
        halo(14, tracer_pack.at[last_rows], tracer_edge.at[0, above_rows], (south, east)),
        halo(15, tracer_pack.at[last_rows], tracer_edge.at[1, above_rows], (south, west)),
    ]

    def each(condition, copies, act):
        @pl.when(condition)
        def _():
            for copy in copies:
                act(copy)

    start, arrive, leave = (lambda c: c.start()), (lambda c: c.wait_recv()), (lambda c: c.wait_send())
    each(has_north, wind_north, start)
    each(has_south, wind_south, start)
    for copy in wind_sides:
        copy.start()
    each(has_north, tracer_north, start)
    each(has_south, tracer_south, start)
    for copy in tracer_sides:
        copy.start()

    code_copy.wait()
    flux_load.wait()
    weight_load.wait()
    group = 3 if tiles % 3 == 0 else 1

    def multiply(n, carry):
        for g in range(group):
            t = n * group + g
            right = jnp.concatenate([weights_v[t, k] for k in range(links)], axis=1)
            done = jnp.dot(fluxes_v[t], right, preferred_element_type=jnp.float32)
            for k in range(links):
                products[t * links + k] = done[:, k * lanes : (k + 1) * lanes].astype(jnp.bfloat16)
        return carry

    lax.fori_loop(0, tiles // group, multiply, 0)

    def item_copy(p):
        return pltpu.make_async_remote_copy(
            src_ref=outgoing.at[p], dst_ref=arrived_ref.at[me],
            send_sem=item_send.at[p], recv_sem=item_recv.at[me],
            device_id=(p // lon_count, lax.rem(p, lon_count)), device_id_type=MESH,
        )

    def mark_copy(p):
        return pltpu.make_async_remote_copy(
            src_ref=marks_v, dst_ref=labels_ref.at[me],
            send_sem=mark_send.at[p], recv_sem=mark_recv.at[me],
            device_id=(p // lon_count, lax.rem(p, lon_count)), device_id_type=MESH,
        )

    middle = lat_count // 2
    away = sorted(range(lat_count), key=lambda n: abs(n - middle))
    last = None

    def peer(there, n):
        return there * lon_count + lax.rem(lon + n, lon_count)

    for far in away:
        there = lax.rem(lat + far, lat_count)

        def emit(n, carry, there=there):
            p = peer(there, n)
            for c in range(CAP):
                outgoing[p, c] = products[codes_s[c, p]]
            before = peer(there, n - 1)

            @pl.when(n > 1)
            def _():
                item_copy(before).start()

            mark_copy(p).start()
            return carry

        if last is not None:
            for c in range(CAP):
                outgoing[peer(there, 0), c] = products[codes_s[c, peer(there, 0)]]
            item_copy(last).start()
            if far:
                item_copy(peer(there, 0)).start()
                mark_copy(peer(there, 0)).start()
        else:
            for c in range(CAP):
                outgoing[peer(there, 0), c] = products[codes_s[c, peer(there, 0)]]
            item_copy(peer(there, 0)).start()
            mark_copy(peer(there, 0)).start()
        lax.fori_loop(1, lon_count, emit, 0)
        last = peer(there, lon_count - 1)
    item_copy(last).start()
    own_items = pltpu.make_async_copy(outgoing.at[me], arrived_ref.at[me], item_recv.at[me])
    own_items.start()
    own_marks = pltpu.make_async_copy(marks_v, labels_ref.at[me], mark_recv.at[me])
    own_marks.start()

    deep, across16 = (
        lax.broadcasted_iota(jnp.int32, (16, lanes), 0),
        lax.broadcasted_iota(jnp.int32, (16, lanes), 1),
    )
    groups = lanes // 16
    for t in range(groups):
        near = jnp.abs(16 * t + deep - across16) <= narrow
        masks[t] = jnp.where(near, 1.0, 0.0).astype(jnp.bfloat16)
    outer = jnp.where(deep < 8, deep - 8, deep + (lanes - 8))
    masks[groups] = jnp.where(jnp.abs(outer - across16) <= narrow, 1.0, 0.0).astype(jnp.bfloat16)
    rhs_a[...] = jnp.zeros_like(rhs_a)
    rhs_b[...] = jnp.zeros_like(rhs_b)

    for load in late_loads:
        load.wait()
    for copy in wind_sides:
        copy.wait_recv()
    each(has_north, wind_south, arrive)
    each(has_south, wind_north, arrive)

    def shift_row(r, carry):
        turned = r + 8 - wide
        half, p = turned // 8, turned % 8
        back = lax.rem(2 * lanes - 8 - 16 * p, lanes)
        for comp in range(comps):
            merged = jnp.where(lane8 % 16 < 8, wind_edge[0, half, comp], wind_edge[1, half, comp])
            edge = pltpu.roll(merged, back, 1)
            main = wind_pad[comp, r]
            for e in range(taps):
                d = e - wide
                if d > 0:
                    piece = pltpu.roll(jnp.where(lane8 < d, edge, main), lanes - d, 1)
                elif d < 0:
                    piece = pltpu.roll(jnp.where(lane8 >= lanes + d, edge, main), -d, 1)
                else:
                    piece = main
                low, high = piece[:1], piece[levels - 1 :]
                shifted[e * 5 + 0, comp, r] = jnp.concatenate([low, low, piece[: levels - 2]], axis=0)
                shifted[e * 5 + 1, comp, r] = jnp.concatenate([low, piece[: levels - 1]], axis=0)
                shifted[e * 5 + 2, comp, r] = piece
                shifted[e * 5 + 3, comp, r] = jnp.concatenate([piece[1:], high], axis=0)
                shifted[e * 5 + 4, comp, r] = jnp.concatenate([piece[2:], high, high], axis=0)
        return carry

    lax.fori_loop(0, rows + 2 * wide, shift_row, 0)

    column = lax.broadcasted_iota(jnp.int32, (levels, lanes), 1)

    def wind_start(side, i):
        off = [first_v[comp, i] for comp in range(comps)]
        frac = [
            jnp.clip(-wind_pad[comp, wide + i] - off[comp].astype(jnp.float32), 0.0, 1.0)
            for comp in range(comps)
        ]
        weights = level_weights(off[0], frac[0])
        weights += offset_weights(off[1], frac[1], wide) + offset_weights(off[2], frac[2], wide)
        for n, weight in enumerate(weights):
            wind_w[side, n] = weight
        for comp in range(comps):
            wind_sum[side, comp] = jnp.zeros((levels, lanes), jnp.float32)

    def wind_unit(first, q):
        sides = [side for side in range(2) if 0 <= q - side < taps]
        cw = [[wind_w[side, 5 + taps + e] for e in range(taps)] for side in sides]
        rw = [wind_w[side, 5 + q - side] for side in sides]
        total = [[wind_sum[side, comp] for comp in range(comps)] for side in sides]
        for above in range(5):
            pair = [wind_w[side, above] * rw[n] for n, side in enumerate(sides)]
            for comp in range(comps):
                inner = [None] * len(sides)
                for e in range(taps):
                    value = shifted[e * 5 + above, comp, first + q]
                    for n in range(len(sides)):
                        term = cw[n][e] * value
                        inner[n] = term if e == 0 else inner[n] + term
                for n in range(len(sides)):
                    total[n][comp] = total[n][comp] + pair[n] * inner[n]
        for n, side in enumerate(sides):
            for comp in range(comps):
                wind_sum[side, comp] = total[n][comp]

    def wind_finish(side, i):
        off = [second_v[comp, i] for comp in range(comps)]
        frac = [
            jnp.clip(
                -(wind_pad[comp, wide + i] + wind_sum[side, comp]) * 0.5
                - off[comp].astype(jnp.float32),
                0.0,
                1.0,
            )
            for comp in range(comps)
        ]
        for n, weight in enumerate(level_weights(off[0], frac[0])):
            lev_w[n, i] = weight
        for n, weight in enumerate(offset_weights(off[1], frac[1], narrow)):
            row_w[n, i] = weight
        for n, weight in enumerate(cubic_weights(frac[2])):
            col_w[n, i] = weight
        col_at[i] = off[2] - 1 + column

    for side in range(2):
        wind_start(side, side)

    wind_unit(0, 0)
    for q in range(1, taps):
        wind_unit(0, q)
    wind_unit(0, taps)
    for side in range(2):
        wind_finish(side, side)

    for copy in tracer_sides:
        copy.wait_recv()
    each(has_north, tracer_south, arrive)
    each(has_south, tracer_north, arrive)

    def split_row(r, carry):
        merged = jnp.where(lane16 % 16 < 8, tracer_edge[0, r], tracer_edge[1, r])
        turned = [merged] + [pltpu.roll(merged, lanes - 16 * s, 1) for s in range(1, levels)]
        for level in range(levels):
            value = tracer_pad[level, r]
            top = value.astype(jnp.bfloat16)
            lhs[level, r, :, 0:lanes] = top
            lhs[level, r, :, lanes : 2 * lanes] = (value - top.astype(jnp.float32)).astype(jnp.bfloat16)
            edge = jnp.where(
                lane16 < 16,
                turned[level],
                jnp.where(lane16 < 32, turned[(level - 1) % levels], turned[(level - 2) % levels]),
            )
            edge_top = edge.astype(jnp.bfloat16).astype(jnp.float32)
            edge = jnp.where(lane16 < 32, edge_top, edge - edge_top)
            lhs[level, r, :, 2 * lanes : 3 * lanes] = edge.astype(jnp.bfloat16)
        return carry

    lax.fori_loop(0, rows + 2 * narrow, split_row, 0)

    deep8 = lax.broadcasted_iota(jnp.int32, (8, lanes), 0)

    def build(level, pair, rhs):
        for side in range(2):
            i = pair * 2 + side
            cols = slice(side * lanes, (side + 1) * lanes)
            at = col_at[i, pl.ds(level, 1), :]
            away = jnp.bitwise_and(deep8 - at, 7)
            value = jnp.zeros((8, lanes), jnp.float32)
            for n in range(4):
                value = jnp.where(away == n, col_w[n, i, pl.ds(level, 1), :], value)
            rest = value - value.astype(jnp.bfloat16).astype(jnp.float32)
            top16 = jnp.concatenate([value, value], axis=0).astype(jnp.bfloat16)
            rest16 = jnp.concatenate([rest, rest], axis=0).astype(jnp.bfloat16)
            for t in range(groups):
                top = top16 * masks[t]
                rhs[16 * t : 16 * t + 16, cols] = top
                rhs[2 * lanes + 16 * t : 2 * lanes + 16 * t + 16, cols] = top
                rhs[lanes + 16 * t : lanes + 16 * t + 16, cols] = rest16 * masks[t]
            top = top16 * masks[groups]
            rhs[3 * lanes : 3 * lanes + 16, cols] = top
            rhs[3 * lanes + 16 : 3 * lanes + 32, cols] = rest16 * masks[groups]
            rhs[3 * lanes + 32 : 3 * lanes + 48, cols] = top

    span = reach + 1

    def apply(level, pair, rhs):
        low, high = max(level - 2, 0), min(level + 2, levels - 1)
        count = high - low + 1
        part = lambda at: lhs[
            low : high + 1, pl.ds(pair * 2, span), :, at * lanes : (at + 1) * lanes
        ].reshape(count * span * chans, lanes)
        top, rest, edge = part(0), part(1), part(2)
        left = jnp.concatenate([top, top, rest, edge], axis=1)
        done = jnp.dot(left, rhs[...], preferred_element_type=jnp.float32)
        for side in range(2):
            i = pair * 2 + side
            cols = slice(side * lanes, (side + 1) * lanes)
            rw = [row_w[n, i, pl.ds(level, 1), :] for n in range(reach)]
            total = jnp.zeros((chans, lanes), jnp.float32)
            for m in range(count):
                lw = None
                for n in range(5):
                    if min(max(level - 2 + n, 0), levels - 1) == low + m:
                        weight = lev_w[n, i, pl.ds(level, 1), :]
                        lw = weight if lw is None else lw + weight
                inner = jnp.zeros((chans, lanes), jnp.float32)
                for n in range(reach):
                    first = (m * span + n + side) * chans
                    inner = inner + rw[n] * done[first : first + chans, cols]
                total = total + lw * inner
            moved_v[i, level] = total

    pairs = rows // 2
    shares = levels - 1
    cuts = [(n * (taps + 1) + shares // 2) // shares for n in range(shares + 1)]
    both = [rhs_a, rhs_b]
    build(0, 0, rhs_a)

    def moved_copy(pair):
        return pltpu.make_async_copy(
            moved_v.at[pl.ds(pair * 2, 2)], moved_ref.at[pl.ds(pair * 2, 2)], moved_sem.at[pair]
        )

    def pair_step(pair, carry):
        after = jnp.minimum(pair + 1, pairs - 1)
        def level_step(level):
            if level == 0:
                for side in range(2):
                    wind_start(side, after * 2 + side)
            if level < shares:
                for q in range(cuts[level], cuts[level + 1]):
                    wind_unit(after * 2, q)
            if level == shares - 1:
                for side in range(2):
                    wind_finish(side, after * 2 + side)
            if level < levels - 1:
                build(level + 1, pair, both[(level + 1) % 2])
            else:
                build(0, after, both[0])
            apply(level, pair, both[level % 2])

        for level in range(levels):
            pl.when(pair >= 0)(functools.partial(level_step, level))
        moved_copy(pair).start()
        return carry

    lax.fori_loop(0, pairs, pair_step, 0)
    for pair in range(pairs):
        moved_copy(pair).wait()

    for copy in wind_sides + tracer_sides:
        copy.wait_send()
    each(has_north, wind_north + tracer_north, leave)
    each(has_south, wind_south + tracer_south, leave)
    own_items.wait()
    own_marks.wait()

    def finish(n, carry):
        p = lax.rem(me + n, devices)
        where = (p // lon_count, lax.rem(p, lon_count))
        item_copy(p).wait_send()
        mark_copy(p).wait_send()
        pltpu.make_async_remote_copy(
            src_ref=outgoing.at[p], dst_ref=arrived_ref.at[p],
            send_sem=item_send.at[p], recv_sem=item_recv.at[p],
            device_id=where, device_id_type=MESH,
        ).wait_recv()
        pltpu.make_async_remote_copy(
            src_ref=marks_v, dst_ref=labels_ref.at[p],
            send_sem=mark_send.at[p], recv_sem=mark_recv.at[p],
            device_id=where, device_id_type=MESH,
        ).wait_recv()
        return carry

    lax.fori_loop(1, devices, finish, 0)


def join_kernel(dims, moved_hbm, arrived_hbm, labels_ref, out_hbm, total, more, arrived, moved_sem, item_sem, out_sem):
    chans, levels, rows, blocks, share = dims
    me = lax.axis_index("lat") * lax.axis_size("lon") + lax.axis_index("lon")
    loads = [
        pltpu.make_async_copy(
            moved_hbm.at[:, level], total.at[pl.ds(0, rows), :, level, :], moved_sem.at[level]
        )
        for level in range(levels)
    ]
    for load in loads:
        load.start()
    parts = arrived.shape[0] // share

    def piece(n):
        cut = pl.ds(n * share, share)
        return pltpu.make_async_copy(arrived_hbm.at[cut], arrived.at[cut], item_sem.at[n])

    for n in range(parts):
        piece(n).start()
    more[...] = jnp.zeros_like(more)
    for load in loads:
        load.wait()

    def add(n, carry):
        for c, sums in enumerate((total, more)):
            label = labels_ref[n, c, me]
            at = jnp.where(label < 0, blocks, label)
            sums[at] = sums[at] + arrived[n, c].astype(jnp.float32).reshape(total.shape[1:])
        return carry

    for n in range(parts):
        piece(n).wait()
        lax.fori_loop(n * share, (n + 1) * share, add, 0)
    outs = [
        pltpu.make_async_copy(total.at[s], out_hbm.at[:, :, s, :], out_sem.at[s]) for s in range(rows)
    ]
    for s, out in enumerate(outs):
        total[s] = total[s] + more[s]
        if s:
            outs[s - 1].start()
    outs[rows - 1].start()
    for out in outs:
        out.wait()


def body(
    tracers, winds, depart_first, depart_second, fluxes, remap_weights, target_device, target_block
):
    wide = HMAX + 1
    narrow = max((HMAX + 1) // 2 + 1, HMAX // 2 + 2)
    chans, levels, rows, lanes = tracers.shape
    comps = winds.shape[0]
    tiles, links = target_device.shape
    depth, cells = fluxes.shape[1:]
    cols = remap_weights.shape[3]
    blocks = rows * lanes // cols
    devices = lax.axis_size("lat") * lax.axis_size("lon")
    padded = -(-devices // LANES) * LANES
    halves = rows // 8
    dims = (chans, levels, rows, comps, tiles, links, blocks, wide, narrow)
    hbm = pl.BlockSpec(memory_space=pl.ANY)
    vmem = pl.BlockSpec(memory_space=pltpu.VMEM)
    smem = pl.BlockSpec(memory_space=pltpu.SMEM)
    f32, b16, i32 = jnp.float32, jnp.bfloat16, jnp.int32
    dma = pltpu.SemaphoreType.DMA
    moved, arrived, labels = pl.pallas_call(
        functools.partial(step_kernel, dims),
        out_shape=(
            jax.ShapeDtypeStruct((rows, levels, chans, lanes), f32),
            jax.ShapeDtypeStruct((devices, CAP, depth, cols), b16),
            jax.ShapeDtypeStruct((devices, CAP, padded), i32),
        ),
        in_specs=[hbm] * 6 + [smem] * 2,
        out_specs=(hbm, hbm, hbm),
        scratch_shapes=[
            pltpu.VMEM((comps, rows + 2 * wide, levels, lanes), f32),
            pltpu.VMEM((comps, rows, levels, lanes), i32),
            pltpu.VMEM((comps, rows, levels, lanes), i32),
            pltpu.VMEM((levels, rows + 2 * narrow, chans, lanes), f32),
            pltpu.VMEM((tiles, depth, cells), b16),
            pltpu.VMEM((tiles, links, cells, cols), b16),
            pltpu.VMEM((tiles * links, depth, cols), b16),
            pltpu.VMEM((devices, CAP, depth, cols), b16),
            pltpu.VMEM((CAP, padded), i32),
            pltpu.SMEM((CAP, padded), i32),
            pltpu.VMEM((CAP, padded), i32),
            pltpu.VMEM((halves, comps, levels, lanes), f32),
            pltpu.VMEM((rows, chans, lanes), f32),
            pltpu.VMEM((2, halves + 2, comps, levels, lanes), f32),
            pltpu.VMEM((2, rows + 2 * narrow, chans, lanes), f32),
            pltpu.VMEM((5 * (2 * wide + 1), comps, rows + 2 * wide, levels, lanes), f32),
            pltpu.VMEM((levels, rows + 2 * narrow, chans, 3 * lanes), b16),
            pltpu.VMEM((4 * lanes, 2 * lanes), b16),
            pltpu.VMEM((4 * lanes, 2 * lanes), b16),
            pltpu.VMEM((lanes // 16 + 1, 16, lanes), b16),
            pltpu.VMEM((2, 5 + 2 * (2 * wide + 1), levels, lanes), f32),
            pltpu.VMEM((2, comps, levels, lanes), f32),
            pltpu.VMEM((5, rows, levels, lanes), f32),
            pltpu.VMEM((2 * narrow + 1, rows, levels, lanes), f32),
            pltpu.VMEM((4, rows, levels, lanes), f32),
            pltpu.VMEM((rows, levels, lanes), i32),
            pltpu.VMEM((rows, levels, chans, lanes), f32),
            dma((levels,)),
            dma((chans,)),
            dma((levels,)),
            dma((levels,)),
            dma((2,)),
            dma(()),
            dma((rows // 2,)),
            dma((16,)),
            dma((16,)),
            dma((devices,)),
            dma((devices,)),
            dma((devices,)),
            dma((devices,)),
        ],
        compiler_params=pltpu.CompilerParams(
            collective_id=0, has_side_effects=True, vmem_limit_bytes=62 * 1024 * 1024
        ),
        name="step",
    )(winds, depart_first, depart_second, tracers, fluxes, remap_weights, target_device.T, target_block.T)
    share = devices // 4 if devices % 4 == 0 else devices
    out = pl.pallas_call(
        functools.partial(join_kernel, (chans, levels, rows, blocks, share)),
        out_shape=jax.ShapeDtypeStruct((chans, levels, rows, lanes), f32),
        in_specs=[hbm, hbm, smem],
        out_specs=hbm,
        scratch_shapes=[
            pltpu.VMEM((blocks + 1, chans, levels, lanes), f32),
            pltpu.VMEM((blocks + 1, chans, levels, lanes), f32),
            pltpu.VMEM((devices, CAP, depth, cols), b16),
            dma((levels,)),
            dma((devices // share,)),
            dma((rows,)),
        ],
        compiler_params=pltpu.CompilerParams(vmem_limit_bytes=62 * 1024 * 1024),
        name="join",
    )(moved, arrived, labels)
    return out


def solution(mesh):
    in_specs = (
        P(None, None, "lat", "lon"),
        P(None, None, "lat", "lon"),
        P(None, None, "lat", "lon"),
        P(None, None, "lat", "lon"),
        P(("lat", "lon"), None, None),
        P(("lat", "lon"), None, None, None),
        P(("lat", "lon"), None),
        P(("lat", "lon"), None),
    )
    out_specs = P(None, None, "lat", "lon")
    return jax.shard_map(body, mesh=mesh, in_specs=in_specs, out_specs=out_specs, check_vma=False)
```

```python
import functools
import math

import jax
import jax.numpy as jnp
from jax import lax
from jax.experimental import pallas as pl
from jax.experimental.pallas import tpu as pltpu
from jax.sharding import PartitionSpec as P

CAP = 2
HMAX = 3
MESH = pl.DeviceIdType.MESH
LANES = 128
BIG = 1 << 20
DIRECT_PART = 48
CODES = 32767.0
ITEM_LOW = 0.049804688 * 0.00019931793
ITEM_HIGH = 5.0 * 0.019897461


def cubic_weights(frac):
    first = -frac * (frac - 1.0) * (frac - 2.0) / 6.0
    second = (frac + 1.0) * (frac - 1.0) * (frac - 2.0) / 2.0
    third = -(frac + 1.0) * frac * (frac - 2.0) / 2.0
    fourth = (frac + 1.0) * frac * (frac - 1.0) / 6.0
    return (first, second, third, fourth)


def level_weights(offset, frac):
    s0, s1, s2, s3 = cubic_weights(frac)
    down = offset < 0
    zero = jnp.zeros_like(frac)
    return [
        jnp.where(down, s0, zero),
        jnp.where(down, s1, s0),
        jnp.where(down, s2, s1),
        jnp.where(down, s3, s2),
        jnp.where(down, zero, s3),
    ]


def offset_weights(offset, frac, reach):
    stencil = cubic_weights(frac)
    spread = []
    for target in range(-reach, reach + 1):
        weight = jnp.zeros(frac.shape, jnp.float32)
        for step in range(4):
            weight = jnp.where(offset == target - step + 1, stencil[step], weight)
        spread.append(weight)
    return spread


def code_range(cells, count):
    low = math.log(0.98 * cells * ITEM_LOW)
    high = math.log(1.02 * cells * ITEM_HIGH * count)
    return low, 2.0 * CODES / (high - low)


def step_kernel(
    dims,
    winds_hbm, first_hbm, second_hbm, tracers_hbm, fluxes_hbm, weights_hbm, owner_ref, block_ref,
    moved_ref, arrived_ref, labels_ref, dense_ref,
    wind_pad, first_v, second_v, tracer_pad, fluxes_v, weights_v,
    products, outgoing, codes_v, codes_s, marks_v, relayed, running, dense_v, table_v, table_s,
    wind_pack, tracer_pack, wind_edge, tracer_edge,
    shifted, lhs, rhs_a, rhs_b, masks, wind_w, wind_sum, lev_w, row_w, col_w, col_at, moved_v,
    wind_sem, tracer_sem, first_sem, second_sem, load_sem, code_sem, moved_sem,
    halo_send, halo_recv, item_send, item_recv, mark_send, mark_recv,
    relay_send, relay_recv, dense_sem, table_sem,
):
    chans, levels, rows, comps, tiles, links, blocks, wide, narrow, direct = dims
    lanes = LANES
    taps, reach = 2 * wide + 1, 2 * narrow + 1
    lat, lon = lax.axis_index("lat"), lax.axis_index("lon")
    lat_count, lon_count = lax.axis_size("lat"), lax.axis_size("lon")
    devices = lat_count * lon_count
    me = lat * lon_count + lon

    def by_level(source, target, sem, start):
        return [
            pltpu.make_async_copy(
                source.at[:, level], target.at[:, pl.ds(start, rows), level, :], sem.at[level]
            )
            for level in range(levels)
        ]

    wind_loads = by_level(winds_hbm, wind_pad, wind_sem, wide)
    tracer_loads = [
        pltpu.make_async_copy(
            tracers_hbm.at[chan], tracer_pad.at[:, pl.ds(narrow, rows), chan, :], tracer_sem.at[chan]
        )
        for chan in range(chans)
    ]
    flux_load = pltpu.make_async_copy(fluxes_hbm, fluxes_v, load_sem.at[0])
    weight_load = pltpu.make_async_copy(weights_hbm, weights_v, load_sem.at[1])
    late_loads = by_level(first_hbm, first_v, first_sem, 0) + by_level(second_hbm, second_v, second_sem, 0)
    for load in wind_loads + tracer_loads + [flux_load, weight_load] + late_loads:
        load.start()

    barrier = pltpu.get_barrier_semaphore()

    def greet(k, carry):
        p = lax.rem(me + k, devices)
        pl.semaphore_signal(
            barrier, inc=1, device_id=(p // lon_count, lax.rem(p, lon_count)), device_id_type=MESH
        )
        return carry

    lax.fori_loop(1, devices, greet, 0)

    width = codes_v.shape[1]
    spot = lax.broadcasted_iota(jnp.int32, (1, width), 1)
    lowest = jnp.full((1, width), BIG, jnp.int32)
    highest = jnp.full((1, width), -1, jnp.int32)
    for t in range(tiles):
        for k in range(links):
            code = (t * links + k) * blocks + block_ref[k, t]
            hit = spot == owner_ref[k, t]
            lowest = jnp.minimum(lowest, jnp.where(hit, code, BIG))
            highest = jnp.maximum(highest, jnp.where(hit, code, -1))
    used = highest >= 0
    twice = highest != lowest
    low_code = jnp.where(used, lowest, 0)
    high_code = jnp.where(used, highest, 0)
    codes_v[...] = jnp.concatenate([low_code // blocks, high_code // blocks], axis=0)
    marks_v[...] = jnp.concatenate(
        [
            jnp.where(used, low_code % blocks, -1),
            jnp.where(jnp.logical_and(used, twice), high_code % blocks, -1),
        ],
        axis=0,
    )
    code_copy = pltpu.make_async_copy(codes_v, codes_s, code_sem)
    code_copy.start()

    lane8 = lax.broadcasted_iota(jnp.int32, (levels, lanes), 1)
    lane16 = lax.broadcasted_iota(jnp.int32, (chans, lanes), 1)
    west, east = lax.rem(lon + lon_count - 1, lon_count), lax.rem(lon + 1, lon_count)
    north, south = lat - 1, lat + 1
    has_north, has_south = lat > 0, lat < lat_count - 1
    halves = rows // 8

    for load in wind_loads:
        load.wait()
    for half in range(halves):
        for comp in range(comps):
            packed = jnp.zeros((levels, lanes), jnp.float32)
            for p in range(8):
                value = wind_pad[comp, wide + half * 8 + p]
                packed = jnp.where(
                    lane8 // 16 == p, pltpu.roll(value, (16 * p + 8) % lanes, 1), packed
                )
            wind_pack[half, comp] = packed
    for load in tracer_loads:
        load.wait()

    def pack_row(r, carry):
        for side in range(2):
            packed = jnp.zeros((chans, lanes), jnp.float32)
            for level in range(levels):
                value = tracer_pad[level, narrow + 2 * r + side]
                packed = jnp.where(
                    lane16 // 16 == level, pltpu.roll(value, (16 * level + 8) % lanes, 1), packed
                )
            tracer_pack[2 * r + side] = packed
        return carry

    lax.fori_loop(0, rows // 2, pack_row, 0)

    @pl.when(jnp.logical_not(has_north))
    def _():
        wind_pad[:, 0:wide] = jnp.zeros((comps, wide, levels, lanes), jnp.float32)
        wind_edge[:, 0] = jnp.zeros((2, comps, levels, lanes), jnp.float32)
        tracer_pad[:, 0:narrow] = jnp.zeros((levels, narrow, chans, lanes), jnp.float32)
        tracer_edge[:, 0:narrow] = jnp.zeros((2, narrow, chans, lanes), jnp.float32)

    @pl.when(jnp.logical_not(has_south))
    def _():
        wind_pad[:, wide + rows :] = jnp.zeros((comps, wide, levels, lanes), jnp.float32)
        wind_edge[:, halves + 1] = jnp.zeros((2, comps, levels, lanes), jnp.float32)
        tracer_pad[:, narrow + rows :] = jnp.zeros((levels, narrow, chans, lanes), jnp.float32)
        tracer_edge[:, narrow + rows :] = jnp.zeros((2, narrow, chans, lanes), jnp.float32)

    pl.semaphore_wait(barrier, devices - 1)

    def halo(n, source, target, where):
        return pltpu.make_async_remote_copy(
            src_ref=source, dst_ref=target, send_sem=halo_send.at[n], recv_sem=halo_recv.at[n],
            device_id=where, device_id_type=MESH,
        )

    wind_sides = [
        halo(0, wind_pack, wind_edge.at[0, pl.ds(1, halves)], (lat, east)),
        halo(1, wind_pack, wind_edge.at[1, pl.ds(1, halves)], (lat, west)),
    ]
    wind_north = [
        halo(2, wind_pad.at[:, pl.ds(wide, wide)], wind_pad.at[:, pl.ds(wide + rows, wide)], (north, lon)),
        halo(3, wind_pack.at[0], wind_edge.at[0, halves + 1], (north, east)),
        halo(4, wind_pack.at[0], wind_edge.at[1, halves + 1], (north, west)),
    ]
    wind_south = [
        halo(5, wind_pad.at[:, pl.ds(rows, wide)], wind_pad.at[:, pl.ds(0, wide)], (south, lon)),
        halo(6, wind_pack.at[halves - 1], wind_edge.at[0, 0], (south, east)),
        halo(7, wind_pack.at[halves - 1], wind_edge.at[1, 0], (south, west)),
    ]
    first_rows, last_rows = pl.ds(0, narrow), pl.ds(rows - narrow, narrow)
    above_rows, below_rows = pl.ds(0, narrow), pl.ds(narrow + rows, narrow)
    tracer_sides = [
        halo(8, tracer_pack, tracer_edge.at[0, pl.ds(narrow, rows)], (lat, east)),
        halo(9, tracer_pack, tracer_edge.at[1, pl.ds(narrow, rows)], (lat, west)),
    ]
    tracer_north = [
        halo(10, tracer_pad.at[:, pl.ds(narrow, narrow)], tracer_pad.at[:, below_rows], (north, lon)),
        halo(11, tracer_pack.at[first_rows], tracer_edge.at[0, below_rows], (north, east)),
        halo(12, tracer_pack.at[first_rows], tracer_edge.at[1, below_rows], (north, west)),
    ]
    tracer_south = [
        halo(13, tracer_pad.at[:, pl.ds(rows, narrow)], tracer_pad.at[:, above_rows], (south, lon)),
        halo(14, tracer_pack.at[last_rows], tracer_edge.at[0, above_rows], (south, east)),
        halo(15, tracer_pack.at[last_rows], tracer_edge.at[1, above_rows], (south, west)),
    ]

    def each(condition, copies, act):
        @pl.when(condition)
        def _():
            for copy in copies:
                act(copy)

    start, arrive, leave = (lambda c: c.start()), (lambda c: c.wait_recv()), (lambda c: c.wait_send())
    each(has_north, wind_north, start)
    each(has_south, wind_south, start)
    for copy in wind_sides:
        copy.start()
    each(has_north, tracer_north, start)
    each(has_south, tracer_south, start)
    for copy in tracer_sides:
        copy.start()

    code_copy.wait()
    flux_load.wait()
    weight_load.wait()
    group = 3 if tiles % 3 == 0 else 1

    def multiply(n, carry):
        for g in range(group):
            t = n * group + g
            right = jnp.concatenate([weights_v[t, k] for k in range(links)], axis=1)
            done = jnp.dot(fluxes_v[t], right, preferred_element_type=jnp.float32)
            for k in range(links):
                products[t * links + k] = done[:, k * lanes : (k + 1) * lanes].astype(jnp.bfloat16)
        return carry

    lax.fori_loop(0, tiles // group, multiply, 0)

    half_count = lat_count // 2
    near = half_count * lon_count
    base = lat // half_count * half_count
    near_first = base * lon_count
    far_first = lax.rem(base + half_count, lat_count) * lon_count
    mine = me - near_first
    tail = pl.ds(direct, products.shape[1] - direct)
    head = pl.ds(0, direct)

    def at_device(p):
        return (p // lon_count, lax.rem(p, lon_count))

    def near_copy(s):
        return pltpu.make_async_remote_copy(
            src_ref=outgoing.at[near_first + s], dst_ref=arrived_ref.at[me],
            send_sem=item_send.at[near_first + s], recv_sem=item_recv.at[me],
            device_id=at_device(near_first + s), device_id_type=MESH,
        )

    def far_copy(s):
        return pltpu.make_async_remote_copy(
            src_ref=outgoing.at[far_first + s, :, head], dst_ref=arrived_ref.at[me, :, head],
            send_sem=item_send.at[far_first + s], recv_sem=item_recv.at[me],
            device_id=at_device(far_first + s), device_id_type=MESH,
        )

    def relay_copy(s):
        return pltpu.make_async_remote_copy(
            src_ref=outgoing.at[far_first + s, :, tail], dst_ref=relayed.at[mine],
            send_sem=relay_send.at[s], recv_sem=relay_recv.at[mine],
            device_id=at_device(near_first + s), device_id_type=MESH,
        )

    def mark_copy(p):
        return pltpu.make_async_remote_copy(
            src_ref=marks_v, dst_ref=labels_ref.at[:, me, :],
            send_sem=mark_send.at[p], recv_sem=mark_recv.at[me],
            device_id=at_device(p), device_id_type=MESH,
        )

    def send_mark(k, carry):
        mark_copy(lax.rem(me + k, devices)).start()
        return carry

    lax.fori_loop(1, devices, send_mark, 0)

    def ring(away, n):
        return lax.rem(lat - base + away, half_count) * lon_count + lax.rem(lon + n, lon_count)

    def fill(first, away):
        def one(n, carry):
            p = first + ring(away, n)
            for c in range(CAP):
                outgoing[p, c] = products[codes_s[c, p]]
            return carry

        lax.fori_loop(0, lon_count, one, 0)

    def send(copy, away, begin):
        def one(n, carry):
            copy(ring(away, n)).start()
            return carry

        lax.fori_loop(begin, lon_count, one, 0)

    for away in list(range(1, half_count)) + [0]:
        fill(far_first, away)
        send(relay_copy, away, 0 if away else 1)
        send(far_copy, away, 0)
    for away in [0] + list(range(1, half_count)):
        fill(near_first, away)
        send(near_copy, away, 0 if away else 1)
    own_copies = [
        pltpu.make_async_copy(
            outgoing.at[far_first + mine, :, tail], relayed.at[mine], relay_recv.at[mine]
        ),
        pltpu.make_async_copy(outgoing.at[me], arrived_ref.at[me], item_recv.at[me]),
        pltpu.make_async_copy(marks_v, labels_ref.at[:, me, :], mark_recv.at[me]),
    ]
    for copy in own_copies:
        copy.start()

    def wait_near(begin, act):
        def one(k, carry):
            act(lax.rem(mine + k, near))
            return carry

        lax.fori_loop(begin, near, one, 0)

    def relay_from(s):
        return pltpu.make_async_remote_copy(
            src_ref=outgoing.at[far_first + s, :, tail], dst_ref=relayed.at[s],
            send_sem=relay_send.at[s], recv_sem=relay_recv.at[s],
            device_id=at_device(near_first + s), device_id_type=MESH,
        )

    def mark_from(p):
        return pltpu.make_async_remote_copy(
            src_ref=marks_v, dst_ref=labels_ref.at[:, p, :],
            send_sem=mark_send.at[p], recv_sem=mark_recv.at[p],
            device_id=at_device(p), device_id_type=MESH,
        )

    count = CAP * near
    table_copy = pltpu.make_async_copy(table_v, table_s, table_sem)
    twin = (far_first + mine) // lon_count
    dense_copy = pltpu.make_async_remote_copy(
        src_ref=dense_v, dst_ref=dense_ref, send_sem=dense_sem.at[0], recv_sem=dense_sem.at[1],
        device_id=(twin, lon), device_id_type=MESH,
    )

    def sort_relayed():
        wait_near(1, lambda s: mark_from(near_first + s).wait_recv())
        own_copies[2].wait()
        width = table_v.shape[1]
        sub = lax.broadcasted_iota(jnp.int32, (count, width), 0)
        lane = lax.broadcasted_iota(jnp.int32, (count, width), 1)
        spot = lax.broadcasted_iota(jnp.int32, (near, width), 1)
        column = jnp.concatenate(
            [
                jnp.sum(
                    jnp.where(
                        spot == far_first + mine,
                        labels_ref[c, pl.ds(pl.multiple_of(near_first, 8), near), :],
                        0,
                    ),
                    axis=1,
                    keepdims=True,
                )
                for c in range(CAP)
            ],
            axis=0,
        )
        label = jnp.broadcast_to(jnp.where(column < 0, blocks, column), (count, width))
        across = jnp.sum(jnp.where(sub == lane, label, 0), axis=0, keepdims=True)
        across = jnp.broadcast_to(across, (count, width))
        inside = lane < count
        before = jnp.logical_or(label < across, jnp.logical_and(label == across, sub < lane))
        rank = jnp.sum(jnp.where(before, 1, 0), axis=0, keepdims=True)
        pick = jnp.logical_and(jnp.broadcast_to(rank, (count, width)) == sub, inside)
        code = lax.rem(lane, near) * CAP + lane // near
        item = jnp.sum(jnp.where(pick, code, 0), axis=1, keepdims=True)
        ordered = jnp.sum(jnp.where(pick, across, 0), axis=1, keepdims=True)
        ordered = jnp.broadcast_to(ordered, (count, width))
        same = jnp.logical_and(ordered == pltpu.roll(ordered, 1, 0), sub > 0)
        upto = jnp.sum(jnp.where(jnp.logical_and(across <= sub, inside), 1, 0), axis=1, keepdims=True)
        equal = jnp.sum(jnp.where(jnp.logical_and(across == sub, inside), 1, 0), axis=1, keepdims=True)
        final = jnp.where(equal > 0, upto - 1, count)
        table_v[...] = jnp.where(lane == 0, item, jnp.where(lane == 1, jnp.where(same, 1, 0), final))
        table_copy.start()

    def sum_relayed():
        wait_near(1, lambda s: relay_from(s).wait_recv())
        own_copies[0].wait()
        table_copy.wait()
        size = products.shape[1] - direct

        def add(n, total):
            item = table_s[n, 0]
            kept = table_s[n, 1].astype(jnp.float32)
            total = total * kept + relayed[item // CAP, lax.rem(item, CAP)].astype(jnp.float32)
            running[n] = total
            return total

        lax.fori_loop(0, count, add, jnp.zeros((size, lanes), jnp.float32))
        running[count] = jnp.zeros((size, lanes), jnp.float32)
        low, scale = code_range(fluxes_v.shape[2], count)

        def encode(s, carry):
            value = running[table_s[s, 2]]
            code = jnp.round((jnp.log(value) - low) * scale) - CODES
            code = jnp.where(value > 0.0, jnp.clip(code, -CODES, CODES), -CODES - 1.0)
            dense_v[s] = code.astype(jnp.int32).astype(jnp.int16)
            return carry

        lax.fori_loop(0, blocks, encode, 0)

    deep, across16 = (
        lax.broadcasted_iota(jnp.int32, (16, lanes), 0),
        lax.broadcasted_iota(jnp.int32, (16, lanes), 1),
    )
    groups = lanes // 16
    for t in range(groups):
        reached = jnp.abs(16 * t + deep - across16) <= narrow
        masks[t] = jnp.where(reached, 1.0, 0.0).astype(jnp.bfloat16)
    outer = jnp.where(deep < 8, deep - 8, deep + (lanes - 8))
    masks[groups] = jnp.where(jnp.abs(outer - across16) <= narrow, 1.0, 0.0).astype(jnp.bfloat16)
    rhs_a[...] = jnp.zeros_like(rhs_a)
    rhs_b[...] = jnp.zeros_like(rhs_b)

    for load in late_loads:
        load.wait()
    for copy in wind_sides:
        copy.wait_recv()
    each(has_north, wind_south, arrive)
    each(has_south, wind_north, arrive)

    def shift_row(r, carry):
        turned = r + 8 - wide
        half, p = turned // 8, turned % 8
        back = lax.rem(2 * lanes - 8 - 16 * p, lanes)
        for comp in range(comps):
            merged = jnp.where(lane8 % 16 < 8, wind_edge[0, half, comp], wind_edge[1, half, comp])
            edge = pltpu.roll(merged, back, 1)
            main = wind_pad[comp, r]
            for e in range(taps):
                d = e - wide
                if d > 0:
                    piece = pltpu.roll(jnp.where(lane8 < d, edge, main), lanes - d, 1)
                elif d < 0:
                    piece = pltpu.roll(jnp.where(lane8 >= lanes + d, edge, main), -d, 1)
                else:
                    piece = main
                low, high = piece[:1], piece[levels - 1 :]
                shifted[e * 5 + 0, comp, r] = jnp.concatenate([low, low, piece[: levels - 2]], axis=0)
                shifted[e * 5 + 1, comp, r] = jnp.concatenate([low, piece[: levels - 1]], axis=0)
                shifted[e * 5 + 2, comp, r] = piece
                shifted[e * 5 + 3, comp, r] = jnp.concatenate([piece[1:], high], axis=0)
                shifted[e * 5 + 4, comp, r] = jnp.concatenate([piece[2:], high, high], axis=0)
        return carry

    lax.fori_loop(0, rows + 2 * wide, shift_row, 0)

    column = lax.broadcasted_iota(jnp.int32, (levels, lanes), 1)

    def wind_start(side, i):
        off = [first_v[comp, i] for comp in range(comps)]
        frac = [
            jnp.clip(-wind_pad[comp, wide + i] - off[comp].astype(jnp.float32), 0.0, 1.0)
            for comp in range(comps)
        ]
        weights = level_weights(off[0], frac[0])
        weights += offset_weights(off[1], frac[1], wide) + offset_weights(off[2], frac[2], wide)
        for n, weight in enumerate(weights):
            wind_w[side, n] = weight
        for comp in range(comps):
            wind_sum[side, comp] = jnp.zeros((levels, lanes), jnp.float32)

    def wind_unit(first, q):
        sides = [side for side in range(2) if 0 <= q - side < taps]
        cw = [[wind_w[side, 5 + taps + e] for e in range(taps)] for side in sides]
        rw = [wind_w[side, 5 + q - side] for side in sides]
        total = [[wind_sum[side, comp] for comp in range(comps)] for side in sides]
        for above in range(5):
            pair = [wind_w[side, above] * rw[n] for n, side in enumerate(sides)]
            for comp in range(comps):
                inner = [None] * len(sides)
                for e in range(taps):
                    value = shifted[e * 5 + above, comp, first + q]
                    for n in range(len(sides)):
                        term = cw[n][e] * value
                        inner[n] = term if e == 0 else inner[n] + term
                for n in range(len(sides)):
                    total[n][comp] = total[n][comp] + pair[n] * inner[n]
        for n, side in enumerate(sides):
            for comp in range(comps):
                wind_sum[side, comp] = total[n][comp]

    def wind_finish(side, i):
        off = [second_v[comp, i] for comp in range(comps)]
        frac = [
            jnp.clip(
                -(wind_pad[comp, wide + i] + wind_sum[side, comp]) * 0.5
                - off[comp].astype(jnp.float32),
                0.0,
                1.0,
            )
            for comp in range(comps)
        ]
        for n, weight in enumerate(level_weights(off[0], frac[0])):
            lev_w[n, i] = weight
        for n, weight in enumerate(offset_weights(off[1], frac[1], narrow)):
            row_w[n, i] = weight
        for n, weight in enumerate(cubic_weights(frac[2])):
            col_w[n, i] = weight
        col_at[i] = off[2] - 1 + column

    for side in range(2):
        wind_start(side, side)

    wind_unit(0, 0)
    for q in range(1, taps):
        wind_unit(0, q)
    wind_unit(0, taps)
    for side in range(2):
        wind_finish(side, side)

    for copy in tracer_sides:
        copy.wait_recv()
    each(has_north, tracer_south, arrive)
    each(has_south, tracer_north, arrive)

    def split_row(r, carry):
        merged = jnp.where(lane16 % 16 < 8, tracer_edge[0, r], tracer_edge[1, r])
        turned = [merged] + [pltpu.roll(merged, lanes - 16 * s, 1) for s in range(1, levels)]
        for level in range(levels):
            value = tracer_pad[level, r]
            top = value.astype(jnp.bfloat16)
            lhs[level, r, :, 0:lanes] = top
            lhs[level, r, :, lanes : 2 * lanes] = (value - top.astype(jnp.float32)).astype(jnp.bfloat16)
            edge = jnp.where(
                lane16 < 16,
                turned[level],
                jnp.where(lane16 < 32, turned[(level - 1) % levels], turned[(level - 2) % levels]),
            )
            edge_top = edge.astype(jnp.bfloat16).astype(jnp.float32)
            edge = jnp.where(lane16 < 32, edge_top, edge - edge_top)
            lhs[level, r, :, 2 * lanes : 3 * lanes] = edge.astype(jnp.bfloat16)
        return carry

    lax.fori_loop(0, rows + 2 * narrow, split_row, 0)

    deep8 = lax.broadcasted_iota(jnp.int32, (8, lanes), 0)

    def build(level, pair, rhs):
        for side in range(2):
            i = pair * 2 + side
            cols = slice(side * lanes, (side + 1) * lanes)
            at = col_at[i, pl.ds(level, 1), :]
            away = jnp.bitwise_and(deep8 - at, 7)
            value = jnp.zeros((8, lanes), jnp.float32)
            for n in range(4):
                value = jnp.where(away == n, col_w[n, i, pl.ds(level, 1), :], value)
            rest = value - value.astype(jnp.bfloat16).astype(jnp.float32)
            top16 = jnp.concatenate([value, value], axis=0).astype(jnp.bfloat16)
            rest16 = jnp.concatenate([rest, rest], axis=0).astype(jnp.bfloat16)
            for t in range(groups):
                top = top16 * masks[t]
                rhs[16 * t : 16 * t + 16, cols] = top
                rhs[2 * lanes + 16 * t : 2 * lanes + 16 * t + 16, cols] = top
                rhs[lanes + 16 * t : lanes + 16 * t + 16, cols] = rest16 * masks[t]
            top = top16 * masks[groups]
            rhs[3 * lanes : 3 * lanes + 16, cols] = top
            rhs[3 * lanes + 16 : 3 * lanes + 32, cols] = rest16 * masks[groups]
            rhs[3 * lanes + 32 : 3 * lanes + 48, cols] = top

    span = reach + 1

    def apply(level, pair, rhs):
        low, high = max(level - 2, 0), min(level + 2, levels - 1)
        count = high - low + 1
        part = lambda at: lhs[
            low : high + 1, pl.ds(pair * 2, span), :, at * lanes : (at + 1) * lanes
        ].reshape(count * span * chans, lanes)
        top, rest, edge = part(0), part(1), part(2)
        left = jnp.concatenate([top, top, rest, edge], axis=1)
        done = jnp.dot(left, rhs[...], preferred_element_type=jnp.float32)
        for side in range(2):
            i = pair * 2 + side
            cols = slice(side * lanes, (side + 1) * lanes)
            rw = [row_w[n, i, pl.ds(level, 1), :] for n in range(reach)]
            total = jnp.zeros((chans, lanes), jnp.float32)
            for m in range(count):
                lw = None
                for n in range(5):
                    if min(max(level - 2 + n, 0), levels - 1) == low + m:
                        weight = lev_w[n, i, pl.ds(level, 1), :]
                        lw = weight if lw is None else lw + weight
                inner = jnp.zeros((chans, lanes), jnp.float32)
                for n in range(reach):
                    first = (m * span + n + side) * chans
                    inner = inner + rw[n] * done[first : first + chans, cols]
                total = total + lw * inner
            moved_v[i, level] = total

    pairs = rows // 2
    shares = levels - 1
    cuts = [(n * (taps + 1) + shares // 2) // shares for n in range(shares + 1)]
    both = [rhs_a, rhs_b]
    build(0, 0, rhs_a)

    def moved_copy(pair):
        return pltpu.make_async_copy(
            moved_v.at[pl.ds(pair * 2, 2)], moved_ref.at[pl.ds(pair * 2, 2)], moved_sem.at[pair]
        )

    def pair_step(pair, carry):
        after = jnp.minimum(pair + 1, pairs - 1)
        def level_step(level):
            if level == 0:
                for side in range(2):
                    wind_start(side, after * 2 + side)
            if level < shares:
                for q in range(cuts[level], cuts[level + 1]):
                    wind_unit(after * 2, q)
            if level == shares - 1:
                for side in range(2):
                    wind_finish(side, after * 2 + side)
            if level < levels - 1:
                build(level + 1, pair, both[(level + 1) % 2])
            else:
                build(0, after, both[0])
            apply(level, pair, both[level % 2])

        pl.when(pair == 1)(sort_relayed)
        pl.when(pair == 2)(sum_relayed)
        pl.when(pair == 3)(dense_copy.start)
        for level in range(levels):
            pl.when(pair >= 0)(functools.partial(level_step, level))
        moved_copy(pair).start()
        return carry

    lax.fori_loop(0, pairs, pair_step, 0)
    for pair in range(pairs):
        moved_copy(pair).wait()

    for copy in wind_sides + tracer_sides:
        copy.wait_send()
    each(has_north, wind_north + tracer_north, leave)
    each(has_south, wind_south + tracer_south, leave)
    own_copies[1].wait()

    def near_done(s):
        near_copy(s).wait_send()
        relay_copy(s).wait_send()
        mark_copy(near_first + s).wait_send()
        pltpu.make_async_remote_copy(
            src_ref=outgoing.at[near_first + s], dst_ref=arrived_ref.at[near_first + s],
            send_sem=item_send.at[near_first + s], recv_sem=item_recv.at[near_first + s],
            device_id=at_device(near_first + s), device_id_type=MESH,
        ).wait_recv()

    def far_done(s):
        far_copy(s).wait_send()
        mark_copy(far_first + s).wait_send()
        mark_from(far_first + s).wait_recv()
        pltpu.make_async_remote_copy(
            src_ref=outgoing.at[far_first + s, :, head], dst_ref=arrived_ref.at[far_first + s, :, head],
            send_sem=item_send.at[far_first + s], recv_sem=item_recv.at[far_first + s],
            device_id=at_device(far_first + s), device_id_type=MESH,
        ).wait_recv()

    wait_near(1, near_done)
    wait_near(0, far_done)
    dense_copy.wait()


def join_kernel(
    dims, moved_hbm, arrived_hbm, labels_ref, dense_hbm, out_hbm,
    total, more, near_v, far_v, dense_v, moved_sem, near_sem, far_sem, dense_sem, out_sem,
):
    chans, levels, rows, blocks, direct, cells = dims
    lat_count, lon_count = lax.axis_size("lat"), lax.axis_size("lon")
    me = lax.axis_index("lat") * lon_count + lax.axis_index("lon")
    near = near_v.shape[0]
    near_first = me // near * near
    far_first = lax.rem(near_first + near, lat_count * lon_count)
    lanes = total.shape[3]
    loads = [
        pltpu.make_async_copy(
            moved_hbm.at[:, level], total.at[pl.ds(0, rows), :, level, :], moved_sem.at[level]
        )
        for level in range(levels)
    ]
    near_load = pltpu.make_async_copy(arrived_hbm.at[pl.ds(near_first, near)], near_v, near_sem)
    far_load = pltpu.make_async_copy(
        arrived_hbm.at[pl.ds(far_first, near), :, pl.ds(0, direct)], far_v, far_sem
    )
    dense_load = pltpu.make_async_copy(dense_hbm, dense_v, dense_sem)
    for load in loads + [dense_load, near_load, far_load]:
        load.start()
    more[...] = jnp.zeros_like(more)
    for load in loads:
        load.wait()
    dense_load.wait()
    low, scale = code_range(cells, CAP * near)
    cut = direct // levels

    def decode(s, carry):
        code = dense_v[s].astype(jnp.int32).astype(jnp.float32)
        value = jnp.exp((code + CODES) * (1.0 / scale) + low)
        value = jnp.where(code < -CODES, 0.0, value)
        more[s, cut:] = value.reshape(chans - cut, levels, lanes)
        return carry

    lax.fori_loop(0, blocks, decode, 0)

    def place(n, c):
        label = labels_ref[c, n, me]
        return jnp.where(label < 0, blocks, label)

    def add_near(n, carry):
        for c, sums in enumerate((total, more)):
            at = place(near_first + n, c)
            sums[at] = sums[at] + near_v[n, c].astype(jnp.float32).reshape(chans, levels, lanes)
        return carry

    def add_far(n, carry):
        for c, sums in enumerate((total, more)):
            at = place(far_first + n, c)
            sums[at, :cut] = sums[at, :cut] + far_v[n, c].astype(jnp.float32).reshape(cut, levels, lanes)
        return carry

    near_load.wait()
    lax.fori_loop(0, near, add_near, 0)
    far_load.wait()
    lax.fori_loop(0, near, add_far, 0)
    outs = [
        pltpu.make_async_copy(total.at[s], out_hbm.at[:, :, s, :], out_sem.at[s]) for s in range(rows)
    ]
    for s in range(rows):
        total[s] = total[s] + more[s]
        if s:
            outs[s - 1].start()
    outs[rows - 1].start()
    for out in outs:
        out.wait()


def body(
    tracers, winds, depart_first, depart_second, fluxes, remap_weights, target_device, target_block
):
    wide = HMAX + 1
    narrow = max((HMAX + 1) // 2 + 1, HMAX // 2 + 2)
    chans, levels, rows, lanes = tracers.shape
    comps = winds.shape[0]
    tiles, links = target_device.shape
    depth, cells = fluxes.shape[1:]
    cols = remap_weights.shape[3]
    blocks = rows * lanes // cols
    devices = lax.axis_size("lat") * lax.axis_size("lon")
    padded = -(-devices // LANES) * LANES
    halves = rows // 8
    direct = depth * DIRECT_PART // 128 // 16 * 16
    near = devices // 2
    dims = (chans, levels, rows, comps, tiles, links, blocks, wide, narrow, direct)
    hbm = pl.BlockSpec(memory_space=pl.ANY)
    vmem = pl.BlockSpec(memory_space=pltpu.VMEM)
    smem = pl.BlockSpec(memory_space=pltpu.SMEM)
    f32, b16, i32 = jnp.float32, jnp.bfloat16, jnp.int32
    dma = pltpu.SemaphoreType.DMA
    moved, arrived, labels, dense = pl.pallas_call(
        functools.partial(step_kernel, dims),
        out_shape=(
            jax.ShapeDtypeStruct((rows, levels, chans, lanes), f32),
            jax.ShapeDtypeStruct((devices, CAP, depth, cols), b16),
            jax.ShapeDtypeStruct((CAP, devices, padded), i32),
            jax.ShapeDtypeStruct((blocks, depth - direct, cols), jnp.int16),
        ),
        in_specs=[hbm] * 6 + [smem] * 2,
        out_specs=(hbm, hbm, vmem, hbm),
        scratch_shapes=[
            pltpu.VMEM((comps, rows + 2 * wide, levels, lanes), f32),
            pltpu.VMEM((comps, rows, levels, lanes), i32),
            pltpu.VMEM((comps, rows, levels, lanes), i32),
            pltpu.VMEM((levels, rows + 2 * narrow, chans, lanes), f32),
            pltpu.VMEM((tiles, depth, cells), b16),
            pltpu.VMEM((tiles, links, cells, cols), b16),
            pltpu.VMEM((tiles * links, depth, cols), b16),
            pltpu.VMEM((devices, CAP, depth, cols), b16),
            pltpu.VMEM((CAP, padded), i32),
            pltpu.SMEM((CAP, padded), i32),
            pltpu.VMEM((CAP, padded), i32),
            pltpu.VMEM((near, CAP, depth - direct, cols), b16),
            pltpu.VMEM((near * CAP + 1, depth - direct, cols), f32),
            pltpu.VMEM((blocks, depth - direct, cols), jnp.int16),
            pltpu.VMEM((near * CAP, padded), i32),
            pltpu.SMEM((near * CAP, padded), i32),
            pltpu.VMEM((halves, comps, levels, lanes), f32),
            pltpu.VMEM((rows, chans, lanes), f32),
            pltpu.VMEM((2, halves + 2, comps, levels, lanes), f32),
            pltpu.VMEM((2, rows + 2 * narrow, chans, lanes), f32),
            pltpu.VMEM((5 * (2 * wide + 1), comps, rows + 2 * wide, levels, lanes), f32),
            pltpu.VMEM((levels, rows + 2 * narrow, chans, 3 * lanes), b16),
            pltpu.VMEM((4 * lanes, 2 * lanes), b16),
            pltpu.VMEM((4 * lanes, 2 * lanes), b16),
            pltpu.VMEM((lanes // 16 + 1, 16, lanes), b16),
            pltpu.VMEM((2, 5 + 2 * (2 * wide + 1), levels, lanes), f32),
            pltpu.VMEM((2, comps, levels, lanes), f32),
            pltpu.VMEM((5, rows, levels, lanes), f32),
            pltpu.VMEM((2 * narrow + 1, rows, levels, lanes), f32),
            pltpu.VMEM((4, rows, levels, lanes), f32),
            pltpu.VMEM((rows, levels, lanes), i32),
            pltpu.VMEM((rows, levels, chans, lanes), f32),
            dma((levels,)),
            dma((chans,)),
            dma((levels,)),
            dma((levels,)),
            dma((2,)),
            dma(()),
            dma((rows // 2,)),
            dma((16,)),
            dma((16,)),
            dma((devices,)),
            dma((devices,)),
            dma((devices,)),
            dma((devices,)),
            dma((near,)),
            dma((near,)),
            dma((2,)),
            dma(()),
        ],
        compiler_params=pltpu.CompilerParams(
            collective_id=0, has_side_effects=True, vmem_limit_bytes=62 * 1024 * 1024
        ),
        name="step",
    )(winds, depart_first, depart_second, tracers, fluxes, remap_weights, target_device.T, target_block.T)
    return pl.pallas_call(
        functools.partial(join_kernel, (chans, levels, rows, blocks, direct, cells)),
        out_shape=jax.ShapeDtypeStruct((chans, levels, rows, lanes), f32),
        in_specs=[hbm, hbm, smem, hbm],
        out_specs=hbm,
        scratch_shapes=[
            pltpu.VMEM((blocks + 1, chans, levels, lanes), f32),
            pltpu.VMEM((blocks + 1, chans, levels, lanes), f32),
            pltpu.VMEM((near, CAP, depth, cols), b16),
            pltpu.VMEM((near, CAP, direct, cols), b16),
            pltpu.VMEM((blocks, depth - direct, cols), jnp.int16),
            dma((levels,)),
            dma(()),
            dma(()),
            dma(()),
            dma((rows,)),
        ],
        compiler_params=pltpu.CompilerParams(vmem_limit_bytes=62 * 1024 * 1024),
        name="join",
    )(moved, arrived, labels, dense)


def solution(mesh):
    in_specs = (
        P(None, None, "lat", "lon"),
        P(None, None, "lat", "lon"),
        P(None, None, "lat", "lon"),
        P(None, None, "lat", "lon"),
        P(("lat", "lon"), None, None),
        P(("lat", "lon"), None, None, None),
        P(("lat", "lon"), None),
        P(("lat", "lon"), None),
    )
    out_specs = P(None, None, "lat", "lon")
    return jax.shard_map(body, mesh=mesh, in_specs=in_specs, out_specs=out_specs, check_vma=False)
```

```python
import functools
import math

import jax
import jax.numpy as jnp
from jax import lax
from jax.experimental import pallas as pl
from jax.experimental.pallas import tpu as pltpu
from jax.sharding import PartitionSpec as P

CAP = 2
HMAX = 3
MESH = pl.DeviceIdType.MESH
LANES = 128
BIG = 1 << 20
DIRECT_PART = 48
CODES = 32767.0
ITEM_LOW = 0.049804688 * 0.00019931793
ITEM_HIGH = 5.0 * 0.019897461


def cubic_weights(frac):
    first = -frac * (frac - 1.0) * (frac - 2.0) / 6.0
    second = (frac + 1.0) * (frac - 1.0) * (frac - 2.0) / 2.0
    third = -(frac + 1.0) * frac * (frac - 2.0) / 2.0
    fourth = (frac + 1.0) * frac * (frac - 1.0) / 6.0
    return (first, second, third, fourth)


def level_weights(offset, frac):
    s0, s1, s2, s3 = cubic_weights(frac)
    down = offset < 0
    zero = jnp.zeros_like(frac)
    return [
        jnp.where(down, s0, zero),
        jnp.where(down, s1, s0),
        jnp.where(down, s2, s1),
        jnp.where(down, s3, s2),
        jnp.where(down, zero, s3),
    ]


def offset_weights(offset, frac, reach):
    stencil = cubic_weights(frac)
    spread = []
    for target in range(-reach, reach + 1):
        weight = jnp.zeros(frac.shape, jnp.float32)
        for step in range(4):
            weight = jnp.where(offset == target - step + 1, stencil[step], weight)
        spread.append(weight)
    return spread


def code_range(cells, count):
    low = math.log(0.98 * cells * ITEM_LOW)
    high = math.log(1.02 * cells * ITEM_HIGH * count)
    return low, 2.0 * CODES / (high - low)


def step_kernel(
    dims,
    winds_hbm, first_hbm, second_hbm, tracers_hbm, fluxes_hbm, weights_hbm, owner_hbm, block_hbm,
    moved_ref, arrived_ref, labels_out, dense_ref,
    owner_ref, block_ref, labels_ref,
    wind_pad, first_v, second_v, tracer_pad, fluxes_v, weights_v,
    products, outgoing, codes_v, codes_s, marks_v, relayed, running, dense_v, table_v, table_s,
    wind_pack, tracer_pack, wind_edge, tracer_edge,
    shifted, lhs, rhs_a, rhs_b, masks, wind_w, wind_sum, lev_w, row_w, col_w, col_at, moved_v,
    load_sem, code_sem, moved_sem, halo_send, halo_recv, near_sem, far_sem, mark_sem, relay_sem,
    dense_sem, table_sem, own_sem, labels_sem,
):
    chans, levels, rows, comps, tiles, links, blocks, wide, narrow, direct = dims
    lanes = LANES
    taps, reach = 2 * wide + 1, 2 * narrow + 1
    lat, lon = lax.axis_index("lat"), lax.axis_index("lon")
    lat_count, lon_count = lax.axis_size("lat"), lax.axis_size("lon")
    devices = lat_count * lon_count
    me = lat * lon_count + lon

    def by_level(source, target, n, start):
        return [
            pltpu.make_async_copy(
                source.at[:, level], target.at[:, pl.ds(start, rows), level, :], load_sem.at[n]
            )
            for level in range(levels)
        ]

    def whole(ref, sem):
        return pltpu.make_async_copy(ref, ref, sem)

    tables = [
        pltpu.make_async_copy(owner_hbm, owner_ref, load_sem.at[6]),
        pltpu.make_async_copy(block_hbm, block_ref, load_sem.at[7]),
    ]
    wind_loads = by_level(winds_hbm, wind_pad, 2, wide)
    tracer_loads = [
        pltpu.make_async_copy(
            tracers_hbm.at[chan], tracer_pad.at[:, pl.ds(narrow, rows), chan, :], load_sem.at[3]
        )
        for chan in range(chans)
    ]
    flux_load = pltpu.make_async_copy(fluxes_hbm, fluxes_v, load_sem.at[0])
    weight_load = pltpu.make_async_copy(weights_hbm, weights_v, load_sem.at[1])
    late_loads = by_level(first_hbm, first_v, 4, 0) + by_level(second_hbm, second_v, 5, 0)
    for load in wind_loads + tracer_loads + tables + [flux_load, weight_load] + late_loads:
        load.start()
    inner_winds = wind_pad.at[:, pl.ds(wide, rows)]
    inner_tracers = tracer_pad.at[:, pl.ds(narrow, rows)]

    barrier = pltpu.get_barrier_semaphore()

    for away in range(lat_count):
        there = lax.rem(lat + away, lat_count)

        def greet(n, carry, there=there):
            pl.semaphore_signal(
                barrier, inc=1, device_id=(there, lax.rem(lon + n, lon_count)), device_id_type=MESH
            )
            return carry

        lax.fori_loop(0 if away else 1, lon_count, greet, 0)

    lane8 = lax.broadcasted_iota(jnp.int32, (levels, lanes), 1)
    lane16 = lax.broadcasted_iota(jnp.int32, (chans, lanes), 1)
    west, east = lax.rem(lon + lon_count - 1, lon_count), lax.rem(lon + 1, lon_count)
    north, south = lat - 1, lat + 1
    has_north, has_south = lat > 0, lat < lat_count - 1
    halves = rows // 8

    def halo(n, source, target, where):
        return pltpu.make_async_remote_copy(
            src_ref=source, dst_ref=target, send_sem=halo_send.at[n], recv_sem=halo_recv.at[n],
            device_id=where, device_id_type=MESH,
        )

    wind_sides = [
        halo(0, wind_pack, wind_edge.at[0, pl.ds(1, halves)], (lat, east)),
        halo(1, wind_pack, wind_edge.at[1, pl.ds(1, halves)], (lat, west)),
    ]
    wind_north = [
        halo(2, wind_pad.at[:, pl.ds(wide, wide)], wind_pad.at[:, pl.ds(wide + rows, wide)], (north, lon)),
        halo(3, wind_pack.at[0], wind_edge.at[0, halves + 1], (north, east)),
        halo(4, wind_pack.at[0], wind_edge.at[1, halves + 1], (north, west)),
    ]
    wind_south = [
        halo(5, wind_pad.at[:, pl.ds(rows, wide)], wind_pad.at[:, pl.ds(0, wide)], (south, lon)),
        halo(6, wind_pack.at[halves - 1], wind_edge.at[0, 0], (south, east)),
        halo(7, wind_pack.at[halves - 1], wind_edge.at[1, 0], (south, west)),
    ]
    first_rows, last_rows = pl.ds(0, narrow), pl.ds(rows - narrow, narrow)
    above_rows, below_rows = pl.ds(0, narrow), pl.ds(narrow + rows, narrow)
    tracer_sides = [
        halo(8, tracer_pack, tracer_edge.at[0, pl.ds(narrow, rows)], (lat, east)),
        halo(9, tracer_pack, tracer_edge.at[1, pl.ds(narrow, rows)], (lat, west)),
    ]
    tracer_north = [
        halo(10, tracer_pad.at[:, pl.ds(narrow, narrow)], tracer_pad.at[:, below_rows], (north, lon)),
        halo(11, tracer_pack.at[first_rows], tracer_edge.at[0, below_rows], (north, east)),
        halo(12, tracer_pack.at[first_rows], tracer_edge.at[1, below_rows], (north, west)),
    ]
    tracer_south = [
        halo(13, tracer_pad.at[:, pl.ds(rows, narrow)], tracer_pad.at[:, above_rows], (south, lon)),
        halo(14, tracer_pack.at[last_rows], tracer_edge.at[0, above_rows], (south, east)),
        halo(15, tracer_pack.at[last_rows], tracer_edge.at[1, above_rows], (south, west)),
    ]

    def each(condition, copies, act):
        @pl.when(condition)
        def _():
            for copy in copies:
                act(copy)

    start, arrive, leave = (lambda c: c.start()), (lambda c: c.wait_recv()), (lambda c: c.wait_send())
    whole(inner_winds, load_sem.at[2]).wait()
    whole(inner_tracers, load_sem.at[3]).wait()
    pl.semaphore_wait(barrier, devices - 1)
    each(has_north, [wind_north[0], tracer_north[0]], start)
    each(has_south, [wind_south[0], tracer_south[0]], start)

    for half in range(halves):
        for comp in range(comps):
            packed = jnp.zeros((levels, lanes), jnp.float32)
            for p in range(8):
                value = wind_pad[comp, wide + half * 8 + p]
                packed = jnp.where(
                    lane8 // 16 == p, pltpu.roll(value, (16 * p + 8) % lanes, 1), packed
                )
            wind_pack[half, comp] = packed

    each(has_north, wind_north[1:], start)
    each(has_south, wind_south[1:], start)
    for copy in wind_sides:
        copy.start()

    def pack_row(r, carry):
        for side in range(2):
            packed = jnp.zeros((chans, lanes), jnp.float32)
            for level in range(levels):
                value = tracer_pad[level, narrow + 2 * r + side]
                packed = jnp.where(
                    lane16 // 16 == level, pltpu.roll(value, (16 * level + 8) % lanes, 1), packed
                )
            tracer_pack[2 * r + side] = packed
        return carry

    lax.fori_loop(0, rows // 2, pack_row, 0)

    each(has_north, tracer_north[1:], start)
    each(has_south, tracer_south[1:], start)
    for copy in tracer_sides:
        copy.start()
    for load in tables:
        load.wait()

    width = codes_v.shape[1]
    spot = lax.broadcasted_iota(jnp.int32, (1, width), 1)
    lowest = jnp.full((1, width), BIG, jnp.int32)
    highest = jnp.full((1, width), -1, jnp.int32)
    for t in range(tiles):
        for k in range(links):
            code = (t * links + k) * blocks + block_ref[k, t]
            hit = spot == owner_ref[k, t]
            lowest = jnp.minimum(lowest, jnp.where(hit, code, BIG))
            highest = jnp.maximum(highest, jnp.where(hit, code, -1))
    used = highest >= 0
    twice = highest != lowest
    low_code = jnp.where(used, lowest, 0)
    high_code = jnp.where(used, highest, 0)
    codes_v[...] = jnp.concatenate([low_code // blocks, high_code // blocks], axis=0)
    marks_v[...] = jnp.concatenate(
        [
            jnp.where(used, low_code % blocks, -1),
            jnp.where(jnp.logical_and(used, twice), high_code % blocks, -1),
        ],
        axis=0,
    )
    code_copy = pltpu.make_async_copy(codes_v, codes_s, code_sem)
    code_copy.start()

    @pl.when(jnp.logical_not(has_north))
    def _():
        wind_pad[:, 0:wide] = jnp.zeros((comps, wide, levels, lanes), jnp.float32)
        wind_edge[:, 0] = jnp.zeros((2, comps, levels, lanes), jnp.float32)
        tracer_pad[:, 0:narrow] = jnp.zeros((levels, narrow, chans, lanes), jnp.float32)
        tracer_edge[:, 0:narrow] = jnp.zeros((2, narrow, chans, lanes), jnp.float32)

    @pl.when(jnp.logical_not(has_south))
    def _():
        wind_pad[:, wide + rows :] = jnp.zeros((comps, wide, levels, lanes), jnp.float32)
        wind_edge[:, halves + 1] = jnp.zeros((2, comps, levels, lanes), jnp.float32)
        tracer_pad[:, narrow + rows :] = jnp.zeros((levels, narrow, chans, lanes), jnp.float32)
        tracer_edge[:, narrow + rows :] = jnp.zeros((2, narrow, chans, lanes), jnp.float32)

    code_copy.wait()
    flux_load.wait()
    weight_load.wait()
    group = 3 if tiles % 3 == 0 else 1

    def multiply(n, carry):
        for g in range(group):
            t = n * group + g
            right = jnp.concatenate([weights_v[t, k] for k in range(links)], axis=1)
            done = jnp.dot(fluxes_v[t], right, preferred_element_type=jnp.float32)
            for k in range(links):
                products[t * links + k] = done[:, k * lanes : (k + 1) * lanes].astype(jnp.bfloat16)
        return carry

    lax.fori_loop(0, tiles // group, multiply, 0)

    half_count = lat_count // 2
    near = half_count * lon_count
    base = lat // half_count * half_count
    near_first = base * lon_count
    far_first = lax.rem(base + half_count, lat_count) * lon_count
    mine = me - near_first
    tail = pl.ds(direct, products.shape[1] - direct)
    head = pl.ds(0, direct)

    def at_device(p):
        return (p // lon_count, lax.rem(p, lon_count))

    def near_copy(s):
        return pltpu.make_async_remote_copy(
            src_ref=outgoing.at[near_first + s], dst_ref=arrived_ref.at[me],
            send_sem=near_sem.at[0], recv_sem=near_sem.at[1],
            device_id=at_device(near_first + s), device_id_type=MESH,
        )

    def far_copy(s):
        return pltpu.make_async_remote_copy(
            src_ref=outgoing.at[far_first + s, :, head], dst_ref=arrived_ref.at[me, :, head],
            send_sem=far_sem.at[0], recv_sem=far_sem.at[1],
            device_id=at_device(far_first + s), device_id_type=MESH,
        )

    def relay_copy(s):
        return pltpu.make_async_remote_copy(
            src_ref=outgoing.at[far_first + s, :, tail], dst_ref=relayed.at[mine],
            send_sem=relay_sem.at[0], recv_sem=relay_sem.at[1],
            device_id=at_device(near_first + s), device_id_type=MESH,
        )

    def send_marks(first, recv, begin):
        def one(k, carry):
            s = lax.rem(mine + k, near)
            pltpu.make_async_remote_copy(
                src_ref=marks_v, dst_ref=labels_ref.at[:, me, :],
                send_sem=mark_sem.at[0], recv_sem=mark_sem.at[recv],
                device_id=at_device(first + s), device_id_type=MESH,
            ).start()
            return carry

        lax.fori_loop(begin, near, one, 0)

    send_marks(near_first, 1, 1)
    send_marks(far_first, 2, 0)

    def ring(away, n):
        return lax.rem(lat - base + away, half_count) * lon_count + lax.rem(lon + n, lon_count)

    def fill(first, away):
        def one(n, carry):
            p = first + ring(away, n)
            for c in range(CAP):
                outgoing[p, c] = products[codes_s[c, p]]
            return carry

        lax.fori_loop(0, lon_count, one, 0)

    def send(copy, away, begin):
        def one(n, carry):
            copy(ring(away, n)).start()
            return carry

        lax.fori_loop(begin, lon_count, one, 0)

    for away in list(range(1, half_count)) + [0]:
        fill(far_first, away)
        send(relay_copy, away, 0 if away else 1)
        send(far_copy, away, 0)
    for away in [0] + list(range(1, half_count)):
        fill(near_first, away)
        send(near_copy, away, 0 if away else 1)
    own_copies = [
        pltpu.make_async_copy(
            outgoing.at[far_first + mine, :, tail], relayed.at[mine], own_sem.at[0]
        ),
        pltpu.make_async_copy(outgoing.at[me], arrived_ref.at[me], own_sem.at[1]),
        pltpu.make_async_copy(marks_v, labels_ref.at[:, me, :], own_sem.at[2]),
    ]
    for copy in own_copies:
        copy.start()

    others = pl.ds(0, near - 1)
    labels_copy = pltpu.make_async_copy(labels_ref, labels_out, labels_sem)

    count = CAP * near
    table_copy = pltpu.make_async_copy(table_v, table_s, table_sem)
    twin = (far_first + mine) // lon_count
    dense_copy = pltpu.make_async_remote_copy(
        src_ref=dense_v, dst_ref=dense_ref, send_sem=dense_sem.at[0], recv_sem=dense_sem.at[1],
        device_id=(twin, lon), device_id_type=MESH,
    )

    def sort_relayed():
        whole(labels_ref.at[:, others], mark_sem.at[1]).wait()
        own_copies[2].wait()
        width = table_v.shape[1]
        sub = lax.broadcasted_iota(jnp.int32, (count, width), 0)
        lane = lax.broadcasted_iota(jnp.int32, (count, width), 1)
        spot = lax.broadcasted_iota(jnp.int32, (near, width), 1)
        column = jnp.concatenate(
            [
                jnp.sum(
                    jnp.where(
                        spot == far_first + mine,
                        labels_ref[c, pl.ds(pl.multiple_of(near_first, 8), near), :],
                        0,
                    ),
                    axis=1,
                    keepdims=True,
                )
                for c in range(CAP)
            ],
            axis=0,
        )
        label = jnp.broadcast_to(jnp.where(column < 0, blocks, column), (count, width))
        across = jnp.sum(jnp.where(sub == lane, label, 0), axis=0, keepdims=True)
        across = jnp.broadcast_to(across, (count, width))
        inside = lane < count
        before = jnp.logical_or(label < across, jnp.logical_and(label == across, sub < lane))
        rank = jnp.sum(jnp.where(before, 1, 0), axis=0, keepdims=True)
        pick = jnp.logical_and(jnp.broadcast_to(rank, (count, width)) == sub, inside)
        code = lax.rem(lane, near) * CAP + lane // near
        item = jnp.sum(jnp.where(pick, code, 0), axis=1, keepdims=True)
        ordered = jnp.sum(jnp.where(pick, across, 0), axis=1, keepdims=True)
        ordered = jnp.broadcast_to(ordered, (count, width))
        same = jnp.logical_and(ordered == pltpu.roll(ordered, 1, 0), sub > 0)
        upto = jnp.sum(jnp.where(jnp.logical_and(across <= sub, inside), 1, 0), axis=1, keepdims=True)
        equal = jnp.sum(jnp.where(jnp.logical_and(across == sub, inside), 1, 0), axis=1, keepdims=True)
        final = jnp.where(equal > 0, upto - 1, count)
        table_v[...] = jnp.where(lane == 0, item, jnp.where(lane == 1, jnp.where(same, 1, 0), final))
        table_copy.start()

    def take_labels():
        whole(labels_ref.at[:, pl.ds(0, near)], mark_sem.at[2]).wait()
        labels_copy.start()

    def sum_relayed():
        whole(relayed.at[others], relay_sem.at[1]).wait()
        own_copies[0].wait()
        table_copy.wait()
        size = products.shape[1] - direct

        def add(n, total):
            item = table_s[n, 0]
            kept = table_s[n, 1].astype(jnp.float32)
            total = total * kept + relayed[item // CAP, lax.rem(item, CAP)].astype(jnp.float32)
            running[n] = total
            return total

        lax.fori_loop(0, count, add, jnp.zeros((size, lanes), jnp.float32))
        running[count] = jnp.zeros((size, lanes), jnp.float32)
        low, scale = code_range(fluxes_v.shape[2], count)

        def encode(s, carry):
            value = running[table_s[s, 2]]
            code = jnp.round((jnp.log(value) - low) * scale) - CODES
            code = jnp.where(value > 0.0, jnp.clip(code, -CODES, CODES), -CODES - 1.0)
            dense_v[s] = code.astype(jnp.int32).astype(jnp.int16)
            return carry

        lax.fori_loop(0, blocks, encode, 0)

    deep, across16 = (
        lax.broadcasted_iota(jnp.int32, (16, lanes), 0),
        lax.broadcasted_iota(jnp.int32, (16, lanes), 1),
    )
    groups = lanes // 16
    for t in range(groups):
        reached = jnp.abs(16 * t + deep - across16) <= narrow
        masks[t] = jnp.where(reached, 1.0, 0.0).astype(jnp.bfloat16)
    outer = jnp.where(deep < 8, deep - 8, deep + (lanes - 8))
    masks[groups] = jnp.where(jnp.abs(outer - across16) <= narrow, 1.0, 0.0).astype(jnp.bfloat16)
    rhs_a[...] = jnp.zeros_like(rhs_a)
    rhs_b[...] = jnp.zeros_like(rhs_b)

    whole(first_v, load_sem.at[4]).wait()
    whole(second_v, load_sem.at[5]).wait()
    for copy in wind_sides:
        copy.wait_recv()
    each(has_north, wind_south, arrive)
    each(has_south, wind_north, arrive)

    def shift_row(r, carry):
        turned = r + 8 - wide
        half, p = turned // 8, turned % 8
        back = lax.rem(2 * lanes - 8 - 16 * p, lanes)
        for comp in range(comps):
            merged = jnp.where(lane8 % 16 < 8, wind_edge[0, half, comp], wind_edge[1, half, comp])
            edge = pltpu.roll(merged, back, 1)
            main = wind_pad[comp, r]
            for e in range(taps):
                d = e - wide
                if d > 0:
                    piece = pltpu.roll(jnp.where(lane8 < d, edge, main), lanes - d, 1)
                elif d < 0:
                    piece = pltpu.roll(jnp.where(lane8 >= lanes + d, edge, main), -d, 1)
                else:
                    piece = main
                low, high = piece[:1], piece[levels - 1 :]
                shifted[e * 5 + 0, comp, r] = jnp.concatenate([low, low, piece[: levels - 2]], axis=0)
                shifted[e * 5 + 1, comp, r] = jnp.concatenate([low, piece[: levels - 1]], axis=0)
                shifted[e * 5 + 2, comp, r] = piece
                shifted[e * 5 + 3, comp, r] = jnp.concatenate([piece[1:], high], axis=0)
                shifted[e * 5 + 4, comp, r] = jnp.concatenate([piece[2:], high, high], axis=0)
        return carry

    lax.fori_loop(0, rows + 2 * wide, shift_row, 0)

    column = lax.broadcasted_iota(jnp.int32, (levels, lanes), 1)

    def wind_start(side, i):
        off = [first_v[comp, i] for comp in range(comps)]
        frac = [
            jnp.clip(-wind_pad[comp, wide + i] - off[comp].astype(jnp.float32), 0.0, 1.0)
            for comp in range(comps)
        ]
        weights = level_weights(off[0], frac[0])
        weights += offset_weights(off[1], frac[1], wide) + offset_weights(off[2], frac[2], wide)
        for n, weight in enumerate(weights):
            wind_w[side, n] = weight
        for comp in range(comps):
            wind_sum[side, comp] = jnp.zeros((levels, lanes), jnp.float32)

    def wind_unit(first, q):
        sides = [side for side in range(2) if 0 <= q - side < taps]
        cw = [[wind_w[side, 5 + taps + e] for e in range(taps)] for side in sides]
        rw = [wind_w[side, 5 + q - side] for side in sides]
        total = [[wind_sum[side, comp] for comp in range(comps)] for side in sides]
        for above in range(5):
            pair = [wind_w[side, above] * rw[n] for n, side in enumerate(sides)]
            for comp in range(comps):
                inner = [None] * len(sides)
                for e in range(taps):
                    value = shifted[e * 5 + above, comp, first + q]
                    for n in range(len(sides)):
                        term = cw[n][e] * value
                        inner[n] = term if e == 0 else inner[n] + term
                for n in range(len(sides)):
                    total[n][comp] = total[n][comp] + pair[n] * inner[n]
        for n, side in enumerate(sides):
            for comp in range(comps):
                wind_sum[side, comp] = total[n][comp]

    def wind_finish(side, i):
        off = [second_v[comp, i] for comp in range(comps)]
        frac = [
            jnp.clip(
                -(wind_pad[comp, wide + i] + wind_sum[side, comp]) * 0.5
                - off[comp].astype(jnp.float32),
                0.0,
                1.0,
            )
            for comp in range(comps)
        ]
        for n, weight in enumerate(level_weights(off[0], frac[0])):
            lev_w[n, i] = weight
        for n, weight in enumerate(offset_weights(off[1], frac[1], narrow)):
            row_w[n, i] = weight
        for n, weight in enumerate(cubic_weights(frac[2])):
            col_w[n, i] = weight
        col_at[i] = off[2] - 1 + column

    for side in range(2):
        wind_start(side, side)

    wind_unit(0, 0)
    for q in range(1, taps):
        wind_unit(0, q)
    wind_unit(0, taps)
    for side in range(2):
        wind_finish(side, side)

    for copy in tracer_sides:
        copy.wait_recv()
    each(has_north, tracer_south, arrive)
    each(has_south, tracer_north, arrive)

    def split_row(r, carry):
        merged = jnp.where(lane16 % 16 < 8, tracer_edge[0, r], tracer_edge[1, r])
        turned = [merged] + [pltpu.roll(merged, lanes - 16 * s, 1) for s in range(1, levels)]
        for level in range(levels):
            value = tracer_pad[level, r]
            top = value.astype(jnp.bfloat16)
            lhs[level, r, :, 0:lanes] = top
            lhs[level, r, :, lanes : 2 * lanes] = (value - top.astype(jnp.float32)).astype(jnp.bfloat16)
            edge = jnp.where(
                lane16 < 16,
                turned[level],
                jnp.where(lane16 < 32, turned[(level - 1) % levels], turned[(level - 2) % levels]),
            )
            edge_top = edge.astype(jnp.bfloat16).astype(jnp.float32)
            edge = jnp.where(lane16 < 32, edge_top, edge - edge_top)
            lhs[level, r, :, 2 * lanes : 3 * lanes] = edge.astype(jnp.bfloat16)
        return carry

    lax.fori_loop(0, rows + 2 * narrow, split_row, 0)

    deep8 = lax.broadcasted_iota(jnp.int32, (8, lanes), 0)

    def build(level, pair, rhs):
        for side in range(2):
            i = pair * 2 + side
            cols = slice(side * lanes, (side + 1) * lanes)
            at = col_at[i, pl.ds(level, 1), :]
            away = jnp.bitwise_and(deep8 - at, 7)
            value = jnp.zeros((8, lanes), jnp.float32)
            for n in range(4):
                value = jnp.where(away == n, col_w[n, i, pl.ds(level, 1), :], value)
            rest = value - value.astype(jnp.bfloat16).astype(jnp.float32)
            top16 = jnp.concatenate([value, value], axis=0).astype(jnp.bfloat16)
            rest16 = jnp.concatenate([rest, rest], axis=0).astype(jnp.bfloat16)
            for t in range(groups):
                top = top16 * masks[t]
                rhs[16 * t : 16 * t + 16, cols] = top
                rhs[2 * lanes + 16 * t : 2 * lanes + 16 * t + 16, cols] = top
                rhs[lanes + 16 * t : lanes + 16 * t + 16, cols] = rest16 * masks[t]
            top = top16 * masks[groups]
            rhs[3 * lanes : 3 * lanes + 16, cols] = top
            rhs[3 * lanes + 16 : 3 * lanes + 32, cols] = rest16 * masks[groups]
            rhs[3 * lanes + 32 : 3 * lanes + 48, cols] = top

    span = reach + 1

    def apply(level, pair, rhs):
        low, high = max(level - 2, 0), min(level + 2, levels - 1)
        count = high - low + 1
        part = lambda at: lhs[
            low : high + 1, pl.ds(pair * 2, span), :, at * lanes : (at + 1) * lanes
        ].reshape(count * span * chans, lanes)
        top, rest, edge = part(0), part(1), part(2)
        left = jnp.concatenate([top, top, rest, edge], axis=1)
        done = jnp.dot(left, rhs[...], preferred_element_type=jnp.float32)
        for side in range(2):
            i = pair * 2 + side
            cols = slice(side * lanes, (side + 1) * lanes)
            rw = [row_w[n, i, pl.ds(level, 1), :] for n in range(reach)]
            total = jnp.zeros((chans, lanes), jnp.float32)
            for m in range(count):
                lw = None
                for n in range(5):
                    if min(max(level - 2 + n, 0), levels - 1) == low + m:
                        weight = lev_w[n, i, pl.ds(level, 1), :]
                        lw = weight if lw is None else lw + weight
                inner = jnp.zeros((chans, lanes), jnp.float32)
                for n in range(reach):
                    first = (m * span + n + side) * chans
                    inner = inner + rw[n] * done[first : first + chans, cols]
                total = total + lw * inner
            moved_v[i, level] = total

    pairs = rows // 2
    shares = levels - 1
    cuts = [(n * (taps + 1) + shares // 2) // shares for n in range(shares + 1)]
    both = [rhs_a, rhs_b]
    build(0, 0, rhs_a)

    def moved_copy(pair):
        return pltpu.make_async_copy(
            moved_v.at[pl.ds(pair * 2, 2)], moved_ref.at[pl.ds(pair * 2, 2)], moved_sem
        )

    def pair_step(pair, carry):
        after = jnp.minimum(pair + 1, pairs - 1)
        def level_step(level):
            if level == 0:
                for side in range(2):
                    wind_start(side, after * 2 + side)
            if level < shares:
                for q in range(cuts[level], cuts[level + 1]):
                    wind_unit(after * 2, q)
            if level == shares - 1:
                for side in range(2):
                    wind_finish(side, after * 2 + side)
            if level < levels - 1:
                build(level + 1, pair, both[(level + 1) % 2])
            else:
                build(0, after, both[0])
            apply(level, pair, both[level % 2])

        pl.when(pair == 1)(sort_relayed)
        pl.when(pair == 2)(sum_relayed)
        pl.when(pair == 3)(dense_copy.start)
        pl.when(pair == pairs - 1)(take_labels)
        for level in range(levels):
            pl.when(pair >= 0)(functools.partial(level_step, level))
        moved_copy(pair).start()
        return carry

    lax.fori_loop(0, pairs, pair_step, 0)
    whole(moved_v, moved_sem).wait()

    for copy in wind_sides + tracer_sides:
        copy.wait_send()
    each(has_north, wind_north + tracer_north, leave)
    each(has_south, wind_south + tracer_south, leave)
    own_copies[1].wait()

    whole(outgoing.at[others], near_sem.at[0]).wait()
    whole(outgoing.at[pl.ds(0, near), :, head], far_sem.at[0]).wait()
    whole(outgoing.at[others, :, tail], relay_sem.at[0]).wait()
    whole(labels_ref.at[:, pl.ds(0, devices - 1)], mark_sem.at[0]).wait()
    labels_copy.wait()
    whole(outgoing.at[pl.ds(0, near), :, head], far_sem.at[1]).wait()
    whole(outgoing.at[others], near_sem.at[1]).wait()
    dense_copy.wait()


def join_kernel(
    dims, moved_hbm, arrived_hbm, labels_hbm, dense_hbm, out_hbm,
    labels_ref, total, sums, more, near_v, far_v, dense_v, load_sem, out_sem,
):
    chans, levels, rows, blocks, direct, cells = dims
    lat_count, lon_count = lax.axis_size("lat"), lax.axis_size("lon")
    me = lax.axis_index("lat") * lon_count + lax.axis_index("lon")
    near = near_v.shape[0]
    near_first = me // near * near
    far_first = lax.rem(near_first + near, lat_count * lon_count)
    lanes = total.shape[3]
    label_load = pltpu.make_async_copy(labels_hbm, labels_ref, load_sem.at[0])
    near_load = pltpu.make_async_copy(arrived_hbm.at[pl.ds(near_first, near)], near_v, load_sem.at[1])
    far_load = pltpu.make_async_copy(
        arrived_hbm.at[pl.ds(far_first, near), :, pl.ds(0, direct)], far_v, load_sem.at[2]
    )
    dense_load = pltpu.make_async_copy(dense_hbm, dense_v, load_sem.at[3])
    loads = [
        pltpu.make_async_copy(moved_hbm.at[:, level], total.at[:, :, level, :], load_sem.at[4])
        for level in range(levels)
    ]
    for load in [label_load, dense_load, near_load, far_load] + loads:
        load.start()
    sums[...] = jnp.zeros_like(sums)
    more[...] = jnp.zeros_like(more)
    dense_load.wait()
    low, scale = code_range(cells, CAP * near)
    cut = direct // levels

    def decode(s, carry):
        code = dense_v[s].astype(jnp.int32).astype(jnp.float32)
        value = jnp.exp((code + CODES) * (1.0 / scale) + low)
        value = jnp.where(code < -CODES, 0.0, value)
        more[s, cut:] = value.reshape(chans - cut, levels, lanes)
        return carry

    lax.fori_loop(0, blocks, decode, 0)

    def place(n, c):
        label = labels_ref[c, n, me]
        return jnp.where(label < 0, blocks, label)

    def add_near(n, carry):
        for c, one in enumerate((sums, more)):
            at = place(near_first + n, c)
            one[at] = one[at] + near_v[n, c].astype(jnp.float32).reshape(chans, levels, lanes)
        return carry

    def add_far(n, carry):
        for c, one in enumerate((sums, more)):
            at = place(far_first + n, c)
            one[at, :cut] = one[at, :cut] + far_v[n, c].astype(jnp.float32).reshape(cut, levels, lanes)
        return carry

    label_load.wait()
    near_load.wait()
    lax.fori_loop(0, near, add_near, 0)
    far_load.wait()
    lax.fori_loop(0, near, add_far, 0)
    outs = [
        pltpu.make_async_copy(total.at[s], out_hbm.at[:, :, s, :], out_sem.at[s]) for s in range(rows)
    ]
    pltpu.make_async_copy(total, total, load_sem.at[4]).wait()
    for s in range(rows):
        total[s] = total[s] + (sums[s] + more[s])
        if s:
            outs[s - 1].start()
    outs[rows - 1].start()
    for out in outs:
        out.wait()


def body(
    tracers, winds, depart_first, depart_second, fluxes, remap_weights, target_device, target_block
):
    wide = HMAX + 1
    narrow = max((HMAX + 1) // 2 + 1, HMAX // 2 + 2)
    chans, levels, rows, lanes = tracers.shape
    comps = winds.shape[0]
    tiles, links = target_device.shape
    depth, cells = fluxes.shape[1:]
    cols = remap_weights.shape[3]
    blocks = rows * lanes // cols
    devices = lax.axis_size("lat") * lax.axis_size("lon")
    padded = -(-devices // LANES) * LANES
    halves = rows // 8
    direct = depth * DIRECT_PART // 128 // 16 * 16
    near = devices // 2
    dims = (chans, levels, rows, comps, tiles, links, blocks, wide, narrow, direct)
    hbm = pl.BlockSpec(memory_space=pl.ANY)
    f32, b16, i32 = jnp.float32, jnp.bfloat16, jnp.int32
    dma = pltpu.SemaphoreType.DMA
    moved, arrived, labels, dense = pl.pallas_call(
        functools.partial(step_kernel, dims),
        out_shape=(
            jax.ShapeDtypeStruct((rows, levels, chans, lanes), f32),
            jax.ShapeDtypeStruct((devices, CAP, depth, cols), b16),
            jax.ShapeDtypeStruct((CAP, devices, padded), i32),
            jax.ShapeDtypeStruct((blocks, depth - direct, cols), jnp.int16),
        ),
        in_specs=[hbm] * 8,
        out_specs=(hbm, hbm, hbm, hbm),
        scratch_shapes=[
            pltpu.SMEM((links, tiles), i32),
            pltpu.SMEM((links, tiles), i32),
            pltpu.VMEM((CAP, devices, padded), i32),
            pltpu.VMEM((comps, rows + 2 * wide, levels, lanes), f32),
            pltpu.VMEM((comps, rows, levels, lanes), i32),
            pltpu.VMEM((comps, rows, levels, lanes), i32),
            pltpu.VMEM((levels, rows + 2 * narrow, chans, lanes), f32),
            pltpu.VMEM((tiles, depth, cells), b16),
            pltpu.VMEM((tiles, links, cells, cols), b16),
            pltpu.VMEM((tiles * links, depth, cols), b16),
            pltpu.VMEM((devices, CAP, depth, cols), b16),
            pltpu.VMEM((CAP, padded), i32),
            pltpu.SMEM((CAP, padded), i32),
            pltpu.VMEM((CAP, padded), i32),
            pltpu.VMEM((near, CAP, depth - direct, cols), b16),
            pltpu.VMEM((near * CAP + 1, depth - direct, cols), f32),
            pltpu.VMEM((blocks, depth - direct, cols), jnp.int16),
            pltpu.VMEM((near * CAP, padded), i32),
            pltpu.SMEM((near * CAP, padded), i32),
            pltpu.VMEM((halves, comps, levels, lanes), f32),
            pltpu.VMEM((rows, chans, lanes), f32),
            pltpu.VMEM((2, halves + 2, comps, levels, lanes), f32),
            pltpu.VMEM((2, rows + 2 * narrow, chans, lanes), f32),
            pltpu.VMEM((5 * (2 * wide + 1), comps, rows + 2 * wide, levels, lanes), f32),
            pltpu.VMEM((levels, rows + 2 * narrow, chans, 3 * lanes), b16),
            pltpu.VMEM((4 * lanes, 2 * lanes), b16),
            pltpu.VMEM((4 * lanes, 2 * lanes), b16),
            pltpu.VMEM((lanes // 16 + 1, 16, lanes), b16),
            pltpu.VMEM((2, 5 + 2 * (2 * wide + 1), levels, lanes), f32),
            pltpu.VMEM((2, comps, levels, lanes), f32),
            pltpu.VMEM((5, rows, levels, lanes), f32),
            pltpu.VMEM((2 * narrow + 1, rows, levels, lanes), f32),
            pltpu.VMEM((4, rows, levels, lanes), f32),
            pltpu.VMEM((rows, levels, lanes), i32),
            pltpu.VMEM((rows, levels, chans, lanes), f32),
            dma((8,)),
            dma(()),
            dma(()),
            dma((16,)),
            dma((16,)),
            dma((2,)),
            dma((2,)),
            dma((3,)),
            dma((2,)),
            dma((2,)),
            dma(()),
            dma((3,)),
            dma(()),
        ],
        compiler_params=pltpu.CompilerParams(
            collective_id=0, has_side_effects=True, vmem_limit_bytes=62 * 1024 * 1024
        ),
        name="step",
    )(winds, depart_first, depart_second, tracers, fluxes, remap_weights, target_device.T, target_block.T)
    return pl.pallas_call(
        functools.partial(join_kernel, (chans, levels, rows, blocks, direct, cells)),
        out_shape=jax.ShapeDtypeStruct((chans, levels, rows, lanes), f32),
        in_specs=[hbm] * 4,
        out_specs=hbm,
        scratch_shapes=[
            pltpu.SMEM((CAP, devices, padded), i32),
            pltpu.VMEM((rows, chans, levels, lanes), f32),
            pltpu.VMEM((blocks + 1, chans, levels, lanes), f32),
            pltpu.VMEM((blocks + 1, chans, levels, lanes), f32),
            pltpu.VMEM((near, CAP, depth, cols), b16),
            pltpu.VMEM((near, CAP, direct, cols), b16),
            pltpu.VMEM((blocks, depth - direct, cols), jnp.int16),
            dma((5,)),
            dma((rows,)),
        ],
        compiler_params=pltpu.CompilerParams(vmem_limit_bytes=62 * 1024 * 1024),
        name="join",
    )(moved, arrived, labels, dense)


def solution(mesh):
    in_specs = (
        P(None, None, "lat", "lon"),
        P(None, None, "lat", "lon"),
        P(None, None, "lat", "lon"),
        P(None, None, "lat", "lon"),
        P(("lat", "lon"), None, None),
        P(("lat", "lon"), None, None, None),
        P(("lat", "lon"), None),
        P(("lat", "lon"), None),
    )
    out_specs = P(None, None, "lat", "lon")
    return jax.shard_map(body, mesh=mesh, in_specs=in_specs, out_specs=out_specs, check_vma=False)
```

```python
import functools
import math

import jax
import jax.numpy as jnp
from jax import lax
from jax.experimental import pallas as pl
from jax.experimental.pallas import tpu as pltpu
from jax.sharding import PartitionSpec as P

CAP = 2
HMAX = 3
MESH = pl.DeviceIdType.MESH
LANES = 128
BIG = 1 << 20
DIRECT_PART = 48
CODES = 32767.0
ITEM_LOW = 0.049804688 * 0.00019931793
ITEM_HIGH = 5.0 * 0.019897461
TRACER_LEAST = 6.0 * 2.0**-24
TRACER_LOW = math.log(TRACER_LEAST)
TRACER_SCALE = (CODES - 1.0) / (math.log(6.0) - TRACER_LOW)


def cubic_weights(frac):
    first = -frac * (frac - 1.0) * (frac - 2.0) / 6.0
    second = (frac + 1.0) * (frac - 1.0) * (frac - 2.0) / 2.0
    third = -(frac + 1.0) * frac * (frac - 2.0) / 2.0
    fourth = (frac + 1.0) * frac * (frac - 1.0) / 6.0
    return (first, second, third, fourth)


def level_weights(offset, frac):
    s0, s1, s2, s3 = cubic_weights(frac)
    down = offset < 0
    zero = jnp.zeros_like(frac)
    return [
        jnp.where(down, s0, zero),
        jnp.where(down, s1, s0),
        jnp.where(down, s2, s1),
        jnp.where(down, s3, s2),
        jnp.where(down, zero, s3),
    ]


def offset_weights(offset, frac, reach):
    stencil = cubic_weights(frac)
    spread = []
    for target in range(-reach, reach + 1):
        weight = jnp.zeros(frac.shape, jnp.float32)
        for step in range(4):
            weight = jnp.where(offset == target - step + 1, stencil[step], weight)
        spread.append(weight)
    return spread


def to_code(value):
    size = jnp.abs(value)
    code = jnp.clip(jnp.round((jnp.log(size) - TRACER_LOW) * TRACER_SCALE), 0.0, CODES - 1.0) + 1.0
    code = jnp.where(size < TRACER_LEAST, 0.0, code)
    return jnp.where(value < 0.0, -code, code).astype(jnp.int32).astype(jnp.int16)


def from_code(code):
    code = code.astype(jnp.int32).astype(jnp.float32)
    size = jnp.exp((jnp.abs(code) - 1.0) * (1.0 / TRACER_SCALE) + TRACER_LOW)
    size = jnp.where(code == 0.0, 0.0, size)
    return jnp.where(code < 0.0, -size, size)


def code_range(cells, count):
    low = math.log(0.98 * cells * ITEM_LOW)
    high = math.log(1.02 * cells * ITEM_HIGH * count)
    return low, 2.0 * CODES / (high - low)


def step_kernel(
    dims,
    winds_hbm, first_hbm, second_hbm, tracers_hbm, fluxes_hbm, weights_hbm, owner_hbm, block_hbm,
    moved_ref, arrived_ref, labels_out, dense_ref,
    owner_ref, block_ref, labels_ref,
    wind_pad, first_v, second_v, tracer_pad, fluxes_v, weights_v,
    products, outgoing, codes_v, codes_s, marks_v, relayed, running, dense_v, table_v, table_s,
    wind_pack, tracer_pack, wind_edge, tracer_edge, codes_out, codes_in,
    shifted, lhs, rhs_a, rhs_b, masks, wind_w, wind_sum, lev_w, row_w, col_w, col_at, moved_v,
    load_sem, code_sem, moved_sem, halo_send, halo_recv, near_sem, far_sem, mark_sem, relay_sem,
    dense_sem, table_sem, own_sem, labels_sem,
):
    chans, levels, rows, comps, tiles, links, blocks, wide, narrow, direct = dims
    lanes = LANES
    taps, reach = 2 * wide + 1, 2 * narrow + 1
    lat, lon = lax.axis_index("lat"), lax.axis_index("lon")
    lat_count, lon_count = lax.axis_size("lat"), lax.axis_size("lon")
    devices = lat_count * lon_count
    me = lat * lon_count + lon

    def by_level(source, target, n, start):
        return [
            pltpu.make_async_copy(
                source.at[:, level], target.at[:, pl.ds(start, rows), level, :], load_sem.at[n]
            )
            for level in range(levels)
        ]

    def whole(ref, sem):
        return pltpu.make_async_copy(ref, ref, sem)

    tables = [
        pltpu.make_async_copy(owner_hbm, owner_ref, load_sem.at[6]),
        pltpu.make_async_copy(block_hbm, block_ref, load_sem.at[7]),
    ]
    wind_loads = by_level(winds_hbm, wind_pad, 2, wide)
    tracer_loads = [
        pltpu.make_async_copy(
            tracers_hbm.at[chan], tracer_pad.at[:, pl.ds(narrow, rows), chan, :], load_sem.at[3]
        )
        for chan in range(chans)
    ]
    flux_load = pltpu.make_async_copy(fluxes_hbm, fluxes_v, load_sem.at[0])
    weight_load = pltpu.make_async_copy(weights_hbm, weights_v, load_sem.at[1])
    late_loads = by_level(first_hbm, first_v, 4, 0) + by_level(second_hbm, second_v, 5, 0)
    for load in wind_loads + tracer_loads + tables + [flux_load, weight_load] + late_loads:
        load.start()
    inner_winds = wind_pad.at[:, pl.ds(wide, rows)]
    inner_tracers = tracer_pad.at[:, pl.ds(narrow, rows)]

    barrier = pltpu.get_barrier_semaphore()

    for away in range(lat_count):
        there = lax.rem(lat + away, lat_count)

        def greet(n, carry, there=there):
            pl.semaphore_signal(
                barrier, inc=1, device_id=(there, lax.rem(lon + n, lon_count)), device_id_type=MESH
            )
            return carry

        lax.fori_loop(0 if away else 1, lon_count, greet, 0)

    lane8 = lax.broadcasted_iota(jnp.int32, (levels, lanes), 1)
    lane16 = lax.broadcasted_iota(jnp.int32, (chans, lanes), 1)
    west, east = lax.rem(lon + lon_count - 1, lon_count), lax.rem(lon + 1, lon_count)
    north, south = lat - 1, lat + 1
    has_north, has_south = lat > 0, lat < lat_count - 1
    halves = rows // 8

    def halo(n, source, target, where):
        return pltpu.make_async_remote_copy(
            src_ref=source, dst_ref=target, send_sem=halo_send.at[n], recv_sem=halo_recv.at[n],
            device_id=where, device_id_type=MESH,
        )

    wind_sides = [
        halo(0, wind_pack, wind_edge.at[0, pl.ds(1, halves)], (lat, east)),
        halo(1, wind_pack, wind_edge.at[1, pl.ds(1, halves)], (lat, west)),
    ]
    wind_north = [
        halo(2, wind_pad.at[:, pl.ds(wide, wide)], wind_pad.at[:, pl.ds(wide + rows, wide)], (north, lon)),
        halo(3, wind_pack.at[0], wind_edge.at[0, halves + 1], (north, east)),
        halo(4, wind_pack.at[0], wind_edge.at[1, halves + 1], (north, west)),
    ]
    wind_south = [
        halo(5, wind_pad.at[:, pl.ds(rows, wide)], wind_pad.at[:, pl.ds(0, wide)], (south, lon)),
        halo(6, wind_pack.at[halves - 1], wind_edge.at[0, 0], (south, east)),
        halo(7, wind_pack.at[halves - 1], wind_edge.at[1, 0], (south, west)),
    ]
    first_rows, last_rows = pl.ds(0, narrow), pl.ds(rows - narrow, narrow)
    above_rows, below_rows = pl.ds(0, narrow), pl.ds(narrow + rows, narrow)
    tracer_sides = [
        halo(8, tracer_pack, tracer_edge.at[0, pl.ds(narrow, rows)], (lat, east)),
        halo(9, tracer_pack, tracer_edge.at[1, pl.ds(narrow, rows)], (lat, west)),
    ]
    tracer_north = [
        halo(10, codes_out.at[0], codes_in.at[1], (north, lon)),
        halo(11, tracer_pack.at[first_rows], tracer_edge.at[0, below_rows], (north, east)),
        halo(12, tracer_pack.at[first_rows], tracer_edge.at[1, below_rows], (north, west)),
    ]
    tracer_south = [
        halo(13, codes_out.at[1], codes_in.at[0], (south, lon)),
        halo(14, tracer_pack.at[last_rows], tracer_edge.at[0, above_rows], (south, east)),
        halo(15, tracer_pack.at[last_rows], tracer_edge.at[1, above_rows], (south, west)),
    ]

    def each(condition, copies, act):
        @pl.when(condition)
        def _():
            for copy in copies:
                act(copy)

    start, arrive, leave = (lambda c: c.start()), (lambda c: c.wait_recv()), (lambda c: c.wait_send())
    whole(inner_winds, load_sem.at[2]).wait()
    pl.semaphore_wait(barrier, devices - 1)
    each(has_north, wind_north[:1], start)
    each(has_south, wind_south[:1], start)
    whole(inner_tracers, load_sem.at[3]).wait()

    def encode_rows(level, carry):
        for side, first in ((0, narrow), (1, rows)):
            for r in range(narrow):
                codes_out[side, level, r] = to_code(tracer_pad[level, first + r])
        return carry

    lax.fori_loop(0, levels, encode_rows, 0)
    each(has_north, tracer_north[:1], start)
    each(has_south, tracer_south[:1], start)

    for half in range(halves):
        for comp in range(comps):
            packed = jnp.zeros((levels, lanes), jnp.float32)
            for p in range(8):
                value = wind_pad[comp, wide + half * 8 + p]
                packed = jnp.where(
                    lane8 // 16 == p, pltpu.roll(value, (16 * p + 8) % lanes, 1), packed
                )
            wind_pack[half, comp] = packed

    each(has_north, wind_north[1:], start)
    each(has_south, wind_south[1:], start)
    for copy in wind_sides:
        copy.start()

    def pack_row(r, carry):
        for side in range(2):
            packed = jnp.zeros((chans, lanes), jnp.float32)
            for level in range(levels):
                value = tracer_pad[level, narrow + 2 * r + side]
                packed = jnp.where(
                    lane16 // 16 == level, pltpu.roll(value, (16 * level + 8) % lanes, 1), packed
                )
            tracer_pack[2 * r + side] = packed
        return carry

    lax.fori_loop(0, rows // 2, pack_row, 0)

    each(has_north, tracer_north[1:], start)
    each(has_south, tracer_south[1:], start)
    for copy in tracer_sides:
        copy.start()
    for load in tables:
        load.wait()

    width = codes_v.shape[1]
    spot = lax.broadcasted_iota(jnp.int32, (1, width), 1)
    lowest = jnp.full((1, width), BIG, jnp.int32)
    highest = jnp.full((1, width), -1, jnp.int32)
    for t in range(tiles):
        for k in range(links):
            code = (t * links + k) * blocks + block_ref[k, t]
            hit = spot == owner_ref[k, t]
            lowest = jnp.minimum(lowest, jnp.where(hit, code, BIG))
            highest = jnp.maximum(highest, jnp.where(hit, code, -1))
    used = highest >= 0
    twice = highest != lowest
    low_code = jnp.where(used, lowest, 0)
    high_code = jnp.where(used, highest, 0)
    codes_v[...] = jnp.concatenate([low_code // blocks, high_code // blocks], axis=0)
    marks_v[...] = jnp.concatenate(
        [
            jnp.where(used, low_code % blocks, -1),
            jnp.where(jnp.logical_and(used, twice), high_code % blocks, -1),
        ],
        axis=0,
    )
    code_copy = pltpu.make_async_copy(codes_v, codes_s, code_sem)
    code_copy.start()

    @pl.when(jnp.logical_not(has_north))
    def _():
        wind_pad[:, 0:wide] = jnp.zeros((comps, wide, levels, lanes), jnp.float32)
        wind_edge[:, 0] = jnp.zeros((2, comps, levels, lanes), jnp.float32)
        tracer_pad[:, 0:narrow] = jnp.zeros((levels, narrow, chans, lanes), jnp.float32)
        tracer_edge[:, 0:narrow] = jnp.zeros((2, narrow, chans, lanes), jnp.float32)

    @pl.when(jnp.logical_not(has_south))
    def _():
        wind_pad[:, wide + rows :] = jnp.zeros((comps, wide, levels, lanes), jnp.float32)
        wind_edge[:, halves + 1] = jnp.zeros((2, comps, levels, lanes), jnp.float32)
        tracer_pad[:, narrow + rows :] = jnp.zeros((levels, narrow, chans, lanes), jnp.float32)
        tracer_edge[:, narrow + rows :] = jnp.zeros((2, narrow, chans, lanes), jnp.float32)

    code_copy.wait()
    flux_load.wait()
    weight_load.wait()
    group = 3 if tiles % 3 == 0 else 1

    def multiply(n, carry):
        for g in range(group):
            t = n * group + g
            right = jnp.concatenate([weights_v[t, k] for k in range(links)], axis=1)
            done = jnp.dot(fluxes_v[t], right, preferred_element_type=jnp.float32)
            for k in range(links):
                products[t * links + k] = done[:, k * lanes : (k + 1) * lanes].astype(jnp.bfloat16)
        return carry

    lax.fori_loop(0, tiles // group, multiply, 0)

    half_count = lat_count // 2
    near = half_count * lon_count
    base = lat // half_count * half_count
    near_first = base * lon_count
    far_first = lax.rem(base + half_count, lat_count) * lon_count
    mine = me - near_first
    tail = pl.ds(direct, products.shape[1] - direct)
    head = pl.ds(0, direct)

    def at_device(p):
        return (p // lon_count, lax.rem(p, lon_count))

    def near_copy(s):
        return pltpu.make_async_remote_copy(
            src_ref=outgoing.at[near_first + s], dst_ref=arrived_ref.at[me],
            send_sem=near_sem.at[0], recv_sem=near_sem.at[1],
            device_id=at_device(near_first + s), device_id_type=MESH,
        )

    def far_copy(s):
        return pltpu.make_async_remote_copy(
            src_ref=outgoing.at[far_first + s, :, head], dst_ref=arrived_ref.at[me, :, head],
            send_sem=far_sem.at[0], recv_sem=far_sem.at[1],
            device_id=at_device(far_first + s), device_id_type=MESH,
        )

    def relay_copy(s):
        return pltpu.make_async_remote_copy(
            src_ref=outgoing.at[far_first + s, :, tail], dst_ref=relayed.at[mine],
            send_sem=relay_sem.at[0], recv_sem=relay_sem.at[1],
            device_id=at_device(near_first + s), device_id_type=MESH,
        )

    def send_marks(first, recv, begin):
        def one(k, carry):
            s = lax.rem(mine + k, near)
            pltpu.make_async_remote_copy(
                src_ref=marks_v, dst_ref=labels_ref.at[:, me, :],
                send_sem=mark_sem.at[0], recv_sem=mark_sem.at[recv],
                device_id=at_device(first + s), device_id_type=MESH,
            ).start()
            return carry

        lax.fori_loop(begin, near, one, 0)

    send_marks(near_first, 1, 1)
    send_marks(far_first, 2, 0)

    def ring(away, n):
        return lax.rem(lat - base + away, half_count) * lon_count + lax.rem(lon + n, lon_count)

    def fill(first, away):
        def one(n, carry):
            p = first + ring(away, n)
            for c in range(CAP):
                outgoing[p, c] = products[codes_s[c, p]]
            return carry

        lax.fori_loop(0, lon_count, one, 0)

    def send(copy, away, begin):
        def one(n, carry):
            copy(ring(away, n)).start()
            return carry

        lax.fori_loop(begin, lon_count, one, 0)

    for away in list(range(1, half_count)) + [0]:
        fill(far_first, away)
        send(relay_copy, away, 0 if away else 1)
        send(far_copy, away, 0)
    for away in [0] + list(range(1, half_count)):
        fill(near_first, away)
        send(near_copy, away, 0 if away else 1)
    own_copies = [
        pltpu.make_async_copy(
            outgoing.at[far_first + mine, :, tail], relayed.at[mine], own_sem.at[0]
        ),
        pltpu.make_async_copy(outgoing.at[me], arrived_ref.at[me], own_sem.at[1]),
        pltpu.make_async_copy(marks_v, labels_ref.at[:, me, :], own_sem.at[2]),
    ]
    for copy in own_copies:
        copy.start()

    others = pl.ds(0, near - 1)
    labels_copy = pltpu.make_async_copy(labels_ref, labels_out, labels_sem)

    count = CAP * near
    table_copy = pltpu.make_async_copy(table_v, table_s, table_sem)
    twin = (far_first + mine) // lon_count
    dense_copy = pltpu.make_async_remote_copy(
        src_ref=dense_v, dst_ref=dense_ref, send_sem=dense_sem.at[0], recv_sem=dense_sem.at[1],
        device_id=(twin, lon), device_id_type=MESH,
    )

    def sort_relayed():
        whole(labels_ref.at[:, others], mark_sem.at[1]).wait()
        own_copies[2].wait()
        width = table_v.shape[1]
        sub = lax.broadcasted_iota(jnp.int32, (count, width), 0)
        lane = lax.broadcasted_iota(jnp.int32, (count, width), 1)
        spot = lax.broadcasted_iota(jnp.int32, (near, width), 1)
        column = jnp.concatenate(
            [
                jnp.sum(
                    jnp.where(
                        spot == far_first + mine,
                        labels_ref[c, pl.ds(pl.multiple_of(near_first, 8), near), :],
                        0,
                    ),
                    axis=1,
                    keepdims=True,
                )
                for c in range(CAP)
            ],
            axis=0,
        )
        label = jnp.broadcast_to(jnp.where(column < 0, blocks, column), (count, width))
        across = jnp.sum(jnp.where(sub == lane, label, 0), axis=0, keepdims=True)
        across = jnp.broadcast_to(across, (count, width))
        inside = lane < count
        before = jnp.logical_or(label < across, jnp.logical_and(label == across, sub < lane))
        rank = jnp.sum(jnp.where(before, 1, 0), axis=0, keepdims=True)
        pick = jnp.logical_and(jnp.broadcast_to(rank, (count, width)) == sub, inside)
        code = lax.rem(lane, near) * CAP + lane // near
        item = jnp.sum(jnp.where(pick, code, 0), axis=1, keepdims=True)
        ordered = jnp.sum(jnp.where(pick, across, 0), axis=1, keepdims=True)
        ordered = jnp.broadcast_to(ordered, (count, width))
        same = jnp.logical_and(ordered == pltpu.roll(ordered, 1, 0), sub > 0)
        upto = jnp.sum(jnp.where(jnp.logical_and(across <= sub, inside), 1, 0), axis=1, keepdims=True)
        equal = jnp.sum(jnp.where(jnp.logical_and(across == sub, inside), 1, 0), axis=1, keepdims=True)
        final = jnp.where(equal > 0, upto - 1, count)
        table_v[...] = jnp.where(lane == 0, item, jnp.where(lane == 1, jnp.where(same, 1, 0), final))
        table_copy.start()

    def take_labels():
        whole(labels_ref.at[:, pl.ds(0, near)], mark_sem.at[2]).wait()
        labels_copy.start()

    def sum_relayed():
        whole(relayed.at[others], relay_sem.at[1]).wait()
        own_copies[0].wait()
        table_copy.wait()
        size = products.shape[1] - direct

        def add(n, total):
            item = table_s[n, 0]
            kept = table_s[n, 1].astype(jnp.float32)
            total = total * kept + relayed[item // CAP, lax.rem(item, CAP)].astype(jnp.float32)
            running[n] = total
            return total

        lax.fori_loop(0, count, add, jnp.zeros((size, lanes), jnp.float32))
        running[count] = jnp.zeros((size, lanes), jnp.float32)
        low, scale = code_range(fluxes_v.shape[2], count)

        def encode(s, carry):
            value = running[table_s[s, 2]]
            code = jnp.round((jnp.log(value) - low) * scale) - CODES
            code = jnp.where(value > 0.0, jnp.clip(code, -CODES, CODES), -CODES - 1.0)
            dense_v[s] = code.astype(jnp.int32).astype(jnp.int16)
            return carry

        lax.fori_loop(0, blocks, encode, 0)

    deep, across16 = (
        lax.broadcasted_iota(jnp.int32, (16, lanes), 0),
        lax.broadcasted_iota(jnp.int32, (16, lanes), 1),
    )
    groups = lanes // 16
    for t in range(groups):
        reached = jnp.abs(16 * t + deep - across16) <= narrow
        masks[t] = jnp.where(reached, 1.0, 0.0).astype(jnp.bfloat16)
    outer = jnp.where(deep < 8, deep - 8, deep + (lanes - 8))
    masks[groups] = jnp.where(jnp.abs(outer - across16) <= narrow, 1.0, 0.0).astype(jnp.bfloat16)
    rhs_a[...] = jnp.zeros_like(rhs_a)
    rhs_b[...] = jnp.zeros_like(rhs_b)

    whole(first_v, load_sem.at[4]).wait()
    whole(second_v, load_sem.at[5]).wait()
    for copy in wind_sides:
        copy.wait_recv()
    each(has_north, wind_south, arrive)
    each(has_south, wind_north, arrive)

    def shift_row(r, carry):
        turned = r + 8 - wide
        half, p = turned // 8, turned % 8
        back = lax.rem(2 * lanes - 8 - 16 * p, lanes)
        for comp in range(comps):
            merged = jnp.where(lane8 % 16 < 8, wind_edge[0, half, comp], wind_edge[1, half, comp])
            edge = pltpu.roll(merged, back, 1)
            main = wind_pad[comp, r]
            for e in range(taps):
                d = e - wide
                if d > 0:
                    piece = pltpu.roll(jnp.where(lane8 < d, edge, main), lanes - d, 1)
                elif d < 0:
                    piece = pltpu.roll(jnp.where(lane8 >= lanes + d, edge, main), -d, 1)
                else:
                    piece = main
                low, high = piece[:1], piece[levels - 1 :]
                shifted[e * 5 + 0, comp, r] = jnp.concatenate([low, low, piece[: levels - 2]], axis=0)
                shifted[e * 5 + 1, comp, r] = jnp.concatenate([low, piece[: levels - 1]], axis=0)
                shifted[e * 5 + 2, comp, r] = piece
                shifted[e * 5 + 3, comp, r] = jnp.concatenate([piece[1:], high], axis=0)
                shifted[e * 5 + 4, comp, r] = jnp.concatenate([piece[2:], high, high], axis=0)
        return carry

    lax.fori_loop(0, rows + 2 * wide, shift_row, 0)

    column = lax.broadcasted_iota(jnp.int32, (levels, lanes), 1)

    def wind_start(side, i):
        off = [first_v[comp, i] for comp in range(comps)]
        frac = [
            jnp.clip(-wind_pad[comp, wide + i] - off[comp].astype(jnp.float32), 0.0, 1.0)
            for comp in range(comps)
        ]
        weights = level_weights(off[0], frac[0])
        weights += offset_weights(off[1], frac[1], wide) + offset_weights(off[2], frac[2], wide)
        for n, weight in enumerate(weights):
            wind_w[side, n] = weight
        for comp in range(comps):
            wind_sum[side, comp] = jnp.zeros((levels, lanes), jnp.float32)

    def wind_unit(first, q):
        sides = [side for side in range(2) if 0 <= q - side < taps]
        cw = [[wind_w[side, 5 + taps + e] for e in range(taps)] for side in sides]
        rw = [wind_w[side, 5 + q - side] for side in sides]
        total = [[wind_sum[side, comp] for comp in range(comps)] for side in sides]
        for above in range(5):
            pair = [wind_w[side, above] * rw[n] for n, side in enumerate(sides)]
            for comp in range(comps):
                inner = [None] * len(sides)
                for e in range(taps):
                    value = shifted[e * 5 + above, comp, first + q]
                    for n in range(len(sides)):
                        term = cw[n][e] * value
                        inner[n] = term if e == 0 else inner[n] + term
                for n in range(len(sides)):
                    total[n][comp] = total[n][comp] + pair[n] * inner[n]
        for n, side in enumerate(sides):
            for comp in range(comps):
                wind_sum[side, comp] = total[n][comp]

    def wind_finish(side, i):
        off = [second_v[comp, i] for comp in range(comps)]
        frac = [
            jnp.clip(
                -(wind_pad[comp, wide + i] + wind_sum[side, comp]) * 0.5
                - off[comp].astype(jnp.float32),
                0.0,
                1.0,
            )
            for comp in range(comps)
        ]
        for n, weight in enumerate(level_weights(off[0], frac[0])):
            lev_w[n, i] = weight
        for n, weight in enumerate(offset_weights(off[1], frac[1], narrow)):
            row_w[n, i] = weight
        for n, weight in enumerate(cubic_weights(frac[2])):
            col_w[n, i] = weight
        col_at[i] = off[2] - 1 + column

    for side in range(2):
        wind_start(side, side)

    wind_unit(0, 0)
    for q in range(1, taps):
        wind_unit(0, q)
    wind_unit(0, taps)
    for side in range(2):
        wind_finish(side, side)

    for copy in tracer_sides:
        copy.wait_recv()
    each(has_north, tracer_south, arrive)
    each(has_south, tracer_north, arrive)

    def decode_rows(place, first):
        def decode_level(level, carry):
            for r in range(narrow):
                tracer_pad[level, first + r] = from_code(codes_in[place, level, r])
            return carry

        lax.fori_loop(0, levels, decode_level, 0)

    pl.when(has_north)(functools.partial(decode_rows, 0, 0))
    pl.when(has_south)(functools.partial(decode_rows, 1, narrow + rows))

    def split_row(r, carry):
        merged = jnp.where(lane16 % 16 < 8, tracer_edge[0, r], tracer_edge[1, r])
        turned = [merged] + [pltpu.roll(merged, lanes - 16 * s, 1) for s in range(1, levels)]
        for level in range(levels):
            value = tracer_pad[level, r]
            top = value.astype(jnp.bfloat16)
            lhs[level, r, :, 0:lanes] = top
            lhs[level, r, :, lanes : 2 * lanes] = (value - top.astype(jnp.float32)).astype(jnp.bfloat16)
            edge = jnp.where(
                lane16 < 16,
                turned[level],
                jnp.where(lane16 < 32, turned[(level - 1) % levels], turned[(level - 2) % levels]),
            )
            edge_top = edge.astype(jnp.bfloat16).astype(jnp.float32)
            edge = jnp.where(lane16 < 32, edge_top, edge - edge_top)
            lhs[level, r, :, 2 * lanes : 3 * lanes] = edge.astype(jnp.bfloat16)
        return carry

    lax.fori_loop(0, rows + 2 * narrow, split_row, 0)

    deep8 = lax.broadcasted_iota(jnp.int32, (8, lanes), 0)

    def build(level, pair, rhs):
        for side in range(2):
            i = pair * 2 + side
            cols = slice(side * lanes, (side + 1) * lanes)
            at = col_at[i, pl.ds(level, 1), :]
            away = jnp.bitwise_and(deep8 - at, 7)
            value = jnp.zeros((8, lanes), jnp.float32)
            for n in range(4):
                value = jnp.where(away == n, col_w[n, i, pl.ds(level, 1), :], value)
            rest = value - value.astype(jnp.bfloat16).astype(jnp.float32)
            top16 = jnp.concatenate([value, value], axis=0).astype(jnp.bfloat16)
            rest16 = jnp.concatenate([rest, rest], axis=0).astype(jnp.bfloat16)
            for t in range(groups):
                top = top16 * masks[t]
                rhs[16 * t : 16 * t + 16, cols] = top
                rhs[2 * lanes + 16 * t : 2 * lanes + 16 * t + 16, cols] = top
                rhs[lanes + 16 * t : lanes + 16 * t + 16, cols] = rest16 * masks[t]
            top = top16 * masks[groups]
            rhs[3 * lanes : 3 * lanes + 16, cols] = top
            rhs[3 * lanes + 16 : 3 * lanes + 32, cols] = rest16 * masks[groups]
            rhs[3 * lanes + 32 : 3 * lanes + 48, cols] = top

    span = reach + 1

    def apply(level, pair, rhs):
        low, high = max(level - 2, 0), min(level + 2, levels - 1)
        count = high - low + 1
        part = lambda at: lhs[
            low : high + 1, pl.ds(pair * 2, span), :, at * lanes : (at + 1) * lanes
        ].reshape(count * span * chans, lanes)
        top, rest, edge = part(0), part(1), part(2)
        left = jnp.concatenate([top, top, rest, edge], axis=1)
        done = jnp.dot(left, rhs[...], preferred_element_type=jnp.float32)
        for side in range(2):
            i = pair * 2 + side
            cols = slice(side * lanes, (side + 1) * lanes)
            rw = [row_w[n, i, pl.ds(level, 1), :] for n in range(reach)]
            total = jnp.zeros((chans, lanes), jnp.float32)
            for m in range(count):
                lw = None
                for n in range(5):
                    if min(max(level - 2 + n, 0), levels - 1) == low + m:
                        weight = lev_w[n, i, pl.ds(level, 1), :]
                        lw = weight if lw is None else lw + weight
                inner = jnp.zeros((chans, lanes), jnp.float32)
                for n in range(reach):
                    first = (m * span + n + side) * chans
                    inner = inner + rw[n] * done[first : first + chans, cols]
                total = total + lw * inner
            moved_v[i, level] = total

    pairs = rows // 2
    shares = levels - 1
    cuts = [(n * (taps + 1) + shares // 2) // shares for n in range(shares + 1)]
    both = [rhs_a, rhs_b]
    build(0, 0, rhs_a)

    def moved_copy(pair):
        return pltpu.make_async_copy(
            moved_v.at[pl.ds(pair * 2, 2)], moved_ref.at[pl.ds(pair * 2, 2)], moved_sem
        )

    def pair_step(pair, carry):
        after = jnp.minimum(pair + 1, pairs - 1)
        def level_step(level):
            if level == 0:
                for side in range(2):
                    wind_start(side, after * 2 + side)
            if level < shares:
                for q in range(cuts[level], cuts[level + 1]):
                    wind_unit(after * 2, q)
            if level == shares - 1:
                for side in range(2):
                    wind_finish(side, after * 2 + side)
            if level < levels - 1:
                build(level + 1, pair, both[(level + 1) % 2])
            else:
                build(0, after, both[0])
            apply(level, pair, both[level % 2])

        pl.when(pair == 1)(sort_relayed)
        pl.when(pair == 2)(sum_relayed)
        pl.when(pair == 3)(dense_copy.start)
        pl.when(pair == pairs - 1)(take_labels)
        for level in range(levels):
            pl.when(pair >= 0)(functools.partial(level_step, level))
        moved_copy(pair).start()
        return carry

    lax.fori_loop(0, pairs, pair_step, 0)
    whole(moved_v, moved_sem).wait()

    for copy in wind_sides + tracer_sides:
        copy.wait_send()
    each(has_north, wind_north + tracer_north, leave)
    each(has_south, wind_south + tracer_south, leave)
    own_copies[1].wait()

    whole(outgoing.at[others], near_sem.at[0]).wait()
    whole(outgoing.at[pl.ds(0, near), :, head], far_sem.at[0]).wait()
    whole(outgoing.at[others, :, tail], relay_sem.at[0]).wait()
    whole(labels_ref.at[:, pl.ds(0, devices - 1)], mark_sem.at[0]).wait()
    labels_copy.wait()
    whole(outgoing.at[pl.ds(0, near), :, head], far_sem.at[1]).wait()
    whole(outgoing.at[others], near_sem.at[1]).wait()
    dense_copy.wait()


def join_kernel(
    dims, moved_hbm, arrived_hbm, labels_hbm, dense_hbm, out_hbm,
    labels_ref, total, sums, more, near_v, far_v, dense_v, load_sem, out_sem,
):
    chans, levels, rows, blocks, direct, cells = dims
    lat_count, lon_count = lax.axis_size("lat"), lax.axis_size("lon")
    me = lax.axis_index("lat") * lon_count + lax.axis_index("lon")
    near = near_v.shape[0]
    near_first = me // near * near
    far_first = lax.rem(near_first + near, lat_count * lon_count)
    lanes = total.shape[3]
    label_load = pltpu.make_async_copy(labels_hbm, labels_ref, load_sem.at[0])
    near_load = pltpu.make_async_copy(arrived_hbm.at[pl.ds(near_first, near)], near_v, load_sem.at[1])
    far_load = pltpu.make_async_copy(
        arrived_hbm.at[pl.ds(far_first, near), :, pl.ds(0, direct)], far_v, load_sem.at[2]
    )
    dense_load = pltpu.make_async_copy(dense_hbm, dense_v, load_sem.at[3])
    loads = [
        pltpu.make_async_copy(moved_hbm.at[:, level], total.at[:, :, level, :], load_sem.at[4])
        for level in range(levels)
    ]
    for load in [label_load, dense_load, near_load, far_load] + loads:
        load.start()
    sums[...] = jnp.zeros_like(sums)
    more[...] = jnp.zeros_like(more)
    dense_load.wait()
    low, scale = code_range(cells, CAP * near)
    cut = direct // levels

    def decode(s, carry):
        code = dense_v[s].astype(jnp.int32).astype(jnp.float32)
        value = jnp.exp((code + CODES) * (1.0 / scale) + low)
        value = jnp.where(code < -CODES, 0.0, value)
        more[s, cut:] = value.reshape(chans - cut, levels, lanes)
        return carry

    lax.fori_loop(0, blocks, decode, 0)

    def place(n, c):
        label = labels_ref[c, n, me]
        return jnp.where(label < 0, blocks, label)

    def add_near(n, carry):
        for c, one in enumerate((sums, more)):
            at = place(near_first + n, c)
            one[at] = one[at] + near_v[n, c].astype(jnp.float32).reshape(chans, levels, lanes)
        return carry

    def add_far(n, carry):
        for c, one in enumerate((sums, more)):
            at = place(far_first + n, c)
            one[at, :cut] = one[at, :cut] + far_v[n, c].astype(jnp.float32).reshape(cut, levels, lanes)
        return carry

    label_load.wait()
    near_load.wait()
    lax.fori_loop(0, near, add_near, 0)
    far_load.wait()
    lax.fori_loop(0, near, add_far, 0)
    outs = [
        pltpu.make_async_copy(total.at[s], out_hbm.at[:, :, s, :], out_sem.at[s]) for s in range(rows)
    ]
    pltpu.make_async_copy(total, total, load_sem.at[4]).wait()
    for s in range(rows):
        total[s] = total[s] + (sums[s] + more[s])
        if s:
            outs[s - 1].start()
    outs[rows - 1].start()
    for out in outs:
        out.wait()


def body(
    tracers, winds, depart_first, depart_second, fluxes, remap_weights, target_device, target_block
):
    wide = HMAX + 1
    narrow = max((HMAX + 1) // 2 + 1, HMAX // 2 + 2)
    chans, levels, rows, lanes = tracers.shape
    comps = winds.shape[0]
    tiles, links = target_device.shape
    depth, cells = fluxes.shape[1:]
    cols = remap_weights.shape[3]
    blocks = rows * lanes // cols
    devices = lax.axis_size("lat") * lax.axis_size("lon")
    padded = -(-devices // LANES) * LANES
    halves = rows // 8
    direct = depth * DIRECT_PART // 128 // 16 * 16
    near = devices // 2
    dims = (chans, levels, rows, comps, tiles, links, blocks, wide, narrow, direct)
    hbm = pl.BlockSpec(memory_space=pl.ANY)
    f32, b16, i32 = jnp.float32, jnp.bfloat16, jnp.int32
    dma = pltpu.SemaphoreType.DMA
    moved, arrived, labels, dense = pl.pallas_call(
        functools.partial(step_kernel, dims),
        out_shape=(
            jax.ShapeDtypeStruct((rows, levels, chans, lanes), f32),
            jax.ShapeDtypeStruct((devices, CAP, depth, cols), b16),
            jax.ShapeDtypeStruct((CAP, devices, padded), i32),
            jax.ShapeDtypeStruct((blocks, depth - direct, cols), jnp.int16),
        ),
        in_specs=[hbm] * 8,
        out_specs=(hbm, hbm, hbm, hbm),
        scratch_shapes=[
            pltpu.SMEM((links, tiles), i32),
            pltpu.SMEM((links, tiles), i32),
            pltpu.VMEM((CAP, devices, padded), i32),
            pltpu.VMEM((comps, rows + 2 * wide, levels, lanes), f32),
            pltpu.VMEM((comps, rows, levels, lanes), i32),
            pltpu.VMEM((comps, rows, levels, lanes), i32),
            pltpu.VMEM((levels, rows + 2 * narrow, chans, lanes), f32),
            pltpu.VMEM((tiles, depth, cells), b16),
            pltpu.VMEM((tiles, links, cells, cols), b16),
            pltpu.VMEM((tiles * links, depth, cols), b16),
            pltpu.VMEM((devices, CAP, depth, cols), b16),
            pltpu.VMEM((CAP, padded), i32),
            pltpu.SMEM((CAP, padded), i32),
            pltpu.VMEM((CAP, padded), i32),
            pltpu.VMEM((near, CAP, depth - direct, cols), b16),
            pltpu.VMEM((near * CAP + 1, depth - direct, cols), f32),
            pltpu.VMEM((blocks, depth - direct, cols), jnp.int16),
            pltpu.VMEM((near * CAP, padded), i32),
            pltpu.SMEM((near * CAP, padded), i32),
            pltpu.VMEM((halves, comps, levels, lanes), f32),
            pltpu.VMEM((rows, chans, lanes), f32),
            pltpu.VMEM((2, halves + 2, comps, levels, lanes), f32),
            pltpu.VMEM((2, rows + 2 * narrow, chans, lanes), f32),
            pltpu.VMEM((2, levels, narrow, chans, lanes), jnp.int16),
            pltpu.VMEM((2, levels, narrow, chans, lanes), jnp.int16),
            pltpu.VMEM((5 * (2 * wide + 1), comps, rows + 2 * wide, levels, lanes), f32),
            pltpu.VMEM((levels, rows + 2 * narrow, chans, 3 * lanes), b16),
            pltpu.VMEM((4 * lanes, 2 * lanes), b16),
            pltpu.VMEM((4 * lanes, 2 * lanes), b16),
            pltpu.VMEM((lanes // 16 + 1, 16, lanes), b16),
            pltpu.VMEM((2, 5 + 2 * (2 * wide + 1), levels, lanes), f32),
            pltpu.VMEM((2, comps, levels, lanes), f32),
            pltpu.VMEM((5, rows, levels, lanes), f32),
            pltpu.VMEM((2 * narrow + 1, rows, levels, lanes), f32),
            pltpu.VMEM((4, rows, levels, lanes), f32),
            pltpu.VMEM((rows, levels, lanes), i32),
            pltpu.VMEM((rows, levels, chans, lanes), f32),
            dma((8,)),
            dma(()),
            dma(()),
            dma((16,)),
            dma((16,)),
            dma((2,)),
            dma((2,)),
            dma((3,)),
            dma((2,)),
            dma((2,)),
            dma(()),
            dma((3,)),
            dma(()),
        ],
        compiler_params=pltpu.CompilerParams(
            collective_id=0, has_side_effects=True, vmem_limit_bytes=62 * 1024 * 1024
        ),
        name="step",
    )(winds, depart_first, depart_second, tracers, fluxes, remap_weights, target_device.T, target_block.T)
    return pl.pallas_call(
        functools.partial(join_kernel, (chans, levels, rows, blocks, direct, cells)),
        out_shape=jax.ShapeDtypeStruct((chans, levels, rows, lanes), f32),
        in_specs=[hbm] * 4,
        out_specs=hbm,
        scratch_shapes=[
            pltpu.SMEM((CAP, devices, padded), i32),
            pltpu.VMEM((rows, chans, levels, lanes), f32),
            pltpu.VMEM((blocks + 1, chans, levels, lanes), f32),
            pltpu.VMEM((blocks + 1, chans, levels, lanes), f32),
            pltpu.VMEM((near, CAP, depth, cols), b16),
            pltpu.VMEM((near, CAP, direct, cols), b16),
            pltpu.VMEM((blocks, depth - direct, cols), jnp.int16),
            dma((5,)),
            dma((rows,)),
        ],
        compiler_params=pltpu.CompilerParams(vmem_limit_bytes=62 * 1024 * 1024),
        name="join",
    )(moved, arrived, labels, dense)


def solution(mesh):
    in_specs = (
        P(None, None, "lat", "lon"),
        P(None, None, "lat", "lon"),
        P(None, None, "lat", "lon"),
        P(None, None, "lat", "lon"),
        P(("lat", "lon"), None, None),
        P(("lat", "lon"), None, None, None),
        P(("lat", "lon"), None),
        P(("lat", "lon"), None),
    )
    out_specs = P(None, None, "lat", "lon")
    return jax.shard_map(body, mesh=mesh, in_specs=in_specs, out_specs=out_specs, check_vma=False)
```

```python
import functools
import math

import jax
import jax.numpy as jnp
from jax import lax
from jax.experimental import pallas as pl
from jax.experimental.pallas import tpu as pltpu
from jax.sharding import PartitionSpec as P

CAP = 2
HMAX = 3
MESH = pl.DeviceIdType.MESH
LANES = 128
BIG = 1 << 20
DIRECT_PART = 48
CODES = 32767.0
ITEM_LOW = 0.049804688 * 0.00019931793
ITEM_HIGH = 5.0 * 0.019897461
WIND_MOST = 4.0
TRACER_LEAST = 6.0 * 2.0**-24
TRACER_LOW = math.log(TRACER_LEAST)
TRACER_SCALE = (CODES - 1.0) / (math.log(6.0) - TRACER_LOW)


def cubic_weights(frac):
    first = -frac * (frac - 1.0) * (frac - 2.0) / 6.0
    second = (frac + 1.0) * (frac - 1.0) * (frac - 2.0) / 2.0
    third = -(frac + 1.0) * frac * (frac - 2.0) / 2.0
    fourth = (frac + 1.0) * frac * (frac - 1.0) / 6.0
    return (first, second, third, fourth)


def level_weights(offset, frac):
    s0, s1, s2, s3 = cubic_weights(frac)
    down = offset < 0
    zero = jnp.zeros_like(frac)
    return [
        jnp.where(down, s0, zero),
        jnp.where(down, s1, s0),
        jnp.where(down, s2, s1),
        jnp.where(down, s3, s2),
        jnp.where(down, zero, s3),
    ]


def offset_weights(offset, frac, reach):
    stencil = cubic_weights(frac)
    spread = []
    for target in range(-reach, reach + 1):
        weight = jnp.zeros(frac.shape, jnp.float32)
        for step in range(4):
            weight = jnp.where(offset == target - step + 1, stencil[step], weight)
        spread.append(weight)
    return spread


def to_code(value):
    size = jnp.abs(value)
    code = jnp.clip(jnp.round((jnp.log(size) - TRACER_LOW) * TRACER_SCALE), 0.0, CODES - 1.0) + 1.0
    code = jnp.where(size < TRACER_LEAST, 0.0, code)
    return jnp.where(value < 0.0, -code, code).astype(jnp.int32).astype(jnp.int16)


def to_fixed(wind):
    return jnp.round(wind * (CODES / WIND_MOST)).astype(jnp.int32).astype(jnp.int16)


def from_fixed(code):
    return code.astype(jnp.int32).astype(jnp.float32) * (WIND_MOST / CODES)


def from_code(code):
    code = code.astype(jnp.int32).astype(jnp.float32)
    size = jnp.exp((jnp.abs(code) - 1.0) * (1.0 / TRACER_SCALE) + TRACER_LOW)
    size = jnp.where(code == 0.0, 0.0, size)
    return jnp.where(code < 0.0, -size, size)


def code_range(cells, count):
    low = math.log(0.98 * cells * ITEM_LOW)
    high = math.log(1.02 * cells * ITEM_HIGH * count)
    return low, 2.0 * CODES / (high - low)


def step_kernel(
    dims,
    winds_hbm, first_hbm, second_hbm, tracers_hbm, fluxes_hbm, weights_hbm, owner_hbm, block_hbm,
    moved_ref, arrived_ref, labels_out, dense_ref,
    owner_ref, block_ref, labels_ref,
    wind_pad, first_v, second_v, tracer_pad, fluxes_v, weights_v,
    products, outgoing, codes_v, codes_s, marks_v, relayed, running, dense_v, table_v, table_s,
    wind_pack, tracer_pack, wind_edge, tracer_edge, codes_out, codes_in,
    pack_out, pack_in, wind_out, wind_in,
    shifted, lhs, rhs_a, rhs_b, masks, wind_w, wind_sum, lev_w, row_w, col_w, col_at, moved_v,
    load_sem, code_sem, moved_sem, halo_send, halo_recv, near_sem, far_sem, mark_sem, relay_sem,
    dense_sem, table_sem, own_sem, labels_sem,
):
    chans, levels, rows, comps, tiles, links, blocks, wide, narrow, direct = dims
    lanes = LANES
    taps, reach = 2 * wide + 1, 2 * narrow + 1
    lat, lon = lax.axis_index("lat"), lax.axis_index("lon")
    lat_count, lon_count = lax.axis_size("lat"), lax.axis_size("lon")
    devices = lat_count * lon_count
    me = lat * lon_count + lon

    def by_level(source, target, n, start):
        return [
            pltpu.make_async_copy(
                source.at[:, level], target.at[:, pl.ds(start, rows), level, :], load_sem.at[n]
            )
            for level in range(levels)
        ]

    def whole(ref, sem):
        return pltpu.make_async_copy(ref, ref, sem)

    tables = [
        pltpu.make_async_copy(owner_hbm, owner_ref, load_sem.at[6]),
        pltpu.make_async_copy(block_hbm, block_ref, load_sem.at[7]),
    ]
    wind_loads = by_level(winds_hbm, wind_pad, 2, wide)
    tracer_loads = [
        pltpu.make_async_copy(
            tracers_hbm.at[chan], tracer_pad.at[:, pl.ds(narrow, rows), chan, :], load_sem.at[3]
        )
        for chan in range(chans)
    ]
    flux_load = pltpu.make_async_copy(fluxes_hbm, fluxes_v, load_sem.at[0])
    weight_load = pltpu.make_async_copy(weights_hbm, weights_v, load_sem.at[1])
    late_loads = by_level(first_hbm, first_v, 4, 0) + by_level(second_hbm, second_v, 5, 0)
    for load in wind_loads + tracer_loads + tables + [flux_load, weight_load] + late_loads:
        load.start()
    inner_winds = wind_pad.at[:, pl.ds(wide, rows)]
    inner_tracers = tracer_pad.at[:, pl.ds(narrow, rows)]

    barrier = pltpu.get_barrier_semaphore()

    for away in range(lat_count):
        there = lax.rem(lat + away, lat_count)

        def greet(n, carry, there=there):
            pl.semaphore_signal(
                barrier, inc=1, device_id=(there, lax.rem(lon + n, lon_count)), device_id_type=MESH
            )
            return carry

        lax.fori_loop(0 if away else 1, lon_count, greet, 0)

    lane8 = lax.broadcasted_iota(jnp.int32, (levels, lanes), 1)
    lane16 = lax.broadcasted_iota(jnp.int32, (chans, lanes), 1)
    west, east = lax.rem(lon + lon_count - 1, lon_count), lax.rem(lon + 1, lon_count)
    north, south = lat - 1, lat + 1
    has_north, has_south = lat > 0, lat < lat_count - 1
    halves = rows // 8

    def halo(n, source, target, where):
        return pltpu.make_async_remote_copy(
            src_ref=source, dst_ref=target, send_sem=halo_send.at[n], recv_sem=halo_recv.at[n],
            device_id=where, device_id_type=MESH,
        )

    wind_sides = [
        halo(0, wind_pack, wind_edge.at[0, pl.ds(1, halves)], (lat, east)),
        halo(1, wind_pack, wind_edge.at[1, pl.ds(1, halves)], (lat, west)),
    ]
    wind_north = [
        halo(2, wind_out.at[0], wind_in.at[1], (north, lon)),
        halo(3, wind_pack.at[0], wind_edge.at[0, halves + 1], (north, east)),
        halo(4, wind_pack.at[0], wind_edge.at[1, halves + 1], (north, west)),
    ]
    wind_south = [
        halo(5, wind_out.at[1], wind_in.at[0], (south, lon)),
        halo(6, wind_pack.at[halves - 1], wind_edge.at[0, 0], (south, east)),
        halo(7, wind_pack.at[halves - 1], wind_edge.at[1, 0], (south, west)),
    ]
    tracer_sides = [
        halo(8, tracer_pack, tracer_edge.at[0, pl.ds(narrow, rows)], (lat, east)),
        halo(9, tracer_pack, tracer_edge.at[1, pl.ds(narrow, rows)], (lat, west)),
    ]
    tracer_north = [
        halo(10, codes_out.at[0], codes_in.at[1], (north, lon)),
        halo(11, pack_out.at[0], pack_in.at[1, 0], (north, east)),
        halo(12, pack_out.at[0], pack_in.at[1, 1], (north, west)),
    ]
    tracer_south = [
        halo(13, codes_out.at[1], codes_in.at[0], (south, lon)),
        halo(14, pack_out.at[1], pack_in.at[0, 0], (south, east)),
        halo(15, pack_out.at[1], pack_in.at[0, 1], (south, west)),
    ]

    def each(condition, copies, act):
        @pl.when(condition)
        def _():
            for copy in copies:
                act(copy)

    start, arrive, leave = (lambda c: c.start()), (lambda c: c.wait_recv()), (lambda c: c.wait_send())
    whole(inner_winds, load_sem.at[2]).wait()
    for side, first in ((0, wide), (1, rows)):
        for comp in range(comps):
            for r in range(wide):
                wind_out[side, comp, r] = to_fixed(wind_pad[comp, first + r])
    pl.semaphore_wait(barrier, devices - 1)
    each(has_north, wind_north[:1], start)
    each(has_south, wind_south[:1], start)
    whole(inner_tracers, load_sem.at[3]).wait()

    def encode_rows(level, carry):
        for side, first in ((0, narrow), (1, rows)):
            for r in range(narrow):
                codes_out[side, level, r] = to_code(tracer_pad[level, first + r])
        return carry

    lax.fori_loop(0, levels, encode_rows, 0)
    each(has_north, tracer_north[:1], start)
    each(has_south, tracer_south[:1], start)

    for half in range(halves):
        for comp in range(comps):
            packed = jnp.zeros((levels, lanes), jnp.float32)
            for p in range(8):
                value = wind_pad[comp, wide + half * 8 + p]
                packed = jnp.where(
                    lane8 // 16 == p, pltpu.roll(value, (16 * p + 8) % lanes, 1), packed
                )
            wind_pack[half, comp] = to_fixed(packed)

    each(has_north, wind_north[1:], start)
    each(has_south, wind_south[1:], start)
    for copy in wind_sides:
        copy.start()

    def pack_row(r, carry):
        for side in range(2):
            packed = jnp.zeros((chans, lanes), jnp.float32)
            for level in range(levels):
                value = tracer_pad[level, narrow + 2 * r + side]
                packed = jnp.where(
                    lane16 // 16 == level, pltpu.roll(value, (16 * level + 8) % lanes, 1), packed
                )
            tracer_pack[2 * r + side] = packed
        return carry

    lax.fori_loop(0, rows // 2, pack_row, 0)

    for r in range(narrow):
        pack_out[0, r] = to_code(tracer_pack[r])
        pack_out[1, r] = to_code(tracer_pack[rows - narrow + r])
    each(has_north, tracer_north[1:], start)
    each(has_south, tracer_south[1:], start)
    for copy in tracer_sides:
        copy.start()
    for load in tables:
        load.wait()

    width = codes_v.shape[1]
    spot = lax.broadcasted_iota(jnp.int32, (1, width), 1)
    lowest = jnp.full((1, width), BIG, jnp.int32)
    highest = jnp.full((1, width), -1, jnp.int32)
    for t in range(tiles):
        for k in range(links):
            code = (t * links + k) * blocks + block_ref[k, t]
            hit = spot == owner_ref[k, t]
            lowest = jnp.minimum(lowest, jnp.where(hit, code, BIG))
            highest = jnp.maximum(highest, jnp.where(hit, code, -1))
    used = highest >= 0
    twice = highest != lowest
    low_code = jnp.where(used, lowest, 0)
    high_code = jnp.where(used, highest, 0)
    codes_v[...] = jnp.concatenate([low_code // blocks, high_code // blocks], axis=0)
    marks_v[...] = jnp.concatenate(
        [
            jnp.where(used, low_code % blocks, -1),
            jnp.where(jnp.logical_and(used, twice), high_code % blocks, -1),
        ],
        axis=0,
    )
    code_copy = pltpu.make_async_copy(codes_v, codes_s, code_sem)
    code_copy.start()

    @pl.when(jnp.logical_not(has_north))
    def _():
        wind_pad[:, 0:wide] = jnp.zeros((comps, wide, levels, lanes), jnp.float32)
        wind_edge[:, 0] = jnp.zeros((2, comps, levels, lanes), jnp.int16)
        tracer_pad[:, 0:narrow] = jnp.zeros((levels, narrow, chans, lanes), jnp.float32)
        tracer_edge[:, 0:narrow] = jnp.zeros((2, narrow, chans, lanes), jnp.float32)

    @pl.when(jnp.logical_not(has_south))
    def _():
        wind_pad[:, wide + rows :] = jnp.zeros((comps, wide, levels, lanes), jnp.float32)
        wind_edge[:, halves + 1] = jnp.zeros((2, comps, levels, lanes), jnp.int16)
        tracer_pad[:, narrow + rows :] = jnp.zeros((levels, narrow, chans, lanes), jnp.float32)
        tracer_edge[:, narrow + rows :] = jnp.zeros((2, narrow, chans, lanes), jnp.float32)

    code_copy.wait()
    flux_load.wait()
    weight_load.wait()
    group = 3 if tiles % 3 == 0 else 1

    def multiply(n, carry):
        for g in range(group):
            t = n * group + g
            right = jnp.concatenate([weights_v[t, k] for k in range(links)], axis=1)
            done = jnp.dot(fluxes_v[t], right, preferred_element_type=jnp.float32)
            for k in range(links):
                products[t * links + k] = done[:, k * lanes : (k + 1) * lanes].astype(jnp.bfloat16)
        return carry

    lax.fori_loop(0, tiles // group, multiply, 0)

    half_count = lat_count // 2
    near = half_count * lon_count
    base = lat // half_count * half_count
    near_first = base * lon_count
    far_first = lax.rem(base + half_count, lat_count) * lon_count
    mine = me - near_first
    tail = pl.ds(direct, products.shape[1] - direct)
    head = pl.ds(0, direct)

    def at_device(p):
        return (p // lon_count, lax.rem(p, lon_count))

    def near_copy(s):
        return pltpu.make_async_remote_copy(
            src_ref=outgoing.at[near_first + s], dst_ref=arrived_ref.at[me],
            send_sem=near_sem.at[0], recv_sem=near_sem.at[1],
            device_id=at_device(near_first + s), device_id_type=MESH,
        )

    def far_copy(s):
        return pltpu.make_async_remote_copy(
            src_ref=outgoing.at[far_first + s, :, head], dst_ref=arrived_ref.at[me, :, head],
            send_sem=far_sem.at[0], recv_sem=far_sem.at[1],
            device_id=at_device(far_first + s), device_id_type=MESH,
        )

    def relay_copy(s):
        return pltpu.make_async_remote_copy(
            src_ref=outgoing.at[far_first + s, :, tail], dst_ref=relayed.at[mine],
            send_sem=relay_sem.at[0], recv_sem=relay_sem.at[1],
            device_id=at_device(near_first + s), device_id_type=MESH,
        )

    def send_marks(first, recv, begin):
        def one(k, carry):
            s = lax.rem(mine + k, near)
            pltpu.make_async_remote_copy(
                src_ref=marks_v, dst_ref=labels_ref.at[:, me, :],
                send_sem=mark_sem.at[0], recv_sem=mark_sem.at[recv],
                device_id=at_device(first + s), device_id_type=MESH,
            ).start()
            return carry

        lax.fori_loop(begin, near, one, 0)

    send_marks(near_first, 1, 1)
    send_marks(far_first, 2, 0)

    def ring(away, n):
        return lax.rem(lat - base + away, half_count) * lon_count + lax.rem(lon + n, lon_count)

    def fill(first, away):
        def one(n, carry):
            p = first + ring(away, n)
            for c in range(CAP):
                outgoing[p, c] = products[codes_s[c, p]]
            return carry

        lax.fori_loop(0, lon_count, one, 0)

    def send(copy, away, begin):
        def one(n, carry):
            copy(ring(away, n)).start()
            return carry

        lax.fori_loop(begin, lon_count, one, 0)

    for away in list(range(1, half_count)) + [0]:
        fill(far_first, away)
        send(relay_copy, away, 0 if away else 1)
        send(far_copy, away, 0)
    for away in [0] + list(range(1, half_count)):
        fill(near_first, away)
        send(near_copy, away, 0 if away else 1)
    own_copies = [
        pltpu.make_async_copy(
            outgoing.at[far_first + mine, :, tail], relayed.at[mine], own_sem.at[0]
        ),
        pltpu.make_async_copy(outgoing.at[me], arrived_ref.at[me], own_sem.at[1]),
        pltpu.make_async_copy(marks_v, labels_ref.at[:, me, :], own_sem.at[2]),
    ]
    for copy in own_copies:
        copy.start()

    others = pl.ds(0, near - 1)
    labels_copy = pltpu.make_async_copy(labels_ref, labels_out, labels_sem)

    count = CAP * near
    table_copy = pltpu.make_async_copy(table_v, table_s, table_sem)
    twin = (far_first + mine) // lon_count
    dense_copy = pltpu.make_async_remote_copy(
        src_ref=dense_v, dst_ref=dense_ref, send_sem=dense_sem.at[0], recv_sem=dense_sem.at[1],
        device_id=(twin, lon), device_id_type=MESH,
    )

    def sort_relayed():
        whole(labels_ref.at[:, others], mark_sem.at[1]).wait()
        own_copies[2].wait()
        width = table_v.shape[1]
        sub = lax.broadcasted_iota(jnp.int32, (count, width), 0)
        lane = lax.broadcasted_iota(jnp.int32, (count, width), 1)
        spot = lax.broadcasted_iota(jnp.int32, (near, width), 1)
        column = jnp.concatenate(
            [
                jnp.sum(
                    jnp.where(
                        spot == far_first + mine,
                        labels_ref[c, pl.ds(pl.multiple_of(near_first, 8), near), :],
                        0,
                    ),
                    axis=1,
                    keepdims=True,
                )
                for c in range(CAP)
            ],
            axis=0,
        )
        label = jnp.broadcast_to(jnp.where(column < 0, blocks, column), (count, width))
        across = jnp.sum(jnp.where(sub == lane, label, 0), axis=0, keepdims=True)
        across = jnp.broadcast_to(across, (count, width))
        inside = lane < count
        before = jnp.logical_or(label < across, jnp.logical_and(label == across, sub < lane))
        rank = jnp.sum(jnp.where(before, 1, 0), axis=0, keepdims=True)
        pick = jnp.logical_and(jnp.broadcast_to(rank, (count, width)) == sub, inside)
        code = lax.rem(lane, near) * CAP + lane // near
        item = jnp.sum(jnp.where(pick, code, 0), axis=1, keepdims=True)
        ordered = jnp.sum(jnp.where(pick, across, 0), axis=1, keepdims=True)
        ordered = jnp.broadcast_to(ordered, (count, width))
        same = jnp.logical_and(ordered == pltpu.roll(ordered, 1, 0), sub > 0)
        upto = jnp.sum(jnp.where(jnp.logical_and(across <= sub, inside), 1, 0), axis=1, keepdims=True)
        equal = jnp.sum(jnp.where(jnp.logical_and(across == sub, inside), 1, 0), axis=1, keepdims=True)
        final = jnp.where(equal > 0, upto - 1, count)
        table_v[...] = jnp.where(lane == 0, item, jnp.where(lane == 1, jnp.where(same, 1, 0), final))
        table_copy.start()

    def take_labels():
        whole(labels_ref.at[:, pl.ds(0, near)], mark_sem.at[2]).wait()
        labels_copy.start()

    def sum_relayed():
        whole(relayed.at[others], relay_sem.at[1]).wait()
        own_copies[0].wait()
        table_copy.wait()
        size = products.shape[1] - direct

        def add(n, total):
            item = table_s[n, 0]
            kept = table_s[n, 1].astype(jnp.float32)
            total = total * kept + relayed[item // CAP, lax.rem(item, CAP)].astype(jnp.float32)
            running[n] = total
            return total

        lax.fori_loop(0, count, add, jnp.zeros((size, lanes), jnp.float32))
        running[count] = jnp.zeros((size, lanes), jnp.float32)
        low, scale = code_range(fluxes_v.shape[2], count)

        def encode(s, carry):
            value = running[table_s[s, 2]]
            code = jnp.round((jnp.log(value) - low) * scale) - CODES
            code = jnp.where(value > 0.0, jnp.clip(code, -CODES, CODES), -CODES - 1.0)
            dense_v[s] = code.astype(jnp.int32).astype(jnp.int16)
            return carry

        lax.fori_loop(0, blocks, encode, 0)

    deep, across16 = (
        lax.broadcasted_iota(jnp.int32, (16, lanes), 0),
        lax.broadcasted_iota(jnp.int32, (16, lanes), 1),
    )
    groups = lanes // 16
    for t in range(groups):
        reached = jnp.abs(16 * t + deep - across16) <= narrow
        masks[t] = jnp.where(reached, 1.0, 0.0).astype(jnp.bfloat16)
    outer = jnp.where(deep < 8, deep - 8, deep + (lanes - 8))
    masks[groups] = jnp.where(jnp.abs(outer - across16) <= narrow, 1.0, 0.0).astype(jnp.bfloat16)
    rhs_a[...] = jnp.zeros_like(rhs_a)
    rhs_b[...] = jnp.zeros_like(rhs_b)

    whole(first_v, load_sem.at[4]).wait()
    whole(second_v, load_sem.at[5]).wait()
    for copy in wind_sides:
        copy.wait_recv()
    each(has_north, wind_south, arrive)
    each(has_south, wind_north, arrive)

    def wind_rows_in(place, first):
        for comp in range(comps):
            for r in range(wide):
                wind_pad[comp, first + r] = from_fixed(wind_in[place, comp, r])

    pl.when(has_north)(functools.partial(wind_rows_in, 0, 0))
    pl.when(has_south)(functools.partial(wind_rows_in, 1, wide + rows))

    def shift_row(r, carry):
        turned = r + 8 - wide
        half, p = turned // 8, turned % 8
        back = lax.rem(2 * lanes - 8 - 16 * p, lanes)
        for comp in range(comps):
            merged = jnp.where(
                lane8 % 16 < 8, from_fixed(wind_edge[0, half, comp]), from_fixed(wind_edge[1, half, comp])
            )
            edge = pltpu.roll(merged, back, 1)
            main = wind_pad[comp, r]
            for e in range(taps):
                d = e - wide
                if d > 0:
                    piece = pltpu.roll(jnp.where(lane8 < d, edge, main), lanes - d, 1)
                elif d < 0:
                    piece = pltpu.roll(jnp.where(lane8 >= lanes + d, edge, main), -d, 1)
                else:
                    piece = main
                low, high = piece[:1], piece[levels - 1 :]
                shifted[e * 5 + 0, comp, r] = jnp.concatenate([low, low, piece[: levels - 2]], axis=0)
                shifted[e * 5 + 1, comp, r] = jnp.concatenate([low, piece[: levels - 1]], axis=0)
                shifted[e * 5 + 2, comp, r] = piece
                shifted[e * 5 + 3, comp, r] = jnp.concatenate([piece[1:], high], axis=0)
                shifted[e * 5 + 4, comp, r] = jnp.concatenate([piece[2:], high, high], axis=0)
        return carry

    lax.fori_loop(0, rows + 2 * wide, shift_row, 0)

    column = lax.broadcasted_iota(jnp.int32, (levels, lanes), 1)

    def wind_start(side, i):
        off = [first_v[comp, i] for comp in range(comps)]
        frac = [
            jnp.clip(-wind_pad[comp, wide + i] - off[comp].astype(jnp.float32), 0.0, 1.0)
            for comp in range(comps)
        ]
        weights = level_weights(off[0], frac[0])
        weights += offset_weights(off[1], frac[1], wide) + offset_weights(off[2], frac[2], wide)
        for n, weight in enumerate(weights):
            wind_w[side, n] = weight
        for comp in range(comps):
            wind_sum[side, comp] = jnp.zeros((levels, lanes), jnp.float32)

    def wind_unit(first, q):
        sides = [side for side in range(2) if 0 <= q - side < taps]
        cw = [[wind_w[side, 5 + taps + e] for e in range(taps)] for side in sides]
        rw = [wind_w[side, 5 + q - side] for side in sides]
        total = [[wind_sum[side, comp] for comp in range(comps)] for side in sides]
        for above in range(5):
            pair = [wind_w[side, above] * rw[n] for n, side in enumerate(sides)]
            for comp in range(comps):
                inner = [None] * len(sides)
                for e in range(taps):
                    value = shifted[e * 5 + above, comp, first + q]
                    for n in range(len(sides)):
                        term = cw[n][e] * value
                        inner[n] = term if e == 0 else inner[n] + term
                for n in range(len(sides)):
                    total[n][comp] = total[n][comp] + pair[n] * inner[n]
        for n, side in enumerate(sides):
            for comp in range(comps):
                wind_sum[side, comp] = total[n][comp]

    def wind_finish(side, i):
        off = [second_v[comp, i] for comp in range(comps)]
        frac = [
            jnp.clip(
                -(wind_pad[comp, wide + i] + wind_sum[side, comp]) * 0.5
                - off[comp].astype(jnp.float32),
                0.0,
                1.0,
            )
            for comp in range(comps)
        ]
        for n, weight in enumerate(level_weights(off[0], frac[0])):
            lev_w[n, i] = weight
        for n, weight in enumerate(offset_weights(off[1], frac[1], narrow)):
            row_w[n, i] = weight
        for n, weight in enumerate(cubic_weights(frac[2])):
            col_w[n, i] = weight
        col_at[i] = off[2] - 1 + column

    for side in range(2):
        wind_start(side, side)

    wind_unit(0, 0)
    for q in range(1, taps):
        wind_unit(0, q)
    wind_unit(0, taps)
    for side in range(2):
        wind_finish(side, side)

    for copy in tracer_sides:
        copy.wait_recv()
    each(has_north, tracer_south, arrive)
    each(has_south, tracer_north, arrive)

    def decode_rows(place, first):
        def decode_level(level, carry):
            for r in range(narrow):
                tracer_pad[level, first + r] = from_code(codes_in[place, level, r])
            return carry

        lax.fori_loop(0, levels, decode_level, 0)
        for side in range(2):
            for r in range(narrow):
                tracer_edge[side, first + r] = from_code(pack_in[place, side, r])

    pl.when(has_north)(functools.partial(decode_rows, 0, 0))
    pl.when(has_south)(functools.partial(decode_rows, 1, narrow + rows))

    def split_row(r, carry):
        merged = jnp.where(lane16 % 16 < 8, tracer_edge[0, r], tracer_edge[1, r])
        turned = [merged] + [pltpu.roll(merged, lanes - 16 * s, 1) for s in range(1, levels)]
        for level in range(levels):
            value = tracer_pad[level, r]
            top = value.astype(jnp.bfloat16)
            lhs[level, r, :, 0:lanes] = top
            lhs[level, r, :, lanes : 2 * lanes] = (value - top.astype(jnp.float32)).astype(jnp.bfloat16)
            edge = jnp.where(
                lane16 < 16,
                turned[level],
                jnp.where(lane16 < 32, turned[(level - 1) % levels], turned[(level - 2) % levels]),
            )
            edge_top = edge.astype(jnp.bfloat16).astype(jnp.float32)
            edge = jnp.where(lane16 < 32, edge_top, edge - edge_top)
            lhs[level, r, :, 2 * lanes : 3 * lanes] = edge.astype(jnp.bfloat16)
        return carry

    lax.fori_loop(0, rows + 2 * narrow, split_row, 0)

    deep8 = lax.broadcasted_iota(jnp.int32, (8, lanes), 0)

    def build(level, pair, rhs):
        for side in range(2):
            i = pair * 2 + side
            cols = slice(side * lanes, (side + 1) * lanes)
            at = col_at[i, pl.ds(level, 1), :]
            away = jnp.bitwise_and(deep8 - at, 7)
            value = jnp.zeros((8, lanes), jnp.float32)
            for n in range(4):
                value = jnp.where(away == n, col_w[n, i, pl.ds(level, 1), :], value)
            rest = value - value.astype(jnp.bfloat16).astype(jnp.float32)
            top16 = jnp.concatenate([value, value], axis=0).astype(jnp.bfloat16)
            rest16 = jnp.concatenate([rest, rest], axis=0).astype(jnp.bfloat16)
            for t in range(groups):
                top = top16 * masks[t]
                rhs[16 * t : 16 * t + 16, cols] = top
                rhs[2 * lanes + 16 * t : 2 * lanes + 16 * t + 16, cols] = top
                rhs[lanes + 16 * t : lanes + 16 * t + 16, cols] = rest16 * masks[t]
            top = top16 * masks[groups]
            rhs[3 * lanes : 3 * lanes + 16, cols] = top
            rhs[3 * lanes + 16 : 3 * lanes + 32, cols] = rest16 * masks[groups]
            rhs[3 * lanes + 32 : 3 * lanes + 48, cols] = top

    span = reach + 1

    def apply(level, pair, rhs):
        low, high = max(level - 2, 0), min(level + 2, levels - 1)
        count = high - low + 1
        part = lambda at: lhs[
            low : high + 1, pl.ds(pair * 2, span), :, at * lanes : (at + 1) * lanes
        ].reshape(count * span * chans, lanes)
        top, rest, edge = part(0), part(1), part(2)
        left = jnp.concatenate([top, top, rest, edge], axis=1)
        done = jnp.dot(left, rhs[...], preferred_element_type=jnp.float32)
        for side in range(2):
            i = pair * 2 + side
            cols = slice(side * lanes, (side + 1) * lanes)
            rw = [row_w[n, i, pl.ds(level, 1), :] for n in range(reach)]
            total = jnp.zeros((chans, lanes), jnp.float32)
            for m in range(count):
                lw = None
                for n in range(5):
                    if min(max(level - 2 + n, 0), levels - 1) == low + m:
                        weight = lev_w[n, i, pl.ds(level, 1), :]
                        lw = weight if lw is None else lw + weight
                inner = jnp.zeros((chans, lanes), jnp.float32)
                for n in range(reach):
                    first = (m * span + n + side) * chans
                    inner = inner + rw[n] * done[first : first + chans, cols]
                total = total + lw * inner
            moved_v[i, level] = total

    pairs = rows // 2
    shares = levels - 1
    cuts = [(n * (taps + 1) + shares // 2) // shares for n in range(shares + 1)]
    both = [rhs_a, rhs_b]
    build(0, 0, rhs_a)

    def moved_copy(pair):
        return pltpu.make_async_copy(
            moved_v.at[pl.ds(pair * 2, 2)], moved_ref.at[pl.ds(pair * 2, 2)], moved_sem
        )

    def pair_step(pair, carry):
        after = jnp.minimum(pair + 1, pairs - 1)
        def level_step(level):
            if level == 0:
                for side in range(2):
                    wind_start(side, after * 2 + side)
            if level < shares:
                for q in range(cuts[level], cuts[level + 1]):
                    wind_unit(after * 2, q)
            if level == shares - 1:
                for side in range(2):
                    wind_finish(side, after * 2 + side)
            if level < levels - 1:
                build(level + 1, pair, both[(level + 1) % 2])
            else:
                build(0, after, both[0])
            apply(level, pair, both[level % 2])

        pl.when(pair == 1)(sort_relayed)
        pl.when(pair == 2)(sum_relayed)
        pl.when(pair == 3)(dense_copy.start)
        pl.when(pair == pairs - 1)(take_labels)
        for level in range(levels):
            pl.when(pair >= 0)(functools.partial(level_step, level))
        moved_copy(pair).start()
        return carry

    lax.fori_loop(0, pairs, pair_step, 0)
    whole(moved_v, moved_sem).wait()

    for copy in wind_sides + tracer_sides:
        copy.wait_send()
    each(has_north, wind_north + tracer_north, leave)
    each(has_south, wind_south + tracer_south, leave)
    own_copies[1].wait()

    whole(outgoing.at[others], near_sem.at[0]).wait()
    whole(outgoing.at[pl.ds(0, near), :, head], far_sem.at[0]).wait()
    whole(outgoing.at[others, :, tail], relay_sem.at[0]).wait()
    whole(labels_ref.at[:, pl.ds(0, devices - 1)], mark_sem.at[0]).wait()
    labels_copy.wait()
    whole(outgoing.at[pl.ds(0, near), :, head], far_sem.at[1]).wait()
    whole(outgoing.at[others], near_sem.at[1]).wait()
    dense_copy.wait()


def join_kernel(
    dims, moved_hbm, arrived_hbm, labels_hbm, dense_hbm, out_hbm,
    labels_ref, total, sums, more, near_v, far_v, dense_v, load_sem, out_sem,
):
    chans, levels, rows, blocks, direct, cells = dims
    lat_count, lon_count = lax.axis_size("lat"), lax.axis_size("lon")
    me = lax.axis_index("lat") * lon_count + lax.axis_index("lon")
    near = near_v.shape[0]
    near_first = me // near * near
    far_first = lax.rem(near_first + near, lat_count * lon_count)
    lanes = total.shape[3]
    label_load = pltpu.make_async_copy(labels_hbm, labels_ref, load_sem.at[0])
    near_load = pltpu.make_async_copy(arrived_hbm.at[pl.ds(near_first, near)], near_v, load_sem.at[1])
    far_load = pltpu.make_async_copy(
        arrived_hbm.at[pl.ds(far_first, near), :, pl.ds(0, direct)], far_v, load_sem.at[2]
    )
    dense_load = pltpu.make_async_copy(dense_hbm, dense_v, load_sem.at[3])
    loads = [
        pltpu.make_async_copy(moved_hbm.at[:, level], total.at[:, :, level, :], load_sem.at[4])
        for level in range(levels)
    ]
    for load in [label_load, dense_load, near_load, far_load] + loads:
        load.start()
    sums[...] = jnp.zeros_like(sums)
    more[...] = jnp.zeros_like(more)
    dense_load.wait()
    low, scale = code_range(cells, CAP * near)
    cut = direct // levels

    def decode(s, carry):
        code = dense_v[s].astype(jnp.int32).astype(jnp.float32)
        value = jnp.exp((code + CODES) * (1.0 / scale) + low)
        value = jnp.where(code < -CODES, 0.0, value)
        more[s, cut:] = value.reshape(chans - cut, levels, lanes)
        return carry

    lax.fori_loop(0, blocks, decode, 0)

    def place(n, c):
        label = labels_ref[c, n, me]
        return jnp.where(label < 0, blocks, label)

    def add_near(n, carry):
        for c, one in enumerate((sums, more)):
            at = place(near_first + n, c)
            one[at] = one[at] + near_v[n, c].astype(jnp.float32).reshape(chans, levels, lanes)
        return carry

    def add_far(n, carry):
        for c, one in enumerate((sums, more)):
            at = place(far_first + n, c)
            one[at, :cut] = one[at, :cut] + far_v[n, c].astype(jnp.float32).reshape(cut, levels, lanes)
        return carry

    label_load.wait()
    near_load.wait()
    lax.fori_loop(0, near, add_near, 0)
    far_load.wait()
    lax.fori_loop(0, near, add_far, 0)
    outs = [
        pltpu.make_async_copy(total.at[s], out_hbm.at[:, :, s, :], out_sem.at[s]) for s in range(rows)
    ]
    pltpu.make_async_copy(total, total, load_sem.at[4]).wait()
    for s in range(rows):
        total[s] = total[s] + (sums[s] + more[s])
        if s:
            outs[s - 1].start()
    outs[rows - 1].start()
    for out in outs:
        out.wait()


def body(
    tracers, winds, depart_first, depart_second, fluxes, remap_weights, target_device, target_block
):
    wide = HMAX + 1
    narrow = max((HMAX + 1) // 2 + 1, HMAX // 2 + 2)
    chans, levels, rows, lanes = tracers.shape
    comps = winds.shape[0]
    tiles, links = target_device.shape
    depth, cells = fluxes.shape[1:]
    cols = remap_weights.shape[3]
    blocks = rows * lanes // cols
    devices = lax.axis_size("lat") * lax.axis_size("lon")
    padded = -(-devices // LANES) * LANES
    halves = rows // 8
    direct = depth * DIRECT_PART // 128 // 16 * 16
    near = devices // 2
    dims = (chans, levels, rows, comps, tiles, links, blocks, wide, narrow, direct)
    hbm = pl.BlockSpec(memory_space=pl.ANY)
    f32, b16, i32 = jnp.float32, jnp.bfloat16, jnp.int32
    dma = pltpu.SemaphoreType.DMA
    moved, arrived, labels, dense = pl.pallas_call(
        functools.partial(step_kernel, dims),
        out_shape=(
            jax.ShapeDtypeStruct((rows, levels, chans, lanes), f32),
            jax.ShapeDtypeStruct((devices, CAP, depth, cols), b16),
            jax.ShapeDtypeStruct((CAP, devices, padded), i32),
            jax.ShapeDtypeStruct((blocks, depth - direct, cols), jnp.int16),
        ),
        in_specs=[hbm] * 8,
        out_specs=(hbm, hbm, hbm, hbm),
        scratch_shapes=[
            pltpu.SMEM((links, tiles), i32),
            pltpu.SMEM((links, tiles), i32),
            pltpu.VMEM((CAP, devices, padded), i32),
            pltpu.VMEM((comps, rows + 2 * wide, levels, lanes), f32),
            pltpu.VMEM((comps, rows, levels, lanes), i32),
            pltpu.VMEM((comps, rows, levels, lanes), i32),
            pltpu.VMEM((levels, rows + 2 * narrow, chans, lanes), f32),
            pltpu.VMEM((tiles, depth, cells), b16),
            pltpu.VMEM((tiles, links, cells, cols), b16),
            pltpu.VMEM((tiles * links, depth, cols), b16),
            pltpu.VMEM((devices, CAP, depth, cols), b16),
            pltpu.VMEM((CAP, padded), i32),
            pltpu.SMEM((CAP, padded), i32),
            pltpu.VMEM((CAP, padded), i32),
            pltpu.VMEM((near, CAP, depth - direct, cols), b16),
            pltpu.VMEM((near * CAP + 1, depth - direct, cols), f32),
            pltpu.VMEM((blocks, depth - direct, cols), jnp.int16),
            pltpu.VMEM((near * CAP, padded), i32),
            pltpu.SMEM((near * CAP, padded), i32),
            pltpu.VMEM((halves, comps, levels, lanes), jnp.int16),
            pltpu.VMEM((rows, chans, lanes), f32),
            pltpu.VMEM((2, halves + 2, comps, levels, lanes), jnp.int16),
            pltpu.VMEM((2, rows + 2 * narrow, chans, lanes), f32),
            pltpu.VMEM((2, levels, narrow, chans, lanes), jnp.int16),
            pltpu.VMEM((2, levels, narrow, chans, lanes), jnp.int16),
            pltpu.VMEM((2, narrow, chans, lanes), jnp.int16),
            pltpu.VMEM((2, 2, narrow, chans, lanes), jnp.int16),
            pltpu.VMEM((2, comps, wide, levels, lanes), jnp.int16),
            pltpu.VMEM((2, comps, wide, levels, lanes), jnp.int16),
            pltpu.VMEM((5 * (2 * wide + 1), comps, rows + 2 * wide, levels, lanes), f32),
            pltpu.VMEM((levels, rows + 2 * narrow, chans, 3 * lanes), b16),
            pltpu.VMEM((4 * lanes, 2 * lanes), b16),
            pltpu.VMEM((4 * lanes, 2 * lanes), b16),
            pltpu.VMEM((lanes // 16 + 1, 16, lanes), b16),
            pltpu.VMEM((2, 5 + 2 * (2 * wide + 1), levels, lanes), f32),
            pltpu.VMEM((2, comps, levels, lanes), f32),
            pltpu.VMEM((5, rows, levels, lanes), f32),
            pltpu.VMEM((2 * narrow + 1, rows, levels, lanes), f32),
            pltpu.VMEM((4, rows, levels, lanes), f32),
            pltpu.VMEM((rows, levels, lanes), i32),
            pltpu.VMEM((rows, levels, chans, lanes), f32),
            dma((8,)),
            dma(()),
            dma(()),
            dma((16,)),
            dma((16,)),
            dma((2,)),
            dma((2,)),
            dma((3,)),
            dma((2,)),
            dma((2,)),
            dma(()),
            dma((3,)),
            dma(()),
        ],
        compiler_params=pltpu.CompilerParams(
            collective_id=0, has_side_effects=True, vmem_limit_bytes=62 * 1024 * 1024
        ),
        name="step",
    )(winds, depart_first, depart_second, tracers, fluxes, remap_weights, target_device.T, target_block.T)
    return pl.pallas_call(
        functools.partial(join_kernel, (chans, levels, rows, blocks, direct, cells)),
        out_shape=jax.ShapeDtypeStruct((chans, levels, rows, lanes), f32),
        in_specs=[hbm] * 4,
        out_specs=hbm,
        scratch_shapes=[
            pltpu.SMEM((CAP, devices, padded), i32),
            pltpu.VMEM((rows, chans, levels, lanes), f32),
            pltpu.VMEM((blocks + 1, chans, levels, lanes), f32),
            pltpu.VMEM((blocks + 1, chans, levels, lanes), f32),
            pltpu.VMEM((near, CAP, depth, cols), b16),
            pltpu.VMEM((near, CAP, direct, cols), b16),
            pltpu.VMEM((blocks, depth - direct, cols), jnp.int16),
            dma((5,)),
            dma((rows,)),
        ],
        compiler_params=pltpu.CompilerParams(vmem_limit_bytes=62 * 1024 * 1024),
        name="join",
    )(moved, arrived, labels, dense)


def solution(mesh):
    in_specs = (
        P(None, None, "lat", "lon"),
        P(None, None, "lat", "lon"),
        P(None, None, "lat", "lon"),
        P(None, None, "lat", "lon"),
        P(("lat", "lon"), None, None),
        P(("lat", "lon"), None, None, None),
        P(("lat", "lon"), None),
        P(("lat", "lon"), None),
    )
    out_specs = P(None, None, "lat", "lon")
    return jax.shard_map(body, mesh=mesh, in_specs=in_specs, out_specs=out_specs, check_vma=False)
```

```python
import functools
import math

import jax
import jax.numpy as jnp
from jax import lax
from jax.experimental import pallas as pl
from jax.experimental.pallas import tpu as pltpu
from jax.sharding import PartitionSpec as P

CAP = 2
HMAX = 3
MESH = pl.DeviceIdType.MESH
LANES = 128
BIG = 1 << 20
DIRECT_PART = 48
CODES = 32767.0
ITEM_LOW = 0.049804688 * 0.00019931793
ITEM_HIGH = 5.0 * 0.019897461
WIND_MOST = 4.0
TRACER_LEAST = 6.0 * 2.0**-24
TRACER_LOW = math.log(TRACER_LEAST)
TRACER_SCALE = (CODES - 1.0) / (math.log(6.0) - TRACER_LOW)


def cubic_weights(frac):
    first = -frac * (frac - 1.0) * (frac - 2.0) / 6.0
    second = (frac + 1.0) * (frac - 1.0) * (frac - 2.0) / 2.0
    third = -(frac + 1.0) * frac * (frac - 2.0) / 2.0
    fourth = (frac + 1.0) * frac * (frac - 1.0) / 6.0
    return (first, second, third, fourth)


def level_weights(offset, frac):
    s0, s1, s2, s3 = cubic_weights(frac)
    down = offset < 0
    zero = jnp.zeros_like(frac)
    return [
        jnp.where(down, s0, zero),
        jnp.where(down, s1, s0),
        jnp.where(down, s2, s1),
        jnp.where(down, s3, s2),
        jnp.where(down, zero, s3),
    ]


def offset_weights(offset, frac, reach):
    stencil = cubic_weights(frac)
    spread = []
    for target in range(-reach, reach + 1):
        weight = jnp.zeros(frac.shape, jnp.float32)
        for step in range(4):
            weight = jnp.where(offset == target - step + 1, stencil[step], weight)
        spread.append(weight)
    return spread


def to_code(value):
    size = jnp.abs(value)
    code = jnp.clip(jnp.round((jnp.log(size) - TRACER_LOW) * TRACER_SCALE), 0.0, CODES - 1.0) + 1.0
    code = jnp.where(size < TRACER_LEAST, 0.0, code)
    return jnp.where(value < 0.0, -code, code).astype(jnp.int32).astype(jnp.int16)


def to_fixed(wind):
    return jnp.round(wind * (CODES / WIND_MOST)).astype(jnp.int32).astype(jnp.int16)


def from_fixed(code):
    return code.astype(jnp.int32).astype(jnp.float32) * (WIND_MOST / CODES)


def from_code(code):
    code = code.astype(jnp.int32).astype(jnp.float32)
    size = jnp.exp((jnp.abs(code) - 1.0) * (1.0 / TRACER_SCALE) + TRACER_LOW)
    size = jnp.where(code == 0.0, 0.0, size)
    return jnp.where(code < 0.0, -size, size)


def code_range(cells, count):
    low = math.log(0.98 * cells * ITEM_LOW)
    high = math.log(1.02 * cells * ITEM_HIGH * count)
    return low, 2.0 * CODES / (high - low)


def step_kernel(
    dims,
    winds_hbm, first_hbm, second_hbm, tracers_hbm, fluxes_hbm, weights_hbm, owner_hbm, block_hbm,
    moved_ref, arrived_ref, labels_out, dense_ref,
    owner_ref, block_ref, labels_ref,
    wind_pad, first_v, second_v, tracer_pad, fluxes_v, weights_v,
    products, outgoing, codes_v, codes_s, marks_v, relayed, running, dense_v, table_v, table_s,
    wind_pack, tracer_pack, wind_edge, tracer_edge, codes_out, codes_in,
    pack_out, pack_in, wind_out, wind_in,
    shifted, lhs, rhs_a, rhs_b, masks, wind_w, wind_sum, lev_w, row_w, col_w, col_at, moved_v,
    load_sem, code_sem, moved_sem, halo_send, halo_recv, near_sem, far_sem, mark_sem, relay_sem,
    dense_sem, table_sem, own_sem, labels_sem,
):
    chans, levels, rows, comps, tiles, links, blocks, wide, narrow, direct = dims
    lanes = LANES
    taps, reach = 2 * wide + 1, 2 * narrow + 1
    lat, lon = lax.axis_index("lat"), lax.axis_index("lon")
    lat_count, lon_count = lax.axis_size("lat"), lax.axis_size("lon")
    devices = lat_count * lon_count
    me = lat * lon_count + lon

    def by_level(source, target, n, start):
        return [
            pltpu.make_async_copy(
                source.at[:, level], target.at[:, pl.ds(start, rows), level, :], load_sem.at[n]
            )
            for level in range(levels)
        ]

    def whole(ref, sem):
        return pltpu.make_async_copy(ref, ref, sem)

    tables = [
        pltpu.make_async_copy(owner_hbm, owner_ref, load_sem.at[6]),
        pltpu.make_async_copy(block_hbm, block_ref, load_sem.at[7]),
    ]
    wind_loads = by_level(winds_hbm, wind_pad, 2, wide)
    tracer_loads = [
        pltpu.make_async_copy(
            tracers_hbm.at[chan], tracer_pad.at[:, pl.ds(narrow, rows), chan, :], load_sem.at[3]
        )
        for chan in range(chans)
    ]
    flux_load = pltpu.make_async_copy(fluxes_hbm, fluxes_v, load_sem.at[0])
    weight_load = pltpu.make_async_copy(weights_hbm, weights_v, load_sem.at[1])
    late_loads = by_level(first_hbm, first_v, 4, 0) + by_level(second_hbm, second_v, 5, 0)
    for load in wind_loads + tracer_loads + tables + [flux_load, weight_load] + late_loads:
        load.start()
    inner_winds = wind_pad.at[:, pl.ds(wide, rows)]
    inner_tracers = tracer_pad.at[:, pl.ds(narrow, rows)]

    barrier = pltpu.get_barrier_semaphore()

    for away in range(lat_count):
        there = lax.rem(lat + away, lat_count)

        def greet(n, carry, there=there):
            pl.semaphore_signal(
                barrier, inc=1, device_id=(there, lax.rem(lon + n, lon_count)), device_id_type=MESH
            )
            return carry

        lax.fori_loop(0 if away else 1, lon_count, greet, 0)

    lane8 = lax.broadcasted_iota(jnp.int32, (levels, lanes), 1)
    lane16 = lax.broadcasted_iota(jnp.int32, (chans, lanes), 1)
    west, east = lax.rem(lon + lon_count - 1, lon_count), lax.rem(lon + 1, lon_count)
    north, south = lat - 1, lat + 1
    has_north, has_south = lat > 0, lat < lat_count - 1
    halves = rows // 8

    def halo(n, source, target, where):
        return pltpu.make_async_remote_copy(
            src_ref=source, dst_ref=target, send_sem=halo_send.at[n], recv_sem=halo_recv.at[n],
            device_id=where, device_id_type=MESH,
        )

    wind_sides = [
        halo(0, wind_pack, wind_edge.at[0, pl.ds(1, halves)], (lat, east)),
        halo(1, wind_pack, wind_edge.at[1, pl.ds(1, halves)], (lat, west)),
    ]
    wind_north = [
        halo(2, wind_out.at[0], wind_in.at[1], (north, lon)),
        halo(3, wind_pack.at[0], wind_edge.at[0, halves + 1], (north, east)),
        halo(4, wind_pack.at[0], wind_edge.at[1, halves + 1], (north, west)),
    ]
    wind_south = [
        halo(5, wind_out.at[1], wind_in.at[0], (south, lon)),
        halo(6, wind_pack.at[halves - 1], wind_edge.at[0, 0], (south, east)),
        halo(7, wind_pack.at[halves - 1], wind_edge.at[1, 0], (south, west)),
    ]
    tracer_sides = [
        halo(8, tracer_pack, tracer_edge.at[0, pl.ds(narrow, rows)], (lat, east)),
        halo(9, tracer_pack, tracer_edge.at[1, pl.ds(narrow, rows)], (lat, west)),
    ]
    tracer_north = [
        halo(10, codes_out.at[0], codes_in.at[1], (north, lon)),
        halo(11, pack_out.at[0], pack_in.at[1, 0], (north, east)),
        halo(12, pack_out.at[0], pack_in.at[1, 1], (north, west)),
    ]
    tracer_south = [
        halo(13, codes_out.at[1], codes_in.at[0], (south, lon)),
        halo(14, pack_out.at[1], pack_in.at[0, 0], (south, east)),
        halo(15, pack_out.at[1], pack_in.at[0, 1], (south, west)),
    ]

    def each(condition, copies, act):
        @pl.when(condition)
        def _():
            for copy in copies:
                act(copy)

    start, arrive, leave = (lambda c: c.start()), (lambda c: c.wait_recv()), (lambda c: c.wait_send())
    whole(inner_winds, load_sem.at[2]).wait()
    for side, first in ((0, wide), (1, rows)):
        for comp in range(comps):
            for r in range(wide):
                wind_out[side, comp, r] = to_fixed(wind_pad[comp, first + r])
    pl.semaphore_wait(barrier, devices - 1)
    each(has_north, wind_north[:1], start)
    each(has_south, wind_south[:1], start)
    whole(inner_tracers, load_sem.at[3]).wait()

    def encode_rows(level, carry):
        for side, first in ((0, narrow), (1, rows)):
            for r in range(narrow):
                codes_out[side, level, r] = to_code(tracer_pad[level, first + r])
        return carry

    lax.fori_loop(0, levels, encode_rows, 0)
    each(has_north, tracer_north[:1], start)
    each(has_south, tracer_south[:1], start)

    for half in range(halves):
        for comp in range(comps):
            packed = jnp.zeros((levels, lanes), jnp.float32)
            for p in range(8):
                value = wind_pad[comp, wide + half * 8 + p]
                packed = jnp.where(
                    lane8 // 16 == p, pltpu.roll(value, (16 * p + 8) % lanes, 1), packed
                )
            wind_pack[half, comp] = to_fixed(packed)

    each(has_north, wind_north[1:], start)
    each(has_south, wind_south[1:], start)
    for copy in wind_sides:
        copy.start()

    def pack_row(r, carry):
        for side in range(2):
            packed = jnp.zeros((chans, lanes), jnp.float32)
            for level in range(levels):
                value = tracer_pad[level, narrow + 2 * r + side]
                packed = jnp.where(
                    lane16 // 16 == level, pltpu.roll(value, (16 * level + 8) % lanes, 1), packed
                )
            tracer_pack[2 * r + side] = packed
        return carry

    lax.fori_loop(0, rows // 2, pack_row, 0)

    for r in range(narrow):
        pack_out[0, r] = to_code(tracer_pack[r])
        pack_out[1, r] = to_code(tracer_pack[rows - narrow + r])
    each(has_north, tracer_north[1:], start)
    each(has_south, tracer_south[1:], start)
    for copy in tracer_sides:
        copy.start()
    for load in tables:
        load.wait()

    width = codes_v.shape[1]
    spot = lax.broadcasted_iota(jnp.int32, (1, width), 1)
    lowest = jnp.full((1, width), BIG, jnp.int32)
    highest = jnp.full((1, width), -1, jnp.int32)
    for t in range(tiles):
        for k in range(links):
            code = (t * links + k) * blocks + block_ref[k, t]
            hit = spot == owner_ref[k, t]
            lowest = jnp.minimum(lowest, jnp.where(hit, code, BIG))
            highest = jnp.maximum(highest, jnp.where(hit, code, -1))
    used = highest >= 0
    twice = highest != lowest
    low_code = jnp.where(used, lowest, 0)
    high_code = jnp.where(used, highest, 0)
    codes_v[...] = jnp.concatenate([low_code // blocks, high_code // blocks], axis=0)
    marks_v[...] = jnp.concatenate(
        [
            jnp.where(used, low_code % blocks, -1),
            jnp.where(jnp.logical_and(used, twice), high_code % blocks, -1),
        ],
        axis=0,
    )
    code_copy = pltpu.make_async_copy(codes_v, codes_s, code_sem)
    code_copy.start()

    @pl.when(jnp.logical_not(has_north))
    def _():
        wind_pad[:, 0:wide] = jnp.zeros((comps, wide, levels, lanes), jnp.float32)
        wind_edge[:, 0] = jnp.zeros((2, comps, levels, lanes), jnp.int16)
        tracer_pad[:, 0:narrow] = jnp.zeros((levels, narrow, chans, lanes), jnp.float32)
        tracer_edge[:, 0:narrow] = jnp.zeros((2, narrow, chans, lanes), jnp.float32)

    @pl.when(jnp.logical_not(has_south))
    def _():
        wind_pad[:, wide + rows :] = jnp.zeros((comps, wide, levels, lanes), jnp.float32)
        wind_edge[:, halves + 1] = jnp.zeros((2, comps, levels, lanes), jnp.int16)
        tracer_pad[:, narrow + rows :] = jnp.zeros((levels, narrow, chans, lanes), jnp.float32)
        tracer_edge[:, narrow + rows :] = jnp.zeros((2, narrow, chans, lanes), jnp.float32)

    code_copy.wait()
    flux_load.wait()
    weight_load.wait()
    group = 3 if tiles % 3 == 0 else 1

    def multiply(n, carry):
        for g in range(group):
            t = n * group + g
            right = jnp.concatenate([weights_v[t, k] for k in range(links)], axis=1)
            done = jnp.dot(fluxes_v[t], right, preferred_element_type=jnp.float32)
            for k in range(links):
                products[t * links + k] = done[:, k * lanes : (k + 1) * lanes].astype(jnp.bfloat16)
        return carry

    lax.fori_loop(0, tiles // group, multiply, 0)

    half_count = lat_count // 2
    near = half_count * lon_count
    base = lat // half_count * half_count
    near_first = base * lon_count
    far_first = lax.rem(base + half_count, lat_count) * lon_count
    mine = me - near_first
    tail = pl.ds(direct, products.shape[1] - direct)
    head = pl.ds(0, direct)

    def at_device(p):
        return (p // lon_count, lax.rem(p, lon_count))

    def near_copy(s):
        return pltpu.make_async_remote_copy(
            src_ref=outgoing.at[near_first + s], dst_ref=arrived_ref.at[me],
            send_sem=near_sem.at[0], recv_sem=near_sem.at[1],
            device_id=at_device(near_first + s), device_id_type=MESH,
        )

    def far_copy(s):
        return pltpu.make_async_remote_copy(
            src_ref=outgoing.at[far_first + s, :, head], dst_ref=arrived_ref.at[me, :, head],
            send_sem=far_sem.at[0], recv_sem=far_sem.at[1],
            device_id=at_device(far_first + s), device_id_type=MESH,
        )

    def relay_copy(s):
        return pltpu.make_async_remote_copy(
            src_ref=outgoing.at[far_first + s, :, tail], dst_ref=relayed.at[mine],
            send_sem=relay_sem.at[0], recv_sem=relay_sem.at[1],
            device_id=at_device(near_first + s), device_id_type=MESH,
        )

    def send_marks(first, recv, begin):
        def one(k, carry):
            s = lax.rem(mine + k, near)
            pltpu.make_async_remote_copy(
                src_ref=marks_v, dst_ref=labels_ref.at[:, me, :],
                send_sem=mark_sem.at[0], recv_sem=mark_sem.at[recv],
                device_id=at_device(first + s), device_id_type=MESH,
            ).start()
            return carry

        lax.fori_loop(begin, near, one, 0)

    send_marks(near_first, 1, 1)
    send_marks(far_first, 2, 0)

    def ring(away, n):
        return lax.rem(lat - base + away, half_count) * lon_count + lax.rem(lon + n, lon_count)

    def fill(first, away):
        def one(n, carry):
            p = first + ring(away, n)
            for c in range(CAP):
                outgoing[p, c] = products[codes_s[c, p]]
            return carry

        lax.fori_loop(0, lon_count, one, 0)

    def send(copy, away, begin):
        def one(n, carry):
            copy(ring(away, n)).start()
            return carry

        lax.fori_loop(begin, lon_count, one, 0)

    for away in list(range(1, half_count)) + [0]:
        fill(far_first, away)
        send(relay_copy, away, 0 if away else 1)
        send(far_copy, away, 0)
    for away in [0] + list(range(1, half_count)):
        fill(near_first, away)
        send(near_copy, away, 0 if away else 1)
    own_copies = [
        pltpu.make_async_copy(
            outgoing.at[far_first + mine, :, tail], relayed.at[mine], own_sem.at[0]
        ),
        pltpu.make_async_copy(outgoing.at[me], arrived_ref.at[me], own_sem.at[1]),
        pltpu.make_async_copy(marks_v, labels_ref.at[:, me, :], own_sem.at[2]),
    ]
    for copy in own_copies:
        copy.start()

    others = pl.ds(0, near - 1)
    labels_copy = pltpu.make_async_copy(labels_ref, labels_out, labels_sem)

    count = CAP * near
    table_copy = pltpu.make_async_copy(table_v, table_s, table_sem)
    twin = (far_first + mine) // lon_count
    dense_copy = pltpu.make_async_remote_copy(
        src_ref=dense_v, dst_ref=dense_ref, send_sem=dense_sem.at[0], recv_sem=dense_sem.at[1],
        device_id=(twin, lon), device_id_type=MESH,
    )

    def sort_relayed():
        whole(labels_ref.at[:, others], mark_sem.at[1]).wait()
        own_copies[2].wait()
        width = table_v.shape[1]
        sub = lax.broadcasted_iota(jnp.int32, (count, width), 0)
        lane = lax.broadcasted_iota(jnp.int32, (count, width), 1)
        spot = lax.broadcasted_iota(jnp.int32, (near, width), 1)
        column = jnp.concatenate(
            [
                jnp.sum(
                    jnp.where(
                        spot == far_first + mine,
                        labels_ref[c, pl.ds(pl.multiple_of(near_first, 8), near), :],
                        0,
                    ),
                    axis=1,
                    keepdims=True,
                )
                for c in range(CAP)
            ],
            axis=0,
        )
        label = jnp.broadcast_to(jnp.where(column < 0, blocks, column), (count, width))
        across = jnp.sum(jnp.where(sub == lane, label, 0), axis=0, keepdims=True)
        across = jnp.broadcast_to(across, (count, width))
        inside = lane < count
        before = jnp.logical_or(label < across, jnp.logical_and(label == across, sub < lane))
        rank = jnp.sum(jnp.where(before, 1, 0), axis=0, keepdims=True)
        pick = jnp.logical_and(jnp.broadcast_to(rank, (count, width)) == sub, inside)
        code = lax.rem(lane, near) * CAP + lane // near
        item = jnp.sum(jnp.where(pick, code, 0), axis=1, keepdims=True)
        ordered = jnp.sum(jnp.where(pick, across, 0), axis=1, keepdims=True)
        ordered = jnp.broadcast_to(ordered, (count, width))
        same = jnp.logical_and(ordered == pltpu.roll(ordered, 1, 0), sub > 0)
        upto = jnp.sum(jnp.where(jnp.logical_and(across <= sub, inside), 1, 0), axis=1, keepdims=True)
        equal = jnp.sum(jnp.where(jnp.logical_and(across == sub, inside), 1, 0), axis=1, keepdims=True)
        final = jnp.where(equal > 0, upto - 1, count)
        table_v[...] = jnp.where(lane == 0, item, jnp.where(lane == 1, jnp.where(same, 1, 0), final))
        table_copy.start()

    def take_labels():
        whole(labels_ref.at[:, pl.ds(0, near)], mark_sem.at[2]).wait()
        labels_copy.start()

    def sum_relayed():
        whole(relayed.at[others], relay_sem.at[1]).wait()
        own_copies[0].wait()
        table_copy.wait()
        size = products.shape[1] - direct

        def add(n, total):
            item = table_s[n, 0]
            kept = table_s[n, 1].astype(jnp.float32)
            total = total * kept + relayed[item // CAP, lax.rem(item, CAP)].astype(jnp.float32)
            running[n] = total
            return total

        lax.fori_loop(0, count, add, jnp.zeros((size, lanes), jnp.float32))
        running[count] = jnp.zeros((size, lanes), jnp.float32)
        low, scale = code_range(fluxes_v.shape[2], count)

        def encode(s, carry):
            value = running[table_s[s, 2]]
            code = jnp.round((jnp.log(value) - low) * scale) - CODES
            code = jnp.where(value > 0.0, jnp.clip(code, -CODES, CODES), -CODES - 1.0)
            dense_v[s] = code.astype(jnp.int32).astype(jnp.int16)
            return carry

        lax.fori_loop(0, blocks, encode, 0)

    deep, across16 = (
        lax.broadcasted_iota(jnp.int32, (16, lanes), 0),
        lax.broadcasted_iota(jnp.int32, (16, lanes), 1),
    )
    groups = lanes // 16
    for t in range(groups):
        reached = jnp.abs(16 * t + deep - across16) <= narrow
        masks[t] = jnp.where(reached, 1.0, 0.0).astype(jnp.bfloat16)
    outer = jnp.where(deep < 8, deep - 8, deep + (lanes - 8))
    masks[groups] = jnp.where(jnp.abs(outer - across16) <= narrow, 1.0, 0.0).astype(jnp.bfloat16)
    rhs_a[...] = jnp.zeros_like(rhs_a)
    rhs_b[...] = jnp.zeros_like(rhs_b)

    whole(first_v, load_sem.at[4]).wait()
    whole(second_v, load_sem.at[5]).wait()
    for copy in wind_sides:
        copy.wait_recv()
    each(has_north, wind_south, arrive)
    each(has_south, wind_north, arrive)

    def wind_rows_in(place, first):
        for comp in range(comps):
            for r in range(wide):
                wind_pad[comp, first + r] = from_fixed(wind_in[place, comp, r])

    pl.when(has_north)(functools.partial(wind_rows_in, 0, 0))
    pl.when(has_south)(functools.partial(wind_rows_in, 1, wide + rows))

    def shift_row(r, carry):
        turned = r + 8 - wide
        half, p = turned // 8, turned % 8
        back = lax.rem(2 * lanes - 8 - 16 * p, lanes)
        for comp in range(comps):
            merged = jnp.where(
                lane8 % 16 < 8, from_fixed(wind_edge[0, half, comp]), from_fixed(wind_edge[1, half, comp])
            )
            edge = pltpu.roll(merged, back, 1)
            main = wind_pad[comp, r]
            for e in range(taps):
                d = e - wide
                if d > 0:
                    piece = pltpu.roll(jnp.where(lane8 < d, edge, main), lanes - d, 1)
                elif d < 0:
                    piece = pltpu.roll(jnp.where(lane8 >= lanes + d, edge, main), -d, 1)
                else:
                    piece = main
                low, high = piece[:1], piece[levels - 1 :]
                shifted[e * 5 + 0, comp, r] = jnp.concatenate([low, low, piece[: levels - 2]], axis=0)
                shifted[e * 5 + 1, comp, r] = jnp.concatenate([low, piece[: levels - 1]], axis=0)
                shifted[e * 5 + 2, comp, r] = piece
                shifted[e * 5 + 3, comp, r] = jnp.concatenate([piece[1:], high], axis=0)
                shifted[e * 5 + 4, comp, r] = jnp.concatenate([piece[2:], high, high], axis=0)
        return carry

    lax.fori_loop(0, rows + 2 * wide, shift_row, 0)

    column = lax.broadcasted_iota(jnp.int32, (levels, lanes), 1)

    def wind_start(side, i):
        off = [first_v[comp, i] for comp in range(comps)]
        frac = [
            jnp.clip(-wind_pad[comp, wide + i] - off[comp].astype(jnp.float32), 0.0, 1.0)
            for comp in range(comps)
        ]
        weights = level_weights(off[0], frac[0])
        weights += offset_weights(off[1], frac[1], wide) + offset_weights(off[2], frac[2], wide)
        for n, weight in enumerate(weights):
            wind_w[side, n] = weight
        for comp in range(comps):
            wind_sum[side, comp] = jnp.zeros((levels, lanes), jnp.float32)

    def wind_unit(first, q):
        sides = [side for side in range(2) if 0 <= q - side < taps]
        cw = [[wind_w[side, 5 + taps + e] for e in range(taps)] for side in sides]
        rw = [wind_w[side, 5 + q - side] for side in sides]
        total = [[wind_sum[side, comp] for comp in range(comps)] for side in sides]
        for above in range(5):
            pair = [wind_w[side, above] * rw[n] for n, side in enumerate(sides)]
            for comp in range(comps):
                inner = [None] * len(sides)
                for e in range(taps):
                    value = shifted[e * 5 + above, comp, first + q]
                    for n in range(len(sides)):
                        term = cw[n][e] * value
                        inner[n] = term if e == 0 else inner[n] + term
                for n in range(len(sides)):
                    total[n][comp] = total[n][comp] + pair[n] * inner[n]
        for n, side in enumerate(sides):
            for comp in range(comps):
                wind_sum[side, comp] = total[n][comp]

    def wind_finish(side, i):
        off = [second_v[comp, i] for comp in range(comps)]
        frac = [
            jnp.clip(
                -(wind_pad[comp, wide + i] + wind_sum[side, comp]) * 0.5
                - off[comp].astype(jnp.float32),
                0.0,
                1.0,
            )
            for comp in range(comps)
        ]
        for n, weight in enumerate(level_weights(off[0], frac[0])):
            lev_w[n, i] = weight
        for n, weight in enumerate(offset_weights(off[1], frac[1], narrow)):
            row_w[n, i] = weight
        for n, weight in enumerate(cubic_weights(frac[2])):
            col_w[n, i] = weight
        col_at[i] = off[2] - 1 + column

    for side in range(2):
        wind_start(side, side)

    wind_unit(0, 0)
    for q in range(1, taps):
        wind_unit(0, q)
    wind_unit(0, taps)
    for side in range(2):
        wind_finish(side, side)

    for copy in tracer_sides:
        copy.wait_recv()
    each(has_north, tracer_south, arrive)
    each(has_south, tracer_north, arrive)

    def decode_rows(place, first):
        def decode_level(level, carry):
            for r in range(narrow):
                tracer_pad[level, first + r] = from_code(codes_in[place, level, r])
            return carry

        lax.fori_loop(0, levels, decode_level, 0)
        for side in range(2):
            for r in range(narrow):
                tracer_edge[side, first + r] = from_code(pack_in[place, side, r])

    pl.when(has_north)(functools.partial(decode_rows, 0, 0))
    pl.when(has_south)(functools.partial(decode_rows, 1, narrow + rows))

    def split_row(r, carry):
        merged = jnp.where(lane16 % 16 < 8, tracer_edge[0, r], tracer_edge[1, r])
        turned = [merged] + [pltpu.roll(merged, lanes - 16 * s, 1) for s in range(1, levels)]
        for level in range(levels):
            value = tracer_pad[level, r]
            top = value.astype(jnp.bfloat16)
            lhs[level, r, :, 0:lanes] = top
            lhs[level, r, :, lanes : 2 * lanes] = (value - top.astype(jnp.float32)).astype(jnp.bfloat16)
            edge = jnp.where(
                lane16 < 16,
                turned[level],
                jnp.where(lane16 < 32, turned[(level - 1) % levels], turned[(level - 2) % levels]),
            )
            edge_top = edge.astype(jnp.bfloat16).astype(jnp.float32)
            edge = jnp.where(lane16 < 32, edge_top, edge - edge_top)
            lhs[level, r, :, 2 * lanes : 3 * lanes] = edge.astype(jnp.bfloat16)
        return carry

    lax.fori_loop(0, rows + 2 * narrow, split_row, 0)

    deep8 = lax.broadcasted_iota(jnp.int32, (8, lanes), 0)

    def build(level, pair, rhs):
        for side in range(2):
            i = pair * 2 + side
            cols = slice(side * lanes, (side + 1) * lanes)
            at = col_at[i, pl.ds(level, 1), :]
            away = jnp.bitwise_and(deep8 - at, 7)
            value = jnp.zeros((8, lanes), jnp.float32)
            for n in range(4):
                value = jnp.where(away == n, col_w[n, i, pl.ds(level, 1), :], value)
            rest = value - value.astype(jnp.bfloat16).astype(jnp.float32)
            top16 = jnp.concatenate([value, value], axis=0).astype(jnp.bfloat16)
            rest16 = jnp.concatenate([rest, rest], axis=0).astype(jnp.bfloat16)
            for t in range(groups):
                top = top16 * masks[t]
                rhs[16 * t : 16 * t + 16, cols] = top
                rhs[2 * lanes + 16 * t : 2 * lanes + 16 * t + 16, cols] = top
                rhs[lanes + 16 * t : lanes + 16 * t + 16, cols] = rest16 * masks[t]
            top = top16 * masks[groups]
            rhs[3 * lanes : 3 * lanes + 16, cols] = top
            rhs[3 * lanes + 16 : 3 * lanes + 32, cols] = rest16 * masks[groups]
            rhs[3 * lanes + 32 : 3 * lanes + 48, cols] = top

    span = reach + 1

    def apply(level, pair, rhs):
        low, high = max(level - 2, 0), min(level + 2, levels - 1)
        count = high - low + 1
        part = lambda at: lhs[
            low : high + 1, pl.ds(pair * 2, span), :, at * lanes : (at + 1) * lanes
        ].reshape(count * span * chans, lanes)
        top, rest, edge = part(0), part(1), part(2)
        left = jnp.concatenate([top, top, rest, edge], axis=1)
        done = jnp.dot(left, rhs[...], preferred_element_type=jnp.float32)
        for side in range(2):
            i = pair * 2 + side
            cols = slice(side * lanes, (side + 1) * lanes)
            rw = [row_w[n, i, pl.ds(level, 1), :] for n in range(reach)]
            total = jnp.zeros((chans, lanes), jnp.float32)
            for m in range(count):
                lw = None
                for n in range(5):
                    if min(max(level - 2 + n, 0), levels - 1) == low + m:
                        weight = lev_w[n, i, pl.ds(level, 1), :]
                        lw = weight if lw is None else lw + weight
                inner = jnp.zeros((chans, lanes), jnp.float32)
                for n in range(reach):
                    first = (m * span + n + side) * chans
                    inner = inner + rw[n] * done[first : first + chans, cols]
                total = total + lw * inner
            moved_v[i, level] = total

    pairs = rows // 2
    shares = levels - 1
    cuts = [(n * (taps + 1) + shares // 2) // shares for n in range(shares + 1)]
    both = [rhs_a, rhs_b]
    build(0, 0, rhs_a)

    def moved_copy(pair):
        return pltpu.make_async_copy(
            moved_v.at[pl.ds(pair * 2, 2)], moved_ref.at[pl.ds(pair * 2, 2)], moved_sem
        )

    def pair_step(pair, carry):
        after = jnp.minimum(pair + 1, pairs - 1)
        def level_step(level):
            if level == 0:
                for side in range(2):
                    wind_start(side, after * 2 + side)
            if level < shares:
                for q in range(cuts[level], cuts[level + 1]):
                    wind_unit(after * 2, q)
            if level == shares - 1:
                for side in range(2):
                    wind_finish(side, after * 2 + side)
            if level < levels - 1:
                build(level + 1, pair, both[(level + 1) % 2])
            else:
                build(0, after, both[0])
            apply(level, pair, both[level % 2])

        pl.when(pair == 1)(sort_relayed)
        pl.when(pair == 2)(sum_relayed)
        pl.when(pair == pairs - 1)(take_labels)
        for level in range(levels):
            if level == 4:
                pl.when(pair == 2)(dense_copy.start)
            pl.when(pair >= 0)(functools.partial(level_step, level))
        moved_copy(pair).start()
        return carry

    lax.fori_loop(0, pairs, pair_step, 0)
    whole(moved_v, moved_sem).wait()

    for copy in wind_sides + tracer_sides:
        copy.wait_send()
    each(has_north, wind_north + tracer_north, leave)
    each(has_south, wind_south + tracer_south, leave)
    own_copies[1].wait()

    whole(outgoing.at[others], near_sem.at[0]).wait()
    whole(outgoing.at[pl.ds(0, near), :, head], far_sem.at[0]).wait()
    whole(outgoing.at[others, :, tail], relay_sem.at[0]).wait()
    whole(labels_ref.at[:, pl.ds(0, devices - 1)], mark_sem.at[0]).wait()
    labels_copy.wait()
    whole(outgoing.at[pl.ds(0, near), :, head], far_sem.at[1]).wait()
    whole(outgoing.at[others], near_sem.at[1]).wait()
    dense_copy.wait()


def join_kernel(
    dims, moved_hbm, arrived_hbm, labels_hbm, dense_hbm, out_hbm,
    labels_ref, total, sums, more, near_v, far_v, dense_v, load_sem, out_sem,
):
    chans, levels, rows, blocks, direct, cells = dims
    lat_count, lon_count = lax.axis_size("lat"), lax.axis_size("lon")
    me = lax.axis_index("lat") * lon_count + lax.axis_index("lon")
    near = near_v.shape[0]
    near_first = me // near * near
    far_first = lax.rem(near_first + near, lat_count * lon_count)
    lanes = total.shape[3]
    label_load = pltpu.make_async_copy(labels_hbm, labels_ref, load_sem.at[0])
    near_load = pltpu.make_async_copy(arrived_hbm.at[pl.ds(near_first, near)], near_v, load_sem.at[1])
    far_load = pltpu.make_async_copy(
        arrived_hbm.at[pl.ds(far_first, near), :, pl.ds(0, direct)], far_v, load_sem.at[2]
    )
    dense_load = pltpu.make_async_copy(dense_hbm, dense_v, load_sem.at[3])
    loads = [
        pltpu.make_async_copy(moved_hbm.at[:, level], total.at[:, :, level, :], load_sem.at[4])
        for level in range(levels)
    ]
    for load in [label_load, dense_load, near_load, far_load] + loads:
        load.start()
    sums[...] = jnp.zeros_like(sums)
    more[...] = jnp.zeros_like(more)
    dense_load.wait()
    low, scale = code_range(cells, CAP * near)
    cut = direct // levels

    def decode(s, carry):
        code = dense_v[s].astype(jnp.int32).astype(jnp.float32)
        value = jnp.exp((code + CODES) * (1.0 / scale) + low)
        value = jnp.where(code < -CODES, 0.0, value)
        more[s, cut:] = value.reshape(chans - cut, levels, lanes)
        return carry

    lax.fori_loop(0, blocks, decode, 0)

    def place(n, c):
        label = labels_ref[c, n, me]
        return jnp.where(label < 0, blocks, label)

    def add_near(n, carry):
        for c, one in enumerate((sums, more)):
            at = place(near_first + n, c)
            one[at] = one[at] + near_v[n, c].astype(jnp.float32).reshape(chans, levels, lanes)
        return carry

    def add_far(n, carry):
        for c, one in enumerate((sums, more)):
            at = place(far_first + n, c)
            one[at, :cut] = one[at, :cut] + far_v[n, c].astype(jnp.float32).reshape(cut, levels, lanes)
        return carry

    label_load.wait()
    near_load.wait()
    lax.fori_loop(0, near, add_near, 0)
    far_load.wait()
    lax.fori_loop(0, near, add_far, 0)
    outs = [
        pltpu.make_async_copy(total.at[s], out_hbm.at[:, :, s, :], out_sem.at[s]) for s in range(rows)
    ]
    pltpu.make_async_copy(total, total, load_sem.at[4]).wait()
    for s in range(rows):
        total[s] = total[s] + (sums[s] + more[s])
        if s:
            outs[s - 1].start()
    outs[rows - 1].start()
    for out in outs:
        out.wait()


def body(
    tracers, winds, depart_first, depart_second, fluxes, remap_weights, target_device, target_block
):
    wide = HMAX + 1
    narrow = max((HMAX + 1) // 2 + 1, HMAX // 2 + 2)
    chans, levels, rows, lanes = tracers.shape
    comps = winds.shape[0]
    tiles, links = target_device.shape
    depth, cells = fluxes.shape[1:]
    cols = remap_weights.shape[3]
    blocks = rows * lanes // cols
    devices = lax.axis_size("lat") * lax.axis_size("lon")
    padded = -(-devices // LANES) * LANES
    halves = rows // 8
    direct = depth * DIRECT_PART // 128 // 16 * 16
    near = devices // 2
    dims = (chans, levels, rows, comps, tiles, links, blocks, wide, narrow, direct)
    hbm = pl.BlockSpec(memory_space=pl.ANY)
    f32, b16, i32 = jnp.float32, jnp.bfloat16, jnp.int32
    dma = pltpu.SemaphoreType.DMA
    moved, arrived, labels, dense = pl.pallas_call(
        functools.partial(step_kernel, dims),
        out_shape=(
            jax.ShapeDtypeStruct((rows, levels, chans, lanes), f32),
            jax.ShapeDtypeStruct((devices, CAP, depth, cols), b16),
            jax.ShapeDtypeStruct((CAP, devices, padded), i32),
            jax.ShapeDtypeStruct((blocks, depth - direct, cols), jnp.int16),
        ),
        in_specs=[hbm] * 8,
        out_specs=(hbm, hbm, hbm, hbm),
        scratch_shapes=[
            pltpu.SMEM((links, tiles), i32),
            pltpu.SMEM((links, tiles), i32),
            pltpu.VMEM((CAP, devices, padded), i32),
            pltpu.VMEM((comps, rows + 2 * wide, levels, lanes), f32),
            pltpu.VMEM((comps, rows, levels, lanes), i32),
            pltpu.VMEM((comps, rows, levels, lanes), i32),
            pltpu.VMEM((levels, rows + 2 * narrow, chans, lanes), f32),
            pltpu.VMEM((tiles, depth, cells), b16),
            pltpu.VMEM((tiles, links, cells, cols), b16),
            pltpu.VMEM((tiles * links, depth, cols), b16),
            pltpu.VMEM((devices, CAP, depth, cols), b16),
            pltpu.VMEM((CAP, padded), i32),
            pltpu.SMEM((CAP, padded), i32),
            pltpu.VMEM((CAP, padded), i32),
            pltpu.VMEM((near, CAP, depth - direct, cols), b16),
            pltpu.VMEM((near * CAP + 1, depth - direct, cols), f32),
            pltpu.VMEM((blocks, depth - direct, cols), jnp.int16),
            pltpu.VMEM((near * CAP, padded), i32),
            pltpu.SMEM((near * CAP, padded), i32),
            pltpu.VMEM((halves, comps, levels, lanes), jnp.int16),
            pltpu.VMEM((rows, chans, lanes), f32),
            pltpu.VMEM((2, halves + 2, comps, levels, lanes), jnp.int16),
            pltpu.VMEM((2, rows + 2 * narrow, chans, lanes), f32),
            pltpu.VMEM((2, levels, narrow, chans, lanes), jnp.int16),
            pltpu.VMEM((2, levels, narrow, chans, lanes), jnp.int16),
            pltpu.VMEM((2, narrow, chans, lanes), jnp.int16),
            pltpu.VMEM((2, 2, narrow, chans, lanes), jnp.int16),
            pltpu.VMEM((2, comps, wide, levels, lanes), jnp.int16),
            pltpu.VMEM((2, comps, wide, levels, lanes), jnp.int16),
            pltpu.VMEM((5 * (2 * wide + 1), comps, rows + 2 * wide, levels, lanes), f32),
            pltpu.VMEM((levels, rows + 2 * narrow, chans, 3 * lanes), b16),
            pltpu.VMEM((4 * lanes, 2 * lanes), b16),
            pltpu.VMEM((4 * lanes, 2 * lanes), b16),
            pltpu.VMEM((lanes // 16 + 1, 16, lanes), b16),
            pltpu.VMEM((2, 5 + 2 * (2 * wide + 1), levels, lanes), f32),
            pltpu.VMEM((2, comps, levels, lanes), f32),
            pltpu.VMEM((5, rows, levels, lanes), f32),
            pltpu.VMEM((2 * narrow + 1, rows, levels, lanes), f32),
            pltpu.VMEM((4, rows, levels, lanes), f32),
            pltpu.VMEM((rows, levels, lanes), i32),
            pltpu.VMEM((rows, levels, chans, lanes), f32),
            dma((8,)),
            dma(()),
            dma(()),
            dma((16,)),
            dma((16,)),
            dma((2,)),
            dma((2,)),
            dma((3,)),
            dma((2,)),
            dma((2,)),
            dma(()),
            dma((3,)),
            dma(()),
        ],
        compiler_params=pltpu.CompilerParams(
            collective_id=0, has_side_effects=True, vmem_limit_bytes=62 * 1024 * 1024
        ),
        name="step",
    )(winds, depart_first, depart_second, tracers, fluxes, remap_weights, target_device.T, target_block.T)
    return pl.pallas_call(
        functools.partial(join_kernel, (chans, levels, rows, blocks, direct, cells)),
        out_shape=jax.ShapeDtypeStruct((chans, levels, rows, lanes), f32),
        in_specs=[hbm] * 4,
        out_specs=hbm,
        scratch_shapes=[
            pltpu.SMEM((CAP, devices, padded), i32),
            pltpu.VMEM((rows, chans, levels, lanes), f32),
            pltpu.VMEM((blocks + 1, chans, levels, lanes), f32),
            pltpu.VMEM((blocks + 1, chans, levels, lanes), f32),
            pltpu.VMEM((near, CAP, depth, cols), b16),
            pltpu.VMEM((near, CAP, direct, cols), b16),
            pltpu.VMEM((blocks, depth - direct, cols), jnp.int16),
            dma((5,)),
            dma((rows,)),
        ],
        compiler_params=pltpu.CompilerParams(vmem_limit_bytes=62 * 1024 * 1024),
        name="join",
    )(moved, arrived, labels, dense)


def solution(mesh):
    in_specs = (
        P(None, None, "lat", "lon"),
        P(None, None, "lat", "lon"),
        P(None, None, "lat", "lon"),
        P(None, None, "lat", "lon"),
        P(("lat", "lon"), None, None),
        P(("lat", "lon"), None, None, None),
        P(("lat", "lon"), None),
        P(("lat", "lon"), None),
    )
    out_specs = P(None, None, "lat", "lon")
    return jax.shard_map(body, mesh=mesh, in_specs=in_specs, out_specs=out_specs, check_vma=False)
```
